128 devices in a mesh: elem: 32 (over x, y, core), freq: 4 (over z).
Axes of the slice: x: 4, y: 4, z: 4, core: 2. Of those that a mesh axis runs over, the one named last changes fastest.
Arguments:
- load: float32 [48, 128, 2, 4096], P(None, 'freq', None, 'elem'), may hold values from -6 to 6
- stiffness: float32 [96, 96], replicated, as said below
- mass_template: float32 [96], replicated, may hold values from 0.5 to 2
- modulus: float32 [4096], P('elem'), may hold values from 0.5 to 2
- element_mass: float32 [4096], P('elem'), may hold values from 0.5 to 2
- strain_map: float32 [6, 96], replicated, may hold values from -0.625 to 0.625
- curves: float32 [4, 16], replicated, may hold values from 0.2 to 1
- soil_type: int32 [4096], P(('elem', 'freq')), may hold values from 0 to 3
Outputs:
- new_modulus: float32 [4096], P(('elem', 'freq'))
- peak_strain: float32 [4096], P(('elem', 'freq'))
The draws below stay inside these ranges and needn't reach their ends.
Inputs may be any that keep to these rules, and one draw needn't show every extreme that they name: `stiffness`: symmetric positive definite.
All inputs are finite; a program needn't handle non-finite values.
Results may differ from the reference program's by a relative error of at most 0.00013.
Values sent between devices are 32-bit elements; how exact they have to be, the bound alone decides.
No kernel may reach another device: no remote copies, remote signals or barrier semaphores. Data moves between devices by JAX's collectives and lax.ppermute only.
A program may use at most 128 MiB of HBM per device.

```python
import math
import jax
import jax.numpy as jnp
from jax import lax

NB = 48
NF = 128
NT = 512
COMPS = 6
NTYPE = 4
LEVELS = 16
ITERS = 3
NN = 4096


def draw_stiffness(key, part):
    first_key, second_key, third_key, fourth_key = jax.random.split(key, 4)
    half_size = NB
    raw_part = jax.random.uniform(first_key, (half_size, half_size), jnp.float32, -0.02, 0.02)
    stiff_block = raw_part + raw_part.T
    identity = jnp.eye(half_size, dtype=jnp.float32)
    block_diag = 0.04 * half_size + jax.random.uniform(second_key, (half_size,), jnp.float32, 0.3, 1.0)
    stiff_block = stiff_block * (1.0 - identity) + identity * block_diag[None, :]
    coupled = jnp.concatenate([jnp.concatenate([stiff_block, -stiff_block], 1), jnp.concatenate([-stiff_block, stiff_block], 1)], 0)
    raw_extra = jax.random.uniform(third_key, (2 * half_size, 2 * half_size), jnp.float32, -0.0005, 0.0005)
    extra_part = raw_extra + raw_extra.T
    identity_two = jnp.eye(2 * half_size, dtype=jnp.float32)
    extra_diag = 0.002 * half_size + jax.random.uniform(fourth_key, (2 * half_size,), jnp.float32, 0.02, 0.08)
    extra_part = extra_part * (1.0 - identity_two) + identity_two * extra_diag[None, :]
    return coupled + extra_part


def with_ends(values, own_key, low, largest):
    spot = [jax.random.randint(jax.random.fold_in(own_key, axis), (), 0, length) for axis, length in enumerate(values.shape)]
    widest = values.shape.index(max(values.shape))
    next_to = spot[:widest] + [(spot[widest] + 1) % values.shape[widest]] + spot[widest + 1:]
    return values.at[tuple(spot)].set(low).at[tuple(next_to)].set(largest)


def steps_of(rng, shape, pieces, least, largest):
    level, own = 1.0, jax.random.fold_in(rng, 6)
    for dim, blocks in pieces:
        heights = jnp.exp(jax.random.uniform(jax.random.fold_in(own, dim), (blocks,), jnp.float32, least / len(pieces), largest / len(pieces)))
        level = level * jnp.repeat(heights, shape[dim] // blocks).reshape([-1 if axis == dim else 1 for axis in range(len(shape))])
    return level


def gaussian(rng, shape, width, bound, cuts=(), held_as=jnp.bfloat16):
    loudness = steps_of(rng, shape, cuts, -0.22, 0.18) if cuts else 1.0
    array = jax.random.normal(rng, shape, jnp.float32) * width * loudness
    return jnp.minimum(jnp.maximum(array, -bound), bound).astype(held_as)


def setup_inputs(seed: int = 0) -> dict:
    key_list = jax.random.split(jax.random.key(seed), 9)
    return {
        "load": gaussian(key_list[0], (NB, NF, 2, NN), 1.0, 6.0, ((1, 4), (3, 32)), jnp.float32),
        "stiffness": draw_stiffness(jax.random.fold_in(key_list[8], 71), 0),
        "mass_template": jnp.clip(jnp.exp(jax.random.uniform(key_list[2], (2 * NB,), jnp.float32, math.log(0.5), math.log(2.0))), 0.5, 2.0),
        "modulus": jnp.clip(jnp.exp(math.log(2.0) - 1.3862944 * jax.random.uniform(key_list[3], (NN,), jnp.float32) ** steps_of(key_list[3], (NN,), ((0, 32),), -0.2, 0.2)), 0.5, 2.0),
        "element_mass": jnp.clip(jnp.exp(math.log(2.0) - 1.3862944 * jax.random.uniform(key_list[4], (NN,), jnp.float32) ** steps_of(key_list[4], (NN,), ((0, 32),), -0.2, 0.2)), 0.5, 2.0),
        "strain_map": gaussian(key_list[5], (COMPS, 2 * NB), (2 * NB) ** -0.5, 0.625, (), jnp.float32),
        "curves": jnp.clip(jax.random.uniform(key_list[6], (NTYPE, LEVELS), jnp.float32, 0.2, 1.0), 0.2, 1.0),
        "soil_type": with_ends(jax.random.randint(key_list[7], (NN,), 0, NTYPE), jax.random.fold_in(key_list[7], 1), 0, NTYPE - 1).astype(jnp.int32),
    }


PRECISE = lax.Precision.HIGHEST
MASS_COEF = 0.5
LOG_LOW = -1.5
LOG_STEP = 0.2
STRAIN_FACTOR = 0.65
EPSILON = 1e-06

def element_vectors(field):
    ahead = jnp.concatenate([field[..., 1:], jnp.zeros_like(field[..., :1])], axis=-1)
    return jnp.concatenate([field, ahead], axis=0)

def operate(field, stiffness, mass_template, modulus, element_mass, mass_shift):
    stacked = element_vectors(field)
    product = jnp.dot(stiffness, stacked.reshape(2 * NB, -1), precision=PRECISE).reshape(stacked.shape)
    forces = modulus * product + mass_shift * element_mass * mass_template[:, None, None] * stacked
    behind = jnp.concatenate([jnp.zeros_like(forces[NB:, :, :1]), forces[NB:, :, :-1]], axis=-1)
    return forces[:NB] + behind

def reference(load, stiffness, mass_template, modulus, element_mass, strain_map, curves, soil_type):
    kdiag = jnp.diagonal(stiffness)
    prev_modulus = jnp.concatenate([jnp.zeros((1,), jnp.float32), modulus[:-1]])
    prev_mass = jnp.concatenate([jnp.zeros((1,), jnp.float32), element_mass[:-1]])

    def solve_one(inputs):
        index, rhs = inputs
        order = (index + 1).astype(jnp.float32)
        mass_shift = MASS_COEF * (order / NF) ** 2
        diag_own = kdiag[:NB, None] * modulus + mass_shift * element_mass * mass_template[:NB, None]
        diag_prev = kdiag[NB:, None] * prev_modulus + mass_shift * prev_mass * mass_template[NB:, None]
        inv_diag = (1.0 / (diag_own + diag_prev))[:, None, :]
        solution = jnp.zeros_like(rhs)
        residual = rhs
        precond = residual * inv_diag
        direction = precond
        rho_now = jnp.sum(residual * precond)
        for iteration in range(ITERS):
            image = operate(direction, stiffness, mass_template, modulus, element_mass, mass_shift)
            alpha = rho_now / jnp.sum(direction * image)
            solution = solution + alpha * direction
            residual = residual - alpha * image
            precond = residual * inv_diag
            rho_next = jnp.sum(residual * precond)
            direction = precond + rho_next / rho_now * direction
            rho_now = rho_next
        stacked = element_vectors(solution)
        strain = jnp.dot(strain_map, stacked.reshape(2 * NB, -1), precision=PRECISE)
        return strain.reshape(COMPS, 2, -1)
    loads = jnp.moveaxis(load, 1, 0)
    spectra = lax.map(solve_one, (jnp.arange(NF, dtype=jnp.int32), loads))
    freqs = jnp.arange(NF, dtype=jnp.int32) + 1
    times = jnp.arange(NT, dtype=jnp.int32)
    phase = (freqs[:, None] * times[None, :] % NT).astype(jnp.float32) * (2.0 * jnp.pi / NT)
    table = jnp.stack([jnp.cos(phase), -jnp.sin(phase)], axis=1)
    history = jnp.einsum('fkt,fcke->cte', table, spectra, precision=PRECISE) * (1.0 / jnp.sqrt(jnp.float32(NF)))
    peak = lax.optimization_barrier(jnp.max(lax.optimization_barrier(jnp.sum(history * history, axis=0)), axis=0))
    peak_strain = STRAIN_FACTOR * jnp.sqrt(peak + EPSILON)
    position = (jnp.log10(peak_strain) - LOG_LOW) / LOG_STEP
    levels = jnp.arange(LEVELS, dtype=jnp.float32)
    hats = jnp.maximum(0.0, 1.0 - jnp.abs(position[:, None] - levels[None, :]))
    onehot = (soil_type[:, None] == jnp.arange(NTYPE, dtype=jnp.int32)[None, :]).astype(jnp.float32)
    own_curve = jnp.dot(onehot, curves, precision=PRECISE)
    ratio = lax.optimization_barrier(jnp.sum(own_curve * hats, axis=1))
    return (modulus * ratio, peak_strain)
```

```python
import jax
import jax.numpy as jnp
import numpy as np
from jax import lax
from jax.experimental import pallas as pl
from jax.experimental.pallas import tpu as pltpu
from jax.sharding import PartitionSpec as P

NT = 512
MASS_COEF = 0.5
LOG_LOW = -1.5
LOG_STEP = 0.2
STRAIN_FACTOR = 0.65
EPSILON = 1e-06
LANES = 128
SLOT = 8
PER_PATCH = LANES // SLOT
DOTS = 6
F32 = jnp.float32
BF16 = jnp.bfloat16
VMEM = pl.BlockSpec(memory_space=pltpu.VMEM)
SMEM = pl.BlockSpec(memory_space=pltpu.SMEM)


def lane_ids(rows=1):
    return lax.broadcasted_iota(jnp.int32, (rows, LANES), 1)


def later(x):
    return pltpu.roll(x, 127, 1)


def earlier(x):
    return pltpu.roll(x, 1, 1)


def halves(x):
    high = x.astype(BF16)
    return high, (x - high.astype(F32)).astype(BF16)


def edges_kernel(load_ref, modulus_ref, mass_ref, out_ref):
    half = load_ref.shape[0] // 64
    parts = 64
    slot = lane_ids(half) // SLOT
    for group in range(parts // PER_PATCH):

        def place(i, held):
            field = load_ref[pl.ds(group * PER_PATCH + i, half, stride=parts), :]
            moved = pltpu.roll(field, 2 + SLOT * i, 1)
            return jnp.where(slot == i, moved, held)

        held = lax.fori_loop(0, PER_PATCH, place, jnp.zeros((half, LANES), F32), unroll=16)
        out_ref[group * half : (group + 1) * half, :] = held
    base = parts // PER_PATCH * half
    out_ref[base : base + 1, :] = modulus_ref[...]
    out_ref[base + 1 : base + 2, :] = mass_ref[...]
    out_ref[base + 2 : base + 8, :] = jnp.zeros((6, LANES), F32)


def pattern(row):
    row = jnp.where(lane_ids() < SLOT, row, 0.0)
    for step in (8, 16, 32, 64):
        row = row + pltpu.roll(row, step, 1)
    return row


def main_kernel(
    info_ref, load_ref, own_ref, left_ref, right_ref, lhs_ref, cols_ref,
    out0_ref, out1_ref, out2_ref, out3_ref, dots_out_ref,
    field_ref, inv_ref, strain_ref, border_ref, dots_ref,
):
    half = lhs_ref.shape[1] // 3
    parts = 64
    freqs = parts // 2
    groups = parts // PER_PATCH
    base = groups * half
    freq_group = info_ref[0]
    is_last = info_ref[1]
    first_order = (freq_group * freqs + 1).astype(F32)
    lanes = lane_ids()
    place = lanes % SLOT

    def shift_of(order):
        return MASS_COEF * (order * (1.0 / (4 * freqs))) ** 2

    cols = cols_ref[...]
    kd_top, kd_low, mt_top, mt_low = (cols[:, i : i + 1] for i in range(4))

    def rows_of(at):
        own, left, right = (r[base + at : base + at + 1, :] for r in (own_ref, left_ref, right_ref))
        prev = jnp.where(lanes == 0, earlier(left), earlier(own))
        right_prev = jnp.where(lanes == 0, earlier(own), earlier(right))
        own2, prev2 = pltpu.roll(own, 2, 1), pltpu.roll(prev, 2, 1)
        near = lanes < 2
        lower = pattern(jnp.where(near, pltpu.roll(left, 2, 1), own2))
        lower_prev = pattern(jnp.where(near, pltpu.roll(left, 3, 1), prev2))
        upper = pattern(jnp.where(near, own2, pltpu.roll(right, 2, 1)))
        upper_prev = pattern(jnp.where(near, prev2, pltpu.roll(right_prev, 2, 1)))
        return (own, prev), (lower, lower_prev), (upper, upper_prev)

    mod_main, mod_lower, mod_upper = rows_of(0)
    mass_main, mass_lower, mass_upper = rows_of(1)

    def diagonals(mod, mass):
        return kd_top * mod[0] + kd_low * mod[1], mt_top * mass[0] + mt_low * mass[1]

    lhs = lhs_ref[...]

    def products(left, right):
        left_high, left_low = halves(left)
        right_high, right_low = halves(right)
        high = jnp.concatenate([left_high, right_high], 1)
        low = jnp.concatenate([left_low, right_low], 1)
        result = jnp.dot(lhs, jnp.concatenate([high, low, high], 0), preferred_element_type=F32)
        cut = [half * i for i in range(5)] + [4 * half + 8, 4 * half + 16]
        return [
            [result[cut[i] : cut[i + 1], LANES * k : LANES * (k + 1)] for i in range(6)]
            for k in range(2)
        ]

    stiff_lower, mass_diag_lower = diagonals(mod_lower, mass_lower)
    stiff_upper, mass_diag_upper = diagonals(mod_upper, mass_upper)
    fixed = jnp.logical_and(is_last == 1, place >= 2)
    for group in range(groups):
        order = first_order + (group * (PER_PATCH // 2) + lanes // (2 * SLOT)).astype(F32)
        shift = shift_of(order)
        diag_lower = stiff_lower + shift * mass_diag_lower
        diag_upper = stiff_upper + shift * mass_diag_upper
        inv_lower = jnp.where(diag_lower > 0, 1.0 / diag_lower, 0.0)
        inv_upper = jnp.where(
            jnp.logical_and(diag_upper > 0, jnp.logical_not(fixed)), 1.0 / diag_upper, 0.0
        )
        rows = slice(group * half, (group + 1) * half)
        own, left, right = own_ref[rows, :], left_ref[rows, :], right_ref[rows, :]
        lower = jnp.where(place < 2, left, own) * inv_lower
        upper = jnp.where(place < 2, own, right) * inv_upper
        for stage in range(3):
            lower_p, upper_p = products(lower, upper)
            l11, l22, l12, l21, _, _ = lower_p
            u11, u22, u12, u21, _, u_strain = upper_p
            from_above = later(mod_upper[1] * u12)
            at = stage * groups + group
            if stage < 2:
                from_below = earlier(mod_lower[0] * l21)
                border = jnp.where(
                    place == 1, from_above, jnp.where(place == 2, from_below, 0.0)
                )
                lower = -inv_lower * (
                    mod_lower[0] * l11 + mod_lower[1] * l22 + later(mod_lower[1] * l12) + from_below
                )
                tail = u_strain
                upper_next = -inv_upper * (
                    mod_upper[0] * u11 + mod_upper[1] * u22 + from_above
                    + earlier(mod_upper[0] * u21)
                )
            else:
                border = jnp.where(place == 1, from_above, 0.0)
                energy = jnp.sum(mod_upper[1] * upper * u22, axis=0, keepdims=True)
                row = lax.broadcasted_iota(jnp.int32, (8, LANES), 0)
                tail = jnp.where(row == 6, energy, u_strain)
                upper_next = None
            border_ref[at, :half, :] = border
            border_ref[at, half:, :] = jnp.where(place == 1, later(tail), 0.0)
            upper = upper_next

    stiff_main, mass_diag_main = diagonals(mod_main, mass_main)
    mod_own, mod_prev = mod_main
    mod_sent_up = jnp.where(lanes == 127, 0.0, mod_own)
    mod_sent_down = jnp.where(lanes == 0, 0.0, mod_prev)
    rim = jnp.logical_or(lanes == 0, lanes == 127)

    def borders(stage, f, k):
        part = 2 * f + k
        group = part // PER_PATCH
        i = part % PER_PATCH
        moved = pltpu.roll(border_ref[stage * groups + group], (126 + LANES - SLOT * i) % LANES, 1)
        moved = jnp.where(rim, moved, 0.0)
        return moved[:half], moved[half:]

    def strain_of(top, low, added):
        return top + jnp.where(lanes == 127, 0.0, later(low)) + added

    def put_dot(which, f, pairs):
        total = sum(a * b for a, b in pairs)
        dots_ref[pl.ds(which * freqs + f, 1), :] = jnp.sum(total, axis=0, keepdims=True)

    def put_strain(stage, f, k, value):
        start = ((stage * 2 + k) * freqs + f) * 8
        strain_ref[pl.ds(pl.multiple_of(start, 8), 8), :] = value

    def images(f, stage, fields):
        result = []
        for k, z in enumerate(products(*fields)):
            z11, z22, z12, z21, s_top, s_low = z
            added, added_strain = borders(stage, f, k)
            image = (
                mod_own * z11 + mod_prev * z22 + later(mod_sent_down * z12)
                + earlier(mod_sent_up * z21) + added
            )
            put_strain(stage, f, k, strain_of(s_top, s_low, added_strain))
            result.append(-image)
        return result

    def first(f, carry):
        inv = 1.0 / (stiff_main + shift_of(first_order + f.astype(F32)) * mass_diag_main)
        inv_ref[f] = inv
        loads = [load_ref[pl.ds(2 * f + k, half, stride=parts), :] for k in range(2)]
        fields = [inv * b for b in loads]
        image = images(f, 0, fields)
        nexts = [inv * t for t in image]
        for k in range(2):
            field_ref[2 * f + k] = nexts[k]
        put_dot(0, f, zip(fields, loads))
        put_dot(1, f, zip(fields, image))
        put_dot(2, f, zip(nexts, image))
        return carry

    def second(f, carry):
        inv = inv_ref[f]
        fields = [field_ref[2 * f + k] for k in range(2)]
        image = images(f, 1, fields)
        nexts = [inv * t for t in image]
        for k in range(2):
            field_ref[2 * f + k] = nexts[k]
        put_dot(3, f, zip(fields, image))
        put_dot(4, f, zip(nexts, image))
        return carry

    def third(f, carry):
        fields = [field_ref[2 * f + k] for k in range(2)]
        total, extra = 0.0, 0.0
        for k, z in enumerate(products(*fields)):
            z11, z22, z12, _, s_top, s_low = z
            added, added_strain = borders(2, f, k)
            twice = 2.0 * (later(mod_sent_down * z12) + added)
            total = total + fields[k] * (mod_own * z11 + mod_sent_down * z22 + twice)
            strain = strain_of(s_top, s_low, added_strain)
            put_strain(2, f, k, strain)
            extra = extra + strain[6:7]
        dots_ref[pl.ds(5 * freqs + f, 1), :] = -(jnp.sum(total, axis=0, keepdims=True) + extra)
        return carry

    lax.fori_loop(0, freqs, first, 0, unroll=2)
    lax.fori_loop(0, freqs, second, 0, unroll=2)
    lax.fori_loop(0, freqs, third, 0, unroll=2)

    dots_ref[DOTS * freqs :, :] = jnp.zeros((256 - DOTS * freqs, LANES), F32)
    sums = lax.dot_general(
        jnp.ones((8, LANES), F32), dots_ref[...], (((1,), (1,)), ((), ())),
        precision=lax.Precision.HIGHEST, preferred_element_type=F32,
    )
    row = lax.broadcasted_iota(jnp.int32, (8, LANES), 0)
    pair = jnp.where(row % 2 == 0, sums[:, :LANES], sums[:, LANES:])
    for i in range(dots_out_ref.shape[0] // 8):
        dots_out_ref[8 * i : 8 * i + 8, :] = pair

    quarter = LANES // 4
    cell = lane_ids(8) // quarter
    outs = (out0_ref, out1_ref, out2_ref, out3_ref)

    def pack(block, carry):
        comps = [
            strain_ref[pl.ds(block * 64 + c, 8, stride=8), :] for c in range(6)
        ]
        for step in range(4):
            dest = (freq_group + step) % 4
            for side in range(2):
                held = jnp.zeros((8, LANES), F32)
                for c in range(4 * side, min(6, 4 * side + 4)):
                    moved = pltpu.roll(comps[c], quarter * ((c + 4 - dest) % 4), 1)
                    held = jnp.where(cell == c % 4, moved, held)
                start = pl.multiple_of(side * 3 * parts + block * 8, 8)
                outs[step][pl.ds(start, 8), :] = held
        return carry

    lax.fori_loop(0, 3 * parts // 8, pack, 0, unroll=2)


def coefficients(h):
    def dot(a, b, energy):
        total = None
        for i, x in enumerate(a):
            for j, y in enumerate(b):
                weight = h[i + j] - h[i + j + 1] if energy else h[i + j]
                term = x * y * weight
                total = term if total is None else total + term
        return total

    one = jnp.ones_like(h[0])
    residual, direction = [one], [one]
    rho = h[0]
    result = []
    for iteration in range(3):
        alpha = rho / dot(direction, direction, True)
        result = [
            (result[i] if i < len(result) else 0.0) + alpha * direction[i]
            for i in range(len(direction))
        ]
        if iteration == 2:
            break
        image = (
            [direction[0]]
            + [direction[i] - direction[i - 1] for i in range(1, len(direction))]
            + [-direction[-1]]
        )
        residual = [
            (residual[i] if i < len(residual) else 0.0) - alpha * image[i]
            for i in range(len(image))
        ]
        rho_next = dot(residual, residual, False)
        beta = rho_next / rho
        rho = rho_next
        direction = [
            residual[i] + (beta * direction[i] if i < len(direction) else 0.0)
            for i in range(len(residual))
        ]
    return result


def final_kernel(
    info_ref, curves_ref, dots_ref, part0_ref, part1_ref, part2_ref, part3_ref,
    table_high_ref, table_low_ref, modulus_ref, soil_ref,
    modulus_out_ref, strain_out_ref, spectra_ref,
):
    freq_group = info_ref[0]
    parts, freqs = 64, 32
    total = jnp.zeros((8, LANES), F32)
    for i in range(dots_ref.shape[0] // 8):
        total = total + dots_ref[8 * i : 8 * i + 8, :]
    square = jnp.concatenate([total, jnp.zeros((LANES - 8, LANES), F32)], 0)
    turned = jnp.transpose(square)
    beside = pltpu.roll(turned, 127, 1)
    h = [turned[freqs * i : freqs * (i + 1)] for i in range(4)]
    h += [beside[freqs * i : freqs * (i + 1)] for i in range(2)]
    coefs = coefficients(h)
    lanes = lane_ids(freqs)
    for step, part_ref in enumerate((part0_ref, part1_ref, part2_ref, part3_ref)):
        source = (freq_group + 4 - step) % 4
        weights = [
            jnp.sum(jnp.where(lanes == 2 * source, c, 0.0), axis=1, keepdims=True) for c in coefs
        ]
        for k in range(2):
            start = pl.multiple_of(source * parts + k * freqs, freqs)
            for side in range(2):
                value = None
                for j in range(3):
                    at = (side * 3 + j) * parts + k * freqs
                    term = weights[j] * part_ref[at : at + freqs, :]
                    value = term if value is None else value + term
                spectra_ref[pl.ds(start, freqs), side * LANES : (side + 1) * LANES] = value
    high, low = halves(spectra_ref[...])
    table_high, table_low = table_high_ref[...], table_low_ref[...]
    history = (
        jnp.dot(table_high, low, preferred_element_type=F32)
        + jnp.dot(table_low, high, preferred_element_type=F32)
        + jnp.dot(table_high, high, preferred_element_type=F32)
    )
    squares = history[:, :LANES] ** 2 + history[:, LANES:] ** 2
    squares = squares + pltpu.roll(squares, 64, 1)
    squares = squares + pltpu.roll(squares, 32, 1)
    peak = jnp.max(squares, axis=0, keepdims=True)[:, : LANES // 4] * (1.0 / (4 * freqs))
    peak_strain = STRAIN_FACTOR * jnp.sqrt(peak + EPSILON)
    position = (jnp.log(peak_strain) * (1.0 / np.log(10.0)) - LOG_LOW) / LOG_STEP
    soil = soil_ref[...]
    ratio = jnp.zeros_like(position)
    for level in range(curves_ref.shape[1]):
        value = jnp.where(soil == 0, curves_ref[0, level], 0.0)
        for kind in range(1, curves_ref.shape[0]):
            value = jnp.where(soil == kind, curves_ref[kind, level], value)
        ratio = ratio + value * jnp.maximum(0.0, 1.0 - jnp.abs(position - level))
    own = pltpu.roll(modulus_ref[...], (LANES - LANES // 4 * freq_group) % LANES, 1)
    modulus_out_ref[...] = own[:, : LANES // 4] * ratio
    strain_out_ref[...] = peak_strain


def time_table(total_freq):
    order = np.arange(1, total_freq + 1)
    phase = (np.arange(NT)[:, None] * order[None, :] % NT) * (2.0 * np.pi / NT)
    waves = np.stack([np.cos(phase), -np.sin(phase)], 1)
    table = waves.reshape(NT, 2, 4, total_freq // 4).transpose(0, 2, 1, 3).reshape(NT, -1)
    high = table.astype(np.float32).astype(jnp.bfloat16)
    low = (table - high.astype(np.float64)).astype(np.float32).astype(jnp.bfloat16)
    return high, low


def per_device(
    load, stiffness, mass_template, modulus, element_mass, strain_map, curves, soil_type
):
    half, freq_dev, _, nodes = load.shape
    parts = 2 * freq_dev
    groups = lax.axis_size("freq")
    slabs = lax.axis_size("elem")
    freq_group = lax.axis_index("freq")
    is_last = (lax.axis_index("elem") == slabs - 1).astype(jnp.int32)
    info = jnp.stack([freq_group.astype(jnp.int32), is_last])
    rows = load.reshape(half * parts, nodes)
    modulus_row, mass_row = modulus.reshape(1, nodes), element_mass.reshape(1, nodes)
    edge_rows = parts // PER_PATCH * half + 8
    edges = pl.pallas_call(
        edges_kernel,
        out_shape=jax.ShapeDtypeStruct((edge_rows, LANES), F32),
        in_specs=[VMEM] * 3,
        out_specs=VMEM,
        name="edges",
    )(rows, modulus_row, mass_row)
    from_left = lax.ppermute(edges, "elem", [(i, i + 1) for i in range(slabs - 1)])
    from_right = lax.ppermute(edges, "elem", [(i + 1, i) for i in range(slabs - 1)])

    kdiag = jnp.diagonal(stiffness)
    off = stiffness * (1.0 - jnp.eye(2 * half, dtype=F32))
    comps = strain_map.shape[0]
    strain_rows = jnp.pad(strain_map, ((0, 8 - comps), (0, 0)))
    stacked = jnp.concatenate(
        [off[:half, :half], off[half:, half:], off[:half, half:], off[half:, :half],
         strain_rows[:, :half], strain_rows[:, half:]], 0
    )
    high, low = halves(stacked)
    lhs = jnp.concatenate([high, high, low], 1)
    cols = jnp.stack([kdiag[:half], kdiag[half:], mass_template[:half], mass_template[half:]], 1)
    packed = 6 * parts
    outs = pl.pallas_call(
        main_kernel,
        out_shape=[jax.ShapeDtypeStruct((packed, LANES), F32)] * 4
        + [jax.ShapeDtypeStruct((2 * slabs * groups, LANES), F32)],
        in_specs=[SMEM] + [VMEM] * 6,
        out_specs=[VMEM] * 5,
        scratch_shapes=[
            pltpu.VMEM((parts, half, LANES), F32),
            pltpu.VMEM((freq_dev, half, LANES), F32),
            pltpu.VMEM((3 * parts * 8, LANES), F32),
            pltpu.VMEM((3 * parts // PER_PATCH, half + 8, LANES), F32),
            pltpu.VMEM((256, LANES), F32),
        ],
        compiler_params=pltpu.CompilerParams(vmem_limit_bytes=32 * 1024 * 1024),
        name="krylov",
    )(info, rows, edges, from_left, from_right, lhs, cols)
    received = [outs[0]] + [
        lax.ppermute(outs[step], "freq", [(i, (i + step) % groups) for i in range(groups)])
        for step in range(1, groups)
    ]
    dots = lax.all_to_all(
        outs[4].reshape(slabs * groups, 2, LANES), ("elem", "freq"), 0, 0
    ).reshape(-1, LANES)
    table_high, table_low = time_table(freq_dev * groups)
    quarter = nodes // groups
    new_modulus, peak_strain = pl.pallas_call(
        final_kernel,
        out_shape=[jax.ShapeDtypeStruct((1, quarter), F32)] * 2,
        in_specs=[SMEM] * 2 + [VMEM] * 9,
        out_specs=[VMEM] * 2,
        scratch_shapes=[pltpu.VMEM((groups * parts, 2 * LANES), F32)],
        compiler_params=pltpu.CompilerParams(vmem_limit_bytes=32 * 1024 * 1024),
        name="response",
    )(info, curves, dots, *received, jnp.asarray(table_high), jnp.asarray(table_low),
      modulus_row, soil_type.reshape(1, quarter))
    return new_modulus.reshape(quarter), peak_strain.reshape(quarter)


def solution(mesh):
    in_specs = (
        P(None, "freq", None, "elem"),
        P(),
        P(),
        P("elem"),
        P("elem"),
        P(),
        P(),
        P(("elem", "freq")),
    )
    out_specs = (P(("elem", "freq")), P(("elem", "freq")))
    return jax.shard_map(
        per_device, mesh=mesh, in_specs=in_specs, out_specs=out_specs, check_vma=False
    )
```

```python
import jax
import jax.numpy as jnp
import numpy as np
from jax import lax
from jax.experimental import pallas as pl
from jax.experimental.pallas import tpu as pltpu
from jax.sharding import PartitionSpec as P

NT = 512
MASS_COEF = 0.5
LOG_LOW = -1.5
LOG_STEP = 0.2
STRAIN_FACTOR = 0.65
EPSILON = 1e-06
LANES = 128
SLOT = 8
PER_PATCH = LANES // SLOT
UNROLL = 32
DOTS = 6
F32 = jnp.float32
BF16 = jnp.bfloat16
VMEM = pl.BlockSpec(memory_space=pltpu.VMEM)
SMEM = pl.BlockSpec(memory_space=pltpu.SMEM)


def lane_ids(rows=1):
    return lax.broadcasted_iota(jnp.int32, (rows, LANES), 1)


def later(x):
    return pltpu.roll(x, 127, 1)


def earlier(x):
    return pltpu.roll(x, 1, 1)


def halves(x):
    high = x.astype(BF16)
    return high, (x - high.astype(F32)).astype(BF16)


def edges_kernel(load_ref, modulus_ref, mass_ref, out_ref):
    half = load_ref.shape[0] // 64
    parts = 64
    slot = lane_ids(half) // SLOT
    for group in range(parts // PER_PATCH):

        def place(i, held):
            field = load_ref[pl.ds(group * PER_PATCH + i, half, stride=parts), :]
            moved = pltpu.roll(field, 2 + SLOT * i, 1)
            return jnp.where(slot == i, moved, held)

        held = lax.fori_loop(0, PER_PATCH, place, jnp.zeros((half, LANES), F32), unroll=16)
        out_ref[group * half : (group + 1) * half, :] = held
    base = parts // PER_PATCH * half
    out_ref[base : base + 1, :] = modulus_ref[...]
    out_ref[base + 1 : base + 2, :] = mass_ref[...]
    out_ref[base + 2 : base + 8, :] = jnp.zeros((6, LANES), F32)


def pattern(row):
    row = jnp.where(lane_ids() < SLOT, row, 0.0)
    for step in (8, 16, 32, 64):
        row = row + pltpu.roll(row, step, 1)
    return row


def main_kernel(
    info_ref, load_ref, own_ref, left_ref, right_ref, lhs_ref, cols_ref,
    strain_ref, dots_out_ref, field_ref, inv_ref, border_ref, dots_ref,
):
    half = lhs_ref.shape[1] // 3
    parts = 64
    freqs = parts // 2
    groups = parts // PER_PATCH
    base = groups * half
    freq_group = info_ref[0]
    is_last = info_ref[1]
    first_order = (freq_group * freqs + 1).astype(F32)
    lanes = lane_ids()
    place = lanes % SLOT

    def shift_of(order):
        return MASS_COEF * (order * (1.0 / (4 * freqs))) ** 2

    cols = cols_ref[...]
    kd_top, kd_low, mt_top, mt_low = (cols[:, i : i + 1] for i in range(4))

    def rows_of(at):
        own, left, right = (r[base + at : base + at + 1, :] for r in (own_ref, left_ref, right_ref))
        prev = jnp.where(lanes == 0, earlier(left), earlier(own))
        right_prev = jnp.where(lanes == 0, earlier(own), earlier(right))
        own2, prev2 = pltpu.roll(own, 2, 1), pltpu.roll(prev, 2, 1)
        near = lanes < 2
        lower = pattern(jnp.where(near, pltpu.roll(left, 2, 1), own2))
        lower_prev = pattern(jnp.where(near, pltpu.roll(left, 3, 1), prev2))
        upper = pattern(jnp.where(near, own2, pltpu.roll(right, 2, 1)))
        upper_prev = pattern(jnp.where(near, prev2, pltpu.roll(right_prev, 2, 1)))
        return (own, prev), (lower, lower_prev), (upper, upper_prev)

    mod_main, mod_lower, mod_upper = rows_of(0)
    mass_main, mass_lower, mass_upper = rows_of(1)

    def diagonals(mod, mass):
        return kd_top * mod[0] + kd_low * mod[1], mt_top * mass[0] + mt_low * mass[1]

    lhs = lhs_ref[...]

    def products(left, right):
        left_high, left_low = halves(left)
        right_high, right_low = halves(right)
        high = jnp.concatenate([left_high, right_high], 1)
        low = jnp.concatenate([left_low, right_low], 1)
        result = jnp.dot(lhs, jnp.concatenate([high, low, high], 0), preferred_element_type=F32)
        cut = [half * i for i in range(5)] + [4 * half + 8, 4 * half + 16]
        return [
            [result[cut[i] : cut[i + 1], LANES * k : LANES * (k + 1)] for i in range(6)]
            for k in range(2)
        ]

    stiff_lower, mass_diag_lower = diagonals(mod_lower, mass_lower)
    stiff_upper, mass_diag_upper = diagonals(mod_upper, mass_upper)
    fixed = jnp.logical_and(is_last == 1, place >= 2)
    for group in range(groups):
        order = first_order + (group * (PER_PATCH // 2) + lanes // (2 * SLOT)).astype(F32)
        shift = shift_of(order)
        diag_lower = stiff_lower + shift * mass_diag_lower
        diag_upper = stiff_upper + shift * mass_diag_upper
        inv_lower = jnp.where(diag_lower > 0, 1.0 / diag_lower, 0.0)
        inv_upper = jnp.where(
            jnp.logical_and(diag_upper > 0, jnp.logical_not(fixed)), 1.0 / diag_upper, 0.0
        )
        rows = slice(group * half, (group + 1) * half)
        own, left, right = own_ref[rows, :], left_ref[rows, :], right_ref[rows, :]
        lower = jnp.where(place < 2, left, own) * inv_lower
        upper = jnp.where(place < 2, own, right) * inv_upper
        for stage in range(3):
            lower_p, upper_p = products(lower, upper)
            l11, l22, l12, l21, _, _ = lower_p
            u11, u22, u12, u21, _, u_strain = upper_p
            from_above = later(mod_upper[1] * u12)
            at = stage * groups + group
            if stage < 2:
                from_below = earlier(mod_lower[0] * l21)
                border = jnp.where(
                    place == 1, from_above, jnp.where(place == 2, from_below, 0.0)
                )
                lower = -inv_lower * (
                    mod_lower[0] * l11 + mod_lower[1] * l22 + later(mod_lower[1] * l12) + from_below
                )
                tail = u_strain
                upper_next = -inv_upper * (
                    mod_upper[0] * u11 + mod_upper[1] * u22 + from_above
                    + earlier(mod_upper[0] * u21)
                )
            else:
                border = jnp.where(place == 1, from_above, 0.0)
                energy = jnp.sum(mod_upper[1] * upper * u22, axis=0, keepdims=True)
                row = lax.broadcasted_iota(jnp.int32, (8, LANES), 0)
                tail = jnp.where(row == 6, energy, u_strain)
                upper_next = None
            border_ref[at, :half, :] = border
            border_ref[at, half:, :] = jnp.where(place == 1, later(tail), 0.0)
            upper = upper_next

    stiff_main, mass_diag_main = diagonals(mod_main, mass_main)
    mod_own, mod_prev = mod_main
    mod_sent_up = jnp.where(lanes == 127, 0.0, mod_own)
    mod_sent_down = jnp.where(lanes == 0, 0.0, mod_prev)
    rim = jnp.logical_or(lanes == 0, lanes == 127)

    def borders(stage, f, k):
        part = 2 * f + k
        group = part // PER_PATCH
        i = part % PER_PATCH
        moved = pltpu.roll(border_ref[stage * groups + group], (126 + LANES - SLOT * i) % LANES, 1)
        moved = jnp.where(rim, moved, 0.0)
        return moved[:half], moved[half:]

    def strain_of(top, low, added):
        return top + jnp.where(lanes == 127, 0.0, later(low)) + added

    def put_dot(which, f, pairs):
        total = sum(a * b for a, b in pairs)
        dots_ref[pl.ds(which * freqs + f, 1), :] = jnp.sum(total, axis=0, keepdims=True)

    def put_strain(stage, f, k, value):
        start = ((stage * 2 + k) * freqs + f) * 8
        strain_ref[pl.ds(pl.multiple_of(start, 8), 8), :] = value

    def images(f, stage, fields):
        result = []
        for k, z in enumerate(products(*fields)):
            z11, z22, z12, z21, s_top, s_low = z
            added, added_strain = borders(stage, f, k)
            image = (
                mod_own * z11 + mod_prev * z22 + later(mod_sent_down * z12)
                + earlier(mod_sent_up * z21) + added
            )
            put_strain(stage, f, k, strain_of(s_top, s_low, added_strain))
            result.append(-image)
        return result

    def first(f, carry):
        inv = 1.0 / (stiff_main + shift_of(first_order + f.astype(F32)) * mass_diag_main)
        inv_ref[f] = inv
        loads = [load_ref[pl.ds(2 * f + k, half, stride=parts), :] for k in range(2)]
        fields = [inv * b for b in loads]
        image = images(f, 0, fields)
        nexts = [inv * t for t in image]
        for k in range(2):
            field_ref[2 * f + k] = nexts[k]
        put_dot(0, f, zip(fields, loads))
        put_dot(1, f, zip(fields, image))
        put_dot(2, f, zip(nexts, image))
        return carry

    def second(f, carry):
        inv = inv_ref[f]
        fields = [field_ref[2 * f + k] for k in range(2)]
        image = images(f, 1, fields)
        nexts = [inv * t for t in image]
        for k in range(2):
            field_ref[2 * f + k] = nexts[k]
        put_dot(3, f, zip(fields, image))
        put_dot(4, f, zip(nexts, image))
        return carry

    def third(f, carry):
        fields = [field_ref[2 * f + k] for k in range(2)]
        total, extra = 0.0, 0.0
        for k, z in enumerate(products(*fields)):
            z11, z22, z12, _, s_top, s_low = z
            added, added_strain = borders(2, f, k)
            twice = 2.0 * (later(mod_sent_down * z12) + added)
            total = total + fields[k] * (mod_own * z11 + mod_sent_down * z22 + twice)
            strain = strain_of(s_top, s_low, added_strain)
            put_strain(2, f, k, strain)
            extra = extra + strain[6:7]
        dots_ref[pl.ds(5 * freqs + f, 1), :] = -(jnp.sum(total, axis=0, keepdims=True) + extra)
        return carry

    lax.fori_loop(0, freqs, first, 0, unroll=UNROLL)
    lax.fori_loop(0, freqs, second, 0, unroll=UNROLL)
    lax.fori_loop(0, freqs, third, 0, unroll=UNROLL)

    dots_ref[DOTS * freqs :, :] = jnp.zeros((256 - DOTS * freqs, LANES), F32)
    sums = lax.dot_general(
        jnp.ones((8, LANES), F32), dots_ref[...], (((1,), (1,)), ((), ())),
        precision=lax.Precision.HIGHEST, preferred_element_type=F32,
    )
    row = lax.broadcasted_iota(jnp.int32, (8, LANES), 0)
    pair = jnp.where(row % 2 == 0, sums[:, :LANES], sums[:, LANES:])
    for i in range(dots_out_ref.shape[0] // 8):
        dots_out_ref[8 * i : 8 * i + 8, :] = pair


def coefficients(h):
    def dot(a, b, energy):
        total = None
        for i, x in enumerate(a):
            for j, y in enumerate(b):
                weight = h[i + j] - h[i + j + 1] if energy else h[i + j]
                term = x * y * weight
                total = term if total is None else total + term
        return total

    one = jnp.ones_like(h[0])
    residual, direction = [one], [one]
    rho = h[0]
    result = []
    for iteration in range(3):
        alpha = rho / dot(direction, direction, True)
        result = [
            (result[i] if i < len(result) else 0.0) + alpha * direction[i]
            for i in range(len(direction))
        ]
        if iteration == 2:
            break
        image = (
            [direction[0]]
            + [direction[i] - direction[i - 1] for i in range(1, len(direction))]
            + [-direction[-1]]
        )
        residual = [
            (residual[i] if i < len(residual) else 0.0) - alpha * image[i]
            for i in range(len(image))
        ]
        rho_next = dot(residual, residual, False)
        beta = rho_next / rho
        rho = rho_next
        direction = [
            residual[i] + (beta * direction[i] if i < len(direction) else 0.0)
            for i in range(len(residual))
        ]
    return result


def combine_kernel(info_ref, dots_ref, strain_ref, out0_ref, out1_ref, out2_ref, out3_ref):
    freq_group = info_ref[0]
    freqs, comps = 32, 6
    total = jnp.zeros((8, LANES), F32)
    for i in range(dots_ref.shape[0] // 8):
        total = total + dots_ref[8 * i : 8 * i + 8, :]
    square = jnp.concatenate([total, jnp.zeros((LANES - 8, LANES), F32)], 0)
    turned = jnp.transpose(square)
    odd = lane_ids(LANES) % 2 == 1
    even_sums = jnp.sum(jnp.where(odd, 0.0, turned), axis=1, keepdims=True)
    odd_sums = jnp.sum(jnp.where(odd, turned, 0.0), axis=1, keepdims=True)
    h = [even_sums[freqs * i : freqs * (i + 1)] for i in range(4)]
    h += [odd_sums[freqs * i : freqs * (i + 1)] for i in range(2)]
    weights = [jnp.broadcast_to(c, (freqs, LANES)) for c in coefficients(h)]
    quarter = LANES // 4
    cell = lane_ids(freqs) // quarter
    outs = (out0_ref, out1_ref, out2_ref, out3_ref)
    for k in range(2):
        spectra = [
            sum(
                weights[j] * strain_ref[pl.ds((2 * j + k) * freqs * 8 + c, freqs, stride=8), :]
                for j in range(3)
            )
            for c in range(comps)
        ]
        for step in range(4):
            dest = (freq_group + step) % 4
            for side in range(2):
                held = jnp.zeros((freqs, LANES), F32)
                for c in range(4 * side, min(comps, 4 * side + 4)):
                    moved = pltpu.roll(spectra[c], quarter * ((c + 4 - dest) % 4), 1)
                    held = jnp.where(cell == c % 4, moved, held)
                start = (2 * side + k) * freqs
                outs[step][start : start + freqs, :] = held


def final_kernel(
    info_ref, curves_ref, part0_ref, part1_ref, part2_ref, part3_ref,
    table_high_ref, table_low_ref, modulus_ref, soil_ref,
    modulus_out_ref, strain_out_ref, spectra_ref,
):
    freq_group = info_ref[0]
    parts, freqs = 64, 32
    for step, part_ref in enumerate((part0_ref, part1_ref, part2_ref, part3_ref)):
        start = pl.multiple_of((freq_group + 4 - step) % 4 * parts, parts)
        for side in range(2):
            spectra_ref[pl.ds(start, parts), side * LANES : (side + 1) * LANES] = part_ref[
                side * parts : (side + 1) * parts, :
            ]
    high, low = halves(spectra_ref[...])
    table_high, table_low = table_high_ref[...], table_low_ref[...]
    history = (
        jnp.dot(table_high, low, preferred_element_type=F32)
        + jnp.dot(table_low, high, preferred_element_type=F32)
        + jnp.dot(table_high, high, preferred_element_type=F32)
    )
    squares = history[:, :LANES] ** 2 + history[:, LANES:] ** 2
    squares = squares + pltpu.roll(squares, 64, 1)
    squares = squares + pltpu.roll(squares, 32, 1)
    peak = jnp.max(squares, axis=0, keepdims=True)[:, : LANES // 4] * (1.0 / (4 * freqs))
    peak_strain = STRAIN_FACTOR * jnp.sqrt(peak + EPSILON)
    position = (jnp.log(peak_strain) * (1.0 / np.log(10.0)) - LOG_LOW) / LOG_STEP
    soil = soil_ref[...]
    ratio = jnp.zeros_like(position)
    for level in range(curves_ref.shape[1]):
        value = jnp.where(soil == 0, curves_ref[0, level], 0.0)
        for kind in range(1, curves_ref.shape[0]):
            value = jnp.where(soil == kind, curves_ref[kind, level], value)
        ratio = ratio + value * jnp.maximum(0.0, 1.0 - jnp.abs(position - level))
    own = pltpu.roll(modulus_ref[...], (LANES - LANES // 4 * freq_group) % LANES, 1)
    modulus_out_ref[...] = own[:, : LANES // 4] * ratio
    strain_out_ref[...] = peak_strain


def time_table(total_freq):
    order = np.arange(1, total_freq + 1)
    phase = (np.arange(NT)[:, None] * order[None, :] % NT) * (2.0 * np.pi / NT)
    waves = np.stack([np.cos(phase), -np.sin(phase)], 1)
    table = waves.reshape(NT, 2, 4, total_freq // 4).transpose(0, 2, 1, 3).reshape(NT, -1)
    high = table.astype(np.float32).astype(jnp.bfloat16)
    low = (table - high.astype(np.float64)).astype(np.float32).astype(jnp.bfloat16)
    return high, low


def per_device(
    load, stiffness, mass_template, modulus, element_mass, strain_map, curves, soil_type
):
    half, freq_dev, _, nodes = load.shape
    parts = 2 * freq_dev
    groups = lax.axis_size("freq")
    slabs = lax.axis_size("elem")
    freq_group = lax.axis_index("freq")
    is_last = (lax.axis_index("elem") == slabs - 1).astype(jnp.int32)
    info = jnp.stack([freq_group.astype(jnp.int32), is_last])
    rows = load.reshape(half * parts, nodes)
    modulus_row, mass_row = modulus.reshape(1, nodes), element_mass.reshape(1, nodes)
    edge_rows = parts // PER_PATCH * half + 8
    edges = pl.pallas_call(
        edges_kernel,
        out_shape=jax.ShapeDtypeStruct((edge_rows, LANES), F32),
        in_specs=[VMEM] * 3,
        out_specs=VMEM,
        name="edges",
    )(rows, modulus_row, mass_row)
    from_left = lax.ppermute(edges, "elem", [(i, i + 1) for i in range(slabs - 1)])
    from_right = lax.ppermute(edges, "elem", [(i + 1, i) for i in range(slabs - 1)])

    kdiag = jnp.diagonal(stiffness)
    off = stiffness * (1.0 - jnp.eye(2 * half, dtype=F32))
    comps = strain_map.shape[0]
    strain_rows = jnp.pad(strain_map, ((0, 8 - comps), (0, 0)))
    stacked = jnp.concatenate(
        [off[:half, :half], off[half:, half:], off[:half, half:], off[half:, :half],
         strain_rows[:, :half], strain_rows[:, half:]], 0
    )
    high, low = halves(stacked)
    lhs = jnp.concatenate([high, high, low], 1)
    cols = jnp.stack([kdiag[:half], kdiag[half:], mass_template[:half], mass_template[half:]], 1)
    strains, dots = pl.pallas_call(
        main_kernel,
        out_shape=[
            jax.ShapeDtypeStruct((3 * parts * 8, LANES), F32),
            jax.ShapeDtypeStruct((2 * slabs, LANES), F32),
        ],
        in_specs=[SMEM] + [VMEM] * 6,
        out_specs=[VMEM] * 2,
        scratch_shapes=[
            pltpu.VMEM((parts, half, LANES), F32),
            pltpu.VMEM((freq_dev, half, LANES), F32),
            pltpu.VMEM((3 * parts // PER_PATCH, half + 8, LANES), F32),
            pltpu.VMEM((256, LANES), F32),
        ],
        compiler_params=pltpu.CompilerParams(vmem_limit_bytes=32 * 1024 * 1024),
        name="krylov",
    )(info, rows, edges, from_left, from_right, lhs, cols)
    dots = lax.all_to_all(dots.reshape(slabs, 2, LANES), "elem", 0, 0).reshape(-1, LANES)
    outs = pl.pallas_call(
        combine_kernel,
        out_shape=[jax.ShapeDtypeStruct((2 * parts, LANES), F32)] * groups,
        in_specs=[SMEM] + [VMEM] * 2,
        out_specs=[VMEM] * groups,
        name="combine",
    )(info, dots, strains)
    received = [outs[0]] + [
        lax.ppermute(outs[step], "freq", [(i, (i + step) % groups) for i in range(groups)])
        for step in range(1, groups)
    ]
    table_high, table_low = time_table(freq_dev * groups)
    quarter = nodes // groups
    new_modulus, peak_strain = pl.pallas_call(
        final_kernel,
        out_shape=[jax.ShapeDtypeStruct((1, quarter), F32)] * 2,
        in_specs=[SMEM] * 2 + [VMEM] * 8,
        out_specs=[VMEM] * 2,
        scratch_shapes=[pltpu.VMEM((groups * parts, 2 * LANES), F32)],
        compiler_params=pltpu.CompilerParams(vmem_limit_bytes=32 * 1024 * 1024),
        name="response",
    )(info, curves, *received, jnp.asarray(table_high), jnp.asarray(table_low),
      modulus_row, soil_type.reshape(1, quarter))
    return new_modulus.reshape(quarter), peak_strain.reshape(quarter)


def solution(mesh):
    in_specs = (
        P(None, "freq", None, "elem"),
        P(),
        P(),
        P("elem"),
        P("elem"),
        P(),
        P(),
        P(("elem", "freq")),
    )
    out_specs = (P(("elem", "freq")), P(("elem", "freq")))
    return jax.shard_map(
        per_device, mesh=mesh, in_specs=in_specs, out_specs=out_specs, check_vma=False
    )
```

```python
import jax
import jax.numpy as jnp
import numpy as np
from jax import lax
from jax.experimental import pallas as pl
from jax.experimental.pallas import tpu as pltpu
from jax.sharding import PartitionSpec as P

NT = 512
MASS_COEF = 0.5
LOG_LOW = -1.5
LOG_STEP = 0.2
STRAIN_FACTOR = 0.65
EPSILON = 1e-06
LANES = 128
SLOT = 8
DEPTH = 176
UNROLL = 32
DOTS = 6
F32 = jnp.float32
BF16 = jnp.bfloat16
VMEM = pl.BlockSpec(memory_space=pltpu.VMEM)
SMEM = pl.BlockSpec(memory_space=pltpu.SMEM)
HBM = pl.BlockSpec(memory_space=pltpu.HBM)
PAIR_ROWS, ROW_AT = 96, 96
UP_ROWS, DOWN_ROWS = 104, 152


def lane_ids(rows=1):
    return lax.broadcasted_iota(jnp.int32, (rows, LANES), 1)


def later(x):
    return pltpu.roll(x, 127, 1)


def earlier(x):
    return pltpu.roll(x, 1, 1)


def halves(x):
    high = x.astype(BF16)
    return high, (x - high.astype(F32)).astype(BF16)


def edges_kernel(
    load_ref, modulus_ref, mass_ref, stiffness_ref, template_ref, strain_map_ref,
    up_ref, down_ref, lhs_ref, cols_ref,
    buffer_ref, slots_ref, turned_ref, square_ref, copied,
):
    half, parts, chunks = 48, 64, 3
    per = half // chunks
    length = per * parts
    copies = [
        pltpu.make_async_copy(
            load_ref.at[pl.ds(i * length, length)], buffer_ref.at[pl.ds(i * length, length)],
            copied.at[i],
        )
        for i in range(chunks)
    ]
    for copy in copies:
        copy.start()

    full = 2 * half
    square_ref[...] = jnp.zeros(square_ref.shape, F32)
    square_ref[:full, :full] = stiffness_ref[...]
    comps = strain_map_ref.shape[0]
    square_ref[full : full + comps, :full] = strain_map_ref[...]
    square_ref[full + 8 : full + 9, :full] = template_ref[...]
    stiff = square_ref[:full, :]
    same = lax.broadcasted_iota(jnp.int32, (full, LANES), 0) == lane_ids(full)
    kdiag = jnp.sum(jnp.where(same, stiff, 0.0), axis=1, keepdims=True)
    template = jnp.sum(
        jnp.where(same, square_ref[full + 8 : full + 9, :], 0.0), axis=1, keepdims=True
    )
    lane = lane_ids(half)
    columns = jnp.zeros((half, LANES), F32)
    for i, col in enumerate((kdiag[:half], kdiag[half:], template[:half], template[half:])):
        columns = jnp.where(lane == i, col, columns)
    cols_ref[...] = columns
    off = jnp.where(same, 0.0, stiff)
    strain_rows = square_ref[full : full + 8, :]
    moved = pltpu.roll(off, LANES - half, 1)
    moved_rows = pltpu.roll(strain_rows, LANES - half, 1)
    stacked = jnp.concatenate(
        [off[:half], moved[half:], moved[:half], off[half:], strain_rows, moved_rows], 0
    )
    rows = stacked.shape[0]
    lane = lane_ids(rows)
    stacked = jnp.where(lane < half, stacked, 0.0)
    high, low = halves(stacked)
    high = high.astype(F32)
    lhs_ref[:, :LANES] = (high + pltpu.roll(high, half, 1)).astype(BF16)
    lhs_ref[:, LANES:] = low

    slot = lane_ids(parts) // SLOT
    for chunk in range(chunks):
        copies[chunk].wait()
        held = jnp.zeros((parts, LANES), F32)
        for i in range(per):
            start = (chunk * per + i) * parts
            moved = pltpu.roll(buffer_ref[start : start + parts, :], 2 + SLOT * i, 1)
            held = jnp.where(slot == i, moved, held)
        at = chunk * per
        for turn, shift in enumerate((LANES - 1, LANES - 3)):
            slots_ref[pl.ds(0, parts, stride=2), :] = held
            slots_ref[pl.ds(1, parts, stride=2), :] = pltpu.roll(held, shift, 1)
            turned_ref[...] = jnp.transpose(slots_ref[...])
            if turn == 0:
                pair = turned_ref[pl.ds(1, per, stride=SLOT), :]
                up_ref[at : at + per, :] = pair
                down_ref[at : at + per, :] = pair
            else:
                pair = turned_ref[pl.ds(0, per, stride=SLOT), :]
                up_ref[half + at : half + at + per, :] = pair
                down_ref[half + at : half + at + per, :] = pair
                down_ref[UP_ROWS + at : UP_ROWS + at + per, :] = turned_ref[
                    pl.ds(1, per, stride=SLOT), :
                ]
    for ref in (up_ref, down_ref):
        ref[ROW_AT : ROW_AT + 1, :] = modulus_ref[...]
        ref[ROW_AT + 1 : ROW_AT + 2, :] = mass_ref[...]
        ref[ROW_AT + 2 : UP_ROWS, :] = jnp.zeros((UP_ROWS - ROW_AT - 2, LANES), F32)


def main_kernel(
    load_ref, own_ref, left_ref, right_ref, lhs_ref, cols_ref, strain_out_ref, dots_out_ref,
    strain_ref, field_ref, inv_ref, border_ref, dots_ref, copied,
):
    half, parts = 48, 64
    freqs = parts // 2
    freq_group = lax.axis_index("freq")
    is_last = lax.axis_index("elem") == lax.axis_size("elem") - 1
    first_order = (freq_group * freqs + 1).astype(F32)
    lanes = lane_ids()
    even = lanes % 2 == 0

    def shift_of(order):
        return MASS_COEF * (order * (1.0 / (4 * freqs))) ** 2

    cols = cols_ref[...]
    kd_top, kd_low, mt_top, mt_low = (cols[:, i : i + 1] for i in range(4))

    def rows_of(at):
        own, left, right = (
            r[ROW_AT + at : ROW_AT + at + 1, :] for r in (own_ref, left_ref, right_ref)
        )
        prev = jnp.where(lanes == 0, earlier(left), earlier(own))

        def sides(*upper_lower):
            (upper, i), (lower, j) = upper_lower
            upper, lower = upper[:, i : i + 1], lower[:, j : j + 1]
            return jnp.where(even, upper, lower)

        zero = jnp.zeros_like(own)
        pairs = [
            (sides((own, 126), (own, 1)), sides((own, 125), (own, 0))),
            (sides((own, 127), (own, 0)), sides((own, 126), (left, 127))),
            (sides((right, 0), (left, 127)), sides((own, 127), (left, 126))),
            (sides((right, 1), (left, 126)), sides((right, 0), (left, 125))),
            (sides((right, 2), (zero, 0)), sides((right, 1), (zero, 0))),
        ]
        return (own, prev), pairs

    mod_main, mod_pairs = rows_of(0)
    mass_main, mass_pairs = rows_of(1)

    def diagonals(mod, mass):
        return kd_top * mod[0] + kd_low * mod[1], mt_top * mass[0] + mt_low * mass[1]

    lhs = lhs_ref[:, :DEPTH]
    blank = jnp.zeros((DEPTH - 3 * half, 2 * LANES), BF16)

    def products(*fields):
        split = [halves(field) for field in fields]
        high = jnp.concatenate([h for h, _ in split], 1)
        low = jnp.concatenate([l for _, l in split], 1)
        gap = blank[:, : high.shape[1]]
        result = jnp.dot(
            lhs, jnp.concatenate([high, low, gap, high], 0), preferred_element_type=F32
        )
        cut = [half * i for i in range(5)] + [4 * half + 8, 4 * half + 16]
        return [
            [result[cut[i] : cut[i + 1], LANES * k : LANES * (k + 1)] for i in range(6)]
            for k in range(len(fields))
        ]

    order = first_order + (lanes // 4).astype(F32)
    beyond = jnp.logical_and(even, is_last)
    inverses = []
    for i, (mod, mass) in enumerate(zip(mod_pairs, mass_pairs)):
        stiff, weight = diagonals(mod, mass)
        diag = stiff + shift_of(order) * weight
        good = diag > 0
        if i >= 2:
            good = jnp.logical_and(good, jnp.logical_not(beyond))
        inverses.append(jnp.where(good, 1.0 / diag, 0.0))

    def met(at):
        inward = later(right_ref[at : at + half, :])
        return jnp.where(even, inward, earlier(left_ref[at : at + half, :]))

    rims = [
        own_ref[half : 2 * half, :],
        own_ref[:half, :],
        met(0),
        met(half),
        jnp.where(even, later(right_ref[UP_ROWS:, :]), 0.0),
    ]
    rims = [field * inv for field, inv in zip(rims, inverses)]

    def rim_stage(stage, rims):
        first = stage
        z = {}
        for i in range(first, len(rims), 2):
            names = list(range(i, min(i + 2, len(rims))))
            for name, value in zip(names, products(*(rims[name] for name in names))):
                z[name] = value
        at_edge = mod_pairs[1]
        outer = z[2]
        if stage < 2:
            border = jnp.where(even, at_edge[0] * outer[2], at_edge[1] * outer[3])
            tail = outer[5]
        else:
            border = jnp.where(even, at_edge[0] * outer[2], 0.0)
            energy = jnp.sum(at_edge[0] * rims[2] * outer[1], axis=0, keepdims=True)
            row = lax.broadcasted_iota(jnp.int32, (8, LANES), 0)
            tail = jnp.where(row == 6, energy, outer[5])
        border_ref[stage, :half, :] = border
        border_ref[stage, half:, :] = jnp.where(even, tail, 0.0)
        nexts = [None] * len(rims)
        for i in range(first + 1, len(rims) - 1):
            above = jnp.where(even, z[i + 1][2], z[i - 1][2])
            below = jnp.where(even, z[i - 1][3], z[i + 1][3])
            top, low = mod_pairs[i]
            nexts[i] = -inverses[i] * (top * (z[i][0] + above) + low * (z[i][1] + below))
        return nexts[: len(rims) - 1]

    stiff_main, mass_diag_main = diagonals(mod_main, mass_main)
    mod_own, mod_prev = mod_main
    mod_sent_up = jnp.where(lanes == 127, 0.0, mod_own)
    mod_sent_down = jnp.where(lanes == 0, 0.0, mod_prev)
    rim = jnp.logical_or(lanes == 0, lanes == 127)

    def borders(stage, f, k):
        moved = pltpu.roll(border_ref[stage], LANES - 1 - 2 * (2 * f + k), 1)
        moved = jnp.where(rim, moved, 0.0)
        return moved[:half], moved[half:]

    def strain_of(top, low, added):
        return top + jnp.where(lanes == 127, 0.0, later(low)) + added

    def put_dot(which, f, pairs):
        total = sum(a * b for a, b in pairs)
        dots_ref[pl.ds(which * freqs + f, 1), :] = jnp.sum(total, axis=0, keepdims=True)

    def put_strain(stage, f, k, value):
        start = ((stage * 2 + k) * freqs + f) * 8
        strain_ref[pl.ds(pl.multiple_of(start, 8), 8), :] = value

    def images(f, stage, fields):
        result = []
        for k, z in enumerate(products(*fields)):
            z11, z22, z12, z21, s_top, s_low = z
            added, added_strain = borders(stage, f, k)
            image = (
                mod_own * z11 + mod_prev * z22 + later(mod_sent_down * z12)
                + earlier(mod_sent_up * z21) + added
            )
            put_strain(stage, f, k, strain_of(s_top, s_low, added_strain))
            result.append(-image)
        return result

    def first(f, carry):
        inv = 1.0 / (stiff_main + shift_of(first_order + f.astype(F32)) * mass_diag_main)
        inv_ref[f] = inv
        loads = [load_ref[pl.ds(2 * f + k, half, stride=parts), :] for k in range(2)]
        fields = [inv * b for b in loads]
        image = images(f, 0, fields)
        nexts = [inv * t for t in image]
        for k in range(2):
            field_ref[2 * f + k] = nexts[k]
        put_dot(0, f, zip(fields, loads))
        put_dot(1, f, zip(fields, image))
        put_dot(2, f, zip(nexts, image))
        return carry

    def second(f, carry):
        inv = inv_ref[f]
        fields = [field_ref[2 * f + k] for k in range(2)]
        image = images(f, 1, fields)
        nexts = [inv * t for t in image]
        for k in range(2):
            field_ref[2 * f + k] = nexts[k]
        put_dot(3, f, zip(fields, image))
        put_dot(4, f, zip(nexts, image))
        return carry

    def third(f, carry):
        fields = [field_ref[2 * f + k] for k in range(2)]
        total, extra = 0.0, 0.0
        for k, z in enumerate(products(*fields)):
            z11, z22, z12, _, s_top, s_low = z
            added, added_strain = borders(2, f, k)
            twice = 2.0 * (later(mod_sent_down * z12) + added)
            total = total + fields[k] * (mod_own * z11 + mod_sent_down * z22 + twice)
            strain = strain_of(s_top, s_low, added_strain)
            put_strain(2, f, k, strain)
            extra = extra + strain[6:7]
        dots_ref[pl.ds(5 * freqs + f, 1), :] = -(jnp.sum(total, axis=0, keepdims=True) + extra)
        return carry

    rows = 2 * freqs * 8
    copies = []
    for stage, step in enumerate((first, second, third)):
        rims = rim_stage(stage, rims)
        lax.fori_loop(0, freqs, step, 0, unroll=UNROLL)
        block = pl.ds(stage * rows, rows)
        copy = pltpu.make_async_copy(
            strain_ref.at[block], strain_out_ref.at[block], copied.at[stage]
        )
        copy.start()
        copies.append(copy)

    dots_ref[DOTS * freqs :, :] = jnp.zeros((256 - DOTS * freqs, LANES), F32)
    sums = lax.dot_general(
        jnp.ones((8, LANES), F32), dots_ref[...], (((1,), (1,)), ((), ())),
        precision=lax.Precision.HIGHEST, preferred_element_type=F32,
    )
    row = lax.broadcasted_iota(jnp.int32, (8, LANES), 0)
    pair = jnp.where(row % 2 == 0, sums[:, :LANES], sums[:, LANES:])
    for i in range(dots_out_ref.shape[0] // 8):
        dots_out_ref[8 * i : 8 * i + 8, :] = pair
    for copy in copies:
        copy.wait()


def coefficients(h):
    def dot(a, b, energy):
        total = None
        for i, x in enumerate(a):
            for j, y in enumerate(b):
                weight = h[i + j] - h[i + j + 1] if energy else h[i + j]
                term = x * y * weight
                total = term if total is None else total + term
        return total

    one = jnp.ones_like(h[0])
    residual, direction = [one], [one]
    rho = h[0]
    result = []
    for iteration in range(3):
        alpha = rho / dot(direction, direction, True)
        result = [
            (result[i] if i < len(result) else 0.0) + alpha * direction[i]
            for i in range(len(direction))
        ]
        if iteration == 2:
            break
        image = (
            [direction[0]]
            + [direction[i] - direction[i - 1] for i in range(1, len(direction))]
            + [-direction[-1]]
        )
        residual = [
            (residual[i] if i < len(residual) else 0.0) - alpha * image[i]
            for i in range(len(image))
        ]
        rho_next = dot(residual, residual, False)
        beta = rho_next / rho
        rho = rho_next
        direction = [
            residual[i] + (beta * direction[i] if i < len(direction) else 0.0)
            for i in range(len(residual))
        ]
    return result


def combine_kernel(
    dots_ref, strain_in_ref, out0_ref, out1_ref, out2_ref, out3_ref, strain_ref, copied
):
    copy = pltpu.make_async_copy(strain_in_ref, strain_ref, copied)
    copy.start()
    freq_group = lax.axis_index("freq")
    freqs, comps = 32, 6
    total = jnp.zeros((8, LANES), F32)
    for i in range(dots_ref.shape[0] // 8):
        total = total + dots_ref[8 * i : 8 * i + 8, :]
    square = jnp.concatenate([total, jnp.zeros((LANES - 8, LANES), F32)], 0)
    turned = jnp.transpose(square)
    odd = lane_ids(LANES) % 2 == 1
    even_sums = jnp.sum(jnp.where(odd, 0.0, turned), axis=1, keepdims=True)
    odd_sums = jnp.sum(jnp.where(odd, turned, 0.0), axis=1, keepdims=True)
    h = [even_sums[freqs * i : freqs * (i + 1)] for i in range(4)]
    h += [odd_sums[freqs * i : freqs * (i + 1)] for i in range(2)]
    weights = [jnp.broadcast_to(c, (freqs, LANES)) for c in coefficients(h)]
    quarter = LANES // 4
    cell = lane_ids(freqs) // quarter
    outs = (out0_ref, out1_ref, out2_ref, out3_ref)
    copy.wait()
    for k in range(2):
        spectra = [
            sum(
                weights[j] * strain_ref[pl.ds((2 * j + k) * freqs * 8 + c, freqs, stride=8), :]
                for j in range(3)
            )
            for c in range(comps)
        ]
        for step in range(4):
            dest = (freq_group + step) % 4
            for side in range(2):
                held = jnp.zeros((freqs, LANES), F32)
                for c in range(4 * side, min(comps, 4 * side + 4)):
                    moved = pltpu.roll(spectra[c], quarter * ((c + 4 - dest) % 4), 1)
                    held = jnp.where(cell == c % 4, moved, held)
                start = (2 * side + k) * freqs
                outs[step][start : start + freqs, :] = held


def final_kernel(
    curves_ref, part0_ref, part1_ref, part2_ref, part3_ref,
    table_high_ref, table_low_ref, modulus_ref, soil_ref,
    modulus_out_ref, strain_out_ref, spectra_ref,
):
    freq_group = lax.axis_index("freq")
    parts, freqs = 64, 32
    for step, part_ref in enumerate((part0_ref, part1_ref, part2_ref, part3_ref)):
        start = pl.multiple_of((freq_group + 4 - step) % 4 * parts, parts)
        for side in range(2):
            spectra_ref[pl.ds(start, parts), side * LANES : (side + 1) * LANES] = part_ref[
                side * parts : (side + 1) * parts, :
            ]
    high, low = halves(spectra_ref[...])
    table_high, table_low = table_high_ref[...], table_low_ref[...]
    history = (
        jnp.dot(table_high, low, preferred_element_type=F32)
        + jnp.dot(table_low, high, preferred_element_type=F32)
        + jnp.dot(table_high, high, preferred_element_type=F32)
    )
    squares = history[:, :LANES] ** 2 + history[:, LANES:] ** 2
    squares = squares + pltpu.roll(squares, 64, 1)
    squares = squares + pltpu.roll(squares, 32, 1)
    peak = jnp.max(squares, axis=0, keepdims=True)[:, : LANES // 4] * (1.0 / (4 * freqs))
    peak_strain = STRAIN_FACTOR * jnp.sqrt(peak + EPSILON)
    position = (jnp.log(peak_strain) * (1.0 / np.log(10.0)) - LOG_LOW) / LOG_STEP
    soil = soil_ref[...]
    ratio = jnp.zeros_like(position)
    for level in range(curves_ref.shape[1]):
        value = jnp.where(soil == 0, curves_ref[0, level], 0.0)
        for kind in range(1, curves_ref.shape[0]):
            value = jnp.where(soil == kind, curves_ref[kind, level], value)
        ratio = ratio + value * jnp.maximum(0.0, 1.0 - jnp.abs(position - level))
    own = pltpu.roll(modulus_ref[...], (LANES - LANES // 4 * freq_group) % LANES, 1)
    modulus_out_ref[...] = own[:, : LANES // 4] * ratio
    strain_out_ref[...] = peak_strain


def time_table(total_freq):
    order = np.arange(1, total_freq + 1)
    phase = (np.arange(NT)[:, None] * order[None, :] % NT) * (2.0 * np.pi / NT)
    waves = np.stack([np.cos(phase), -np.sin(phase)], 1)
    table = waves.reshape(NT, 2, 4, total_freq // 4).transpose(0, 2, 1, 3).reshape(NT, -1)
    high = table.astype(np.float32).astype(jnp.bfloat16)
    low = (table - high.astype(np.float64)).astype(np.float32).astype(jnp.bfloat16)
    return high, low


def per_device(
    load, stiffness, mass_template, modulus, element_mass, strain_map, curves, soil_type
):
    half, freq_dev, _, nodes = load.shape
    parts = 2 * freq_dev
    groups = lax.axis_size("freq")
    slabs = lax.axis_size("elem")
    rows = load.reshape(half * parts, nodes)
    modulus_row, mass_row = modulus.reshape(1, nodes), element_mass.reshape(1, nodes)
    edge_up, edge_down, lhs, cols = pl.pallas_call(
        edges_kernel,
        out_shape=[
            jax.ShapeDtypeStruct((UP_ROWS, LANES), F32),
            jax.ShapeDtypeStruct((DOWN_ROWS, LANES), F32),
            jax.ShapeDtypeStruct((4 * half + 16, 2 * LANES), BF16),
            jax.ShapeDtypeStruct((half, LANES), F32),
        ],
        in_specs=[HBM] + [VMEM] * 5,
        out_specs=[VMEM] * 4,
        scratch_shapes=[
            pltpu.VMEM((half * parts, LANES), F32),
            pltpu.VMEM((LANES, LANES), F32),
            pltpu.VMEM((LANES, LANES), F32),
            pltpu.VMEM((LANES, LANES), F32),
            pltpu.SemaphoreType.DMA((3,)),
        ],
        name="edges",
    )(rows, modulus_row, mass_row, stiffness, mass_template.reshape(1, -1), strain_map)
    from_left = lax.ppermute(edge_up, "elem", [(i, i + 1) for i in range(slabs - 1)])
    from_right = lax.ppermute(edge_down, "elem", [(i + 1, i) for i in range(slabs - 1)])
    strains, dots = pl.pallas_call(
        main_kernel,
        out_shape=[
            jax.ShapeDtypeStruct((3 * parts * 8, LANES), F32),
            jax.ShapeDtypeStruct((2 * slabs, LANES), F32),
        ],
        in_specs=[VMEM] * 6,
        out_specs=[HBM, VMEM],
        scratch_shapes=[
            pltpu.VMEM((3 * parts * 8, LANES), F32),
            pltpu.VMEM((parts, half, LANES), F32),
            pltpu.VMEM((freq_dev, half, LANES), F32),
            pltpu.VMEM((3, half + 8, LANES), F32),
            pltpu.VMEM((256, LANES), F32),
            pltpu.SemaphoreType.DMA((3,)),
        ],
        compiler_params=pltpu.CompilerParams(vmem_limit_bytes=32 * 1024 * 1024),
        name="krylov",
    )(rows, edge_down, from_left, from_right, lhs, cols)
    dots = lax.all_to_all(dots.reshape(slabs, 2, LANES), "elem", 0, 0).reshape(-1, LANES)
    outs = pl.pallas_call(
        combine_kernel,
        out_shape=[jax.ShapeDtypeStruct((2 * parts, LANES), F32)] * groups,
        in_specs=[VMEM, HBM],
        out_specs=[VMEM] * groups,
        scratch_shapes=[
            pltpu.VMEM((3 * parts * 8, LANES), F32),
            pltpu.SemaphoreType.DMA,
        ],
        name="combine",
    )(dots, strains)
    received = [outs[0]] + [
        lax.ppermute(outs[step], "freq", [(i, (i + step) % groups) for i in range(groups)])
        for step in range(1, groups)
    ]
    table_high, table_low = time_table(freq_dev * groups)
    quarter = nodes // groups
    new_modulus, peak_strain = pl.pallas_call(
        final_kernel,
        out_shape=[jax.ShapeDtypeStruct((1, quarter), F32)] * 2,
        in_specs=[SMEM] + [VMEM] * 8,
        out_specs=[VMEM] * 2,
        scratch_shapes=[pltpu.VMEM((groups * parts, 2 * LANES), F32)],
        compiler_params=pltpu.CompilerParams(vmem_limit_bytes=32 * 1024 * 1024),
        name="response",
    )(curves, *received, jnp.asarray(table_high), jnp.asarray(table_low),
      modulus_row, soil_type.reshape(1, quarter))
    return new_modulus.reshape(quarter), peak_strain.reshape(quarter)


def solution(mesh):
    in_specs = (
        P(None, "freq", None, "elem"),
        P(),
        P(),
        P("elem"),
        P("elem"),
        P(),
        P(),
        P(("elem", "freq")),
    )
    out_specs = (P(("elem", "freq")), P(("elem", "freq")))
    return jax.shard_map(
        per_device, mesh=mesh, in_specs=in_specs, out_specs=out_specs, check_vma=False
    )
```

```python
import jax
import jax.numpy as jnp
import numpy as np
from jax import lax
from jax.experimental import pallas as pl
from jax.experimental.pallas import tpu as pltpu
from jax.sharding import PartitionSpec as P

NT = 512
MASS_COEF = 0.5
LOG_LOW = -1.5
LOG_STEP = 0.2
STRAIN_FACTOR = 0.65
EPSILON = 1e-06
LANES = 128
SLOT = 8
DEPTH = 176
UNROLL = 32
DOTS = 6
F32 = jnp.float32
BF16 = jnp.bfloat16
VMEM = pl.BlockSpec(memory_space=pltpu.VMEM)
SMEM = pl.BlockSpec(memory_space=pltpu.SMEM)
HBM = pl.BlockSpec(memory_space=pltpu.HBM)
PAIR_ROWS, ROW_AT = 96, 96
UP_ROWS, DOWN_ROWS = 104, 152


def lane_ids(rows=1):
    return lax.broadcasted_iota(jnp.int32, (rows, LANES), 1)


def later(x):
    return pltpu.roll(x, 127, 1)


def earlier(x):
    return pltpu.roll(x, 1, 1)


def halves(x):
    high = x.astype(BF16)
    return high, (x - high.astype(F32)).astype(BF16)


def edges_kernel(
    load_ref, modulus_ref, mass_ref, stiffness_ref, template_ref, strain_map_ref,
    up_ref, down_ref, own_ref, lhs_ref, cols_ref,
    buffer_ref, slots_ref, turned_ref, square_ref, small_ref, copied,
):
    half, parts, chunks = 48, 64, 3
    per = half // chunks
    length = per * parts
    full = 2 * half
    comps = strain_map_ref.shape[0]
    copies = [
        pltpu.make_async_copy(
            load_ref.at[pl.ds(i * length, length)], buffer_ref.at[pl.ds(i * length, length)],
            copied.at[i],
        )
        for i in range(chunks)
    ]
    smalls = [
        pltpu.make_async_copy(source, target, copied.at[chunks + i])
        for i, (source, target) in enumerate((
            (modulus_ref, small_ref.at[0]), (mass_ref, small_ref.at[1]),
        ))
    ]
    square_ref[...] = jnp.zeros(square_ref.shape, F32)
    for copy in copies + smalls:
        copy.start()

    square_ref[:full, :full] = stiffness_ref[...]
    square_ref[full : full + comps, :full] = strain_map_ref[...]
    square_ref[full + 8 : full + 9, :full] = template_ref[...]
    stiff = square_ref[:full, :]
    same = lax.broadcasted_iota(jnp.int32, (full, LANES), 0) == lane_ids(full)
    kdiag = jnp.sum(jnp.where(same, stiff, 0.0), axis=1, keepdims=True)
    template = jnp.sum(
        jnp.where(same, square_ref[full + 8 : full + 9, :], 0.0), axis=1, keepdims=True
    )
    lane = lane_ids(half)
    columns = jnp.zeros((half, LANES), F32)
    for i, col in enumerate((kdiag[:half], kdiag[half:], template[:half], template[half:])):
        columns = jnp.where(lane == i, col, columns)
    cols_ref[...] = columns
    off = jnp.where(same, 0.0, stiff)
    strain_rows = square_ref[full : full + 8, :]
    moved = pltpu.roll(off, LANES - half, 1)
    moved_rows = pltpu.roll(strain_rows, LANES - half, 1)
    stacked = jnp.concatenate(
        [off[:half], moved[half:], moved[:half], off[half:], strain_rows, moved_rows], 0
    )
    rows = stacked.shape[0]
    lane = lane_ids(rows)
    stacked = jnp.where(lane < half, stacked, 0.0)
    high, low = halves(stacked)
    high = high.astype(F32)
    lhs_ref[:, :LANES] = (high + pltpu.roll(high, half, 1)).astype(BF16)
    lhs_ref[:, LANES:] = low

    slot = lane_ids(parts) // SLOT
    for chunk in range(chunks):
        copies[chunk].wait()
        held = jnp.zeros((parts, LANES), F32)
        for i in range(per):
            start = (chunk * per + i) * parts
            moved = pltpu.roll(buffer_ref[start : start + parts, :], 2 + SLOT * i, 1)
            held = jnp.where(slot == i, moved, held)
        at = chunk * per
        for turn, shift in enumerate((LANES - 1, LANES - 3)):
            slots_ref[pl.ds(0, parts, stride=2), :] = held
            slots_ref[pl.ds(1, parts, stride=2), :] = pltpu.roll(held, shift, 1)
            turned_ref[...] = jnp.transpose(slots_ref[...])
            if turn == 0:
                pair = turned_ref[pl.ds(1, per, stride=SLOT), :]
                for ref in (up_ref, down_ref, own_ref):
                    ref[at : at + per, :] = pair
            else:
                pair = turned_ref[pl.ds(0, per, stride=SLOT), :]
                for ref in (up_ref, down_ref, own_ref):
                    ref[half + at : half + at + per, :] = pair
                down_ref[UP_ROWS + at : UP_ROWS + at + per, :] = turned_ref[
                    pl.ds(1, per, stride=SLOT), :
                ]
    for copy in smalls:
        copy.wait()
    for ref in (up_ref, down_ref, own_ref):
        ref[ROW_AT : ROW_AT + 1, :] = small_ref[0]
        ref[ROW_AT + 1 : ROW_AT + 2, :] = small_ref[1]
        ref[ROW_AT + 2 : UP_ROWS, :] = jnp.zeros((UP_ROWS - ROW_AT - 2, LANES), F32)


def main_kernel(
    load_ref, own_ref, left_ref, right_ref, lhs_ref, cols_ref,
    out0_ref, out1_ref, out2_ref, out3_ref, dots_out_ref,
    strain_ref, field_ref, inv_ref, border_ref, dots_ref,
):
    half, parts = 48, 64
    freqs = parts // 2
    freq_group = lax.axis_index("freq")
    is_last = lax.axis_index("elem") == lax.axis_size("elem") - 1
    first_order = (freq_group * freqs + 1).astype(F32)
    lanes = lane_ids()
    even = lanes % 2 == 0

    def shift_of(order):
        return MASS_COEF * (order * (1.0 / (4 * freqs))) ** 2

    cols = cols_ref[...]
    kd_top, kd_low, mt_top, mt_low = (cols[:, i : i + 1] for i in range(4))

    def rows_of(at):
        own, left, right = (
            r[ROW_AT + at : ROW_AT + at + 1, :] for r in (own_ref, left_ref, right_ref)
        )
        prev = jnp.where(lanes == 0, earlier(left), earlier(own))

        def sides(*upper_lower):
            (upper, i), (lower, j) = upper_lower
            upper, lower = upper[:, i : i + 1], lower[:, j : j + 1]
            return jnp.where(even, upper, lower)

        zero = jnp.zeros_like(own)
        pairs = [
            (sides((own, 126), (own, 1)), sides((own, 125), (own, 0))),
            (sides((own, 127), (own, 0)), sides((own, 126), (left, 127))),
            (sides((right, 0), (left, 127)), sides((own, 127), (left, 126))),
            (sides((right, 1), (left, 126)), sides((right, 0), (left, 125))),
            (sides((right, 2), (zero, 0)), sides((right, 1), (zero, 0))),
        ]
        return (own, prev), pairs

    mod_main, mod_pairs = rows_of(0)
    mass_main, mass_pairs = rows_of(1)

    def diagonals(mod, mass):
        return kd_top * mod[0] + kd_low * mod[1], mt_top * mass[0] + mt_low * mass[1]

    lhs = lhs_ref[:, :DEPTH]
    blank = jnp.zeros((DEPTH - 3 * half, 2 * LANES), BF16)

    def products(*fields):
        split = [halves(field) for field in fields]
        high = jnp.concatenate([h for h, _ in split], 1)
        low = jnp.concatenate([l for _, l in split], 1)
        gap = blank[:, : high.shape[1]]
        result = jnp.dot(
            lhs, jnp.concatenate([high, low, gap, high], 0), preferred_element_type=F32
        )
        cut = [half * i for i in range(5)] + [4 * half + 8, 4 * half + 16]
        return [
            [result[cut[i] : cut[i + 1], LANES * k : LANES * (k + 1)] for i in range(6)]
            for k in range(len(fields))
        ]

    order = first_order + (lanes // 4).astype(F32)
    beyond = jnp.logical_and(even, is_last)
    inverses = []
    for i, (mod, mass) in enumerate(zip(mod_pairs, mass_pairs)):
        stiff, weight = diagonals(mod, mass)
        diag = stiff + shift_of(order) * weight
        good = diag > 0
        if i >= 2:
            good = jnp.logical_and(good, jnp.logical_not(beyond))
        inverses.append(jnp.where(good, 1.0 / diag, 0.0))

    def met(at):
        inward = later(right_ref[at : at + half, :])
        return jnp.where(even, inward, earlier(left_ref[at : at + half, :]))

    rims = [
        own_ref[half : 2 * half, :],
        own_ref[:half, :],
        met(0),
        met(half),
        jnp.where(even, later(right_ref[UP_ROWS:, :]), 0.0),
    ]
    rims = [field * inv for field, inv in zip(rims, inverses)]

    def rim_stage(stage, rims):
        first = stage
        z = {}
        for i in range(first, len(rims), 2):
            names = list(range(i, min(i + 2, len(rims))))
            for name, value in zip(names, products(*(rims[name] for name in names))):
                z[name] = value
        at_edge = mod_pairs[1]
        outer = z[2]
        if stage < 2:
            border = jnp.where(even, at_edge[0] * outer[2], at_edge[1] * outer[3])
            tail = outer[5]
        else:
            border = jnp.where(even, at_edge[0] * outer[2], 0.0)
            energy = jnp.sum(at_edge[0] * rims[2] * outer[1], axis=0, keepdims=True)
            row = lax.broadcasted_iota(jnp.int32, (8, LANES), 0)
            tail = jnp.where(row == 6, energy, outer[5])
        border_ref[stage, :half, :] = border
        border_ref[stage, half:, :] = jnp.where(even, tail, 0.0)
        nexts = [None] * len(rims)
        for i in range(first + 1, len(rims) - 1):
            above = jnp.where(even, z[i + 1][2], z[i - 1][2])
            below = jnp.where(even, z[i - 1][3], z[i + 1][3])
            top, low = mod_pairs[i]
            nexts[i] = -inverses[i] * (top * (z[i][0] + above) + low * (z[i][1] + below))
        return nexts[: len(rims) - 1]

    stiff_main, mass_diag_main = diagonals(mod_main, mass_main)
    mod_own, mod_prev = mod_main
    mod_sent_up = jnp.where(lanes == 127, 0.0, mod_own)
    mod_sent_down = jnp.where(lanes == 0, 0.0, mod_prev)
    rim = jnp.logical_or(lanes == 0, lanes == 127)

    def borders(stage, f, k):
        moved = pltpu.roll(border_ref[stage], LANES - 1 - 2 * (2 * f + k), 1)
        moved = jnp.where(rim, moved, 0.0)
        return moved[:half], moved[half:]

    def strain_of(top, low, added):
        return top + jnp.where(lanes == 127, 0.0, later(low)) + added

    def put_dot(which, f, pairs):
        total = sum(a * b for a, b in pairs)
        dots_ref[pl.ds(which * freqs + f, 1), :] = jnp.sum(total, axis=0, keepdims=True)

    def put_strain(stage, f, k, value):
        start = ((stage * 2 + k) * freqs + f) * 8
        strain_ref[pl.ds(pl.multiple_of(start, 8), 8), :] = value

    def images(f, stage, fields):
        result = []
        for k, z in enumerate(products(*fields)):
            z11, z22, z12, z21, s_top, s_low = z
            added, added_strain = borders(stage, f, k)
            image = (
                mod_own * z11 + mod_prev * z22 + later(mod_sent_down * z12)
                + earlier(mod_sent_up * z21) + added
            )
            put_strain(stage, f, k, strain_of(s_top, s_low, added_strain))
            result.append(-image)
        return result

    def first(f, carry):
        inv = 1.0 / (stiff_main + shift_of(first_order + f.astype(F32)) * mass_diag_main)
        inv_ref[f] = inv
        loads = [load_ref[pl.ds(2 * f + k, half, stride=parts), :] for k in range(2)]
        fields = [inv * b for b in loads]
        image = images(f, 0, fields)
        nexts = [inv * t for t in image]
        for k in range(2):
            field_ref[2 * f + k] = nexts[k]
        put_dot(0, f, zip(fields, loads))
        put_dot(1, f, zip(fields, image))
        put_dot(2, f, zip(nexts, image))
        return carry

    def second(f, carry):
        inv = inv_ref[f]
        fields = [field_ref[2 * f + k] for k in range(2)]
        image = images(f, 1, fields)
        nexts = [inv * t for t in image]
        for k in range(2):
            field_ref[2 * f + k] = nexts[k]
        put_dot(3, f, zip(fields, image))
        put_dot(4, f, zip(nexts, image))
        return carry

    def third(f, carry):
        fields = [field_ref[2 * f + k] for k in range(2)]
        total, extra = 0.0, 0.0
        for k, z in enumerate(products(*fields)):
            z11, z22, z12, _, s_top, s_low = z
            added, added_strain = borders(2, f, k)
            twice = 2.0 * (later(mod_sent_down * z12) + added)
            total = total + fields[k] * (mod_own * z11 + mod_sent_down * z22 + twice)
            strain = strain_of(s_top, s_low, added_strain)
            put_strain(2, f, k, strain)
            extra = extra + strain[6:7]
        dots_ref[pl.ds(5 * freqs + f, 1), :] = -(jnp.sum(total, axis=0, keepdims=True) + extra)
        return carry

    quarter = LANES // 4
    cell = lane_ids(8) // quarter
    outs = (out0_ref, out1_ref, out2_ref, out3_ref)

    def pack(stage, block):
        def comp(k, c):
            start = (((stage * 2 + k) * freqs) + block * 8) * 8 + c
            return strain_ref[pl.ds(start, 8, stride=8), :]

        comps = {(k, c): comp(k, c) for k in range(2) for c in range(6)}
        places = [
            (stage * parts + k * freqs, [(k, c) for c in range(4)]) for k in range(2)
        ] + [(3 * parts + stage * freqs, [(0, 4), (0, 5), (1, 4), (1, 5)])]
        for step in range(4):
            dest = (freq_group + step) % 4
            for row, names in places:
                held = None
                for i, name in enumerate(names):
                    moved = pltpu.roll(comps[name], quarter * ((i + 4 - dest) % 4), 1)
                    held = moved if held is None else jnp.where(cell == i, moved, held)
                outs[step][row + block * 8 : row + block * 8 + 8, :] = held

    for stage, step in enumerate((first, second, third)):
        rims = rim_stage(stage, rims)
        lax.fori_loop(0, freqs, step, 0, unroll=UNROLL)
        for block in range(freqs // 8):
            pack(stage, block)

    dots_ref[DOTS * freqs :, :] = jnp.zeros((256 - DOTS * freqs, LANES), F32)
    sums = lax.dot_general(
        jnp.ones((8, LANES), F32), dots_ref[...], (((1,), (1,)), ((), ())),
        precision=lax.Precision.HIGHEST, preferred_element_type=F32,
    )
    row = lax.broadcasted_iota(jnp.int32, (8, LANES), 0)
    pair = jnp.where(row % 2 == 0, sums[:, :LANES], sums[:, LANES:])
    for i in range(dots_out_ref.shape[0] // 8):
        dots_out_ref[8 * i : 8 * i + 8, :] = pair


def coefficients(h):
    def dot(a, b, energy):
        total = None
        for i, x in enumerate(a):
            for j, y in enumerate(b):
                weight = h[i + j] - h[i + j + 1] if energy else h[i + j]
                term = x * y * weight
                total = term if total is None else total + term
        return total

    one = jnp.ones_like(h[0])
    residual, direction = [one], [one]
    rho = h[0]
    result = []
    for iteration in range(3):
        alpha = rho / dot(direction, direction, True)
        result = [
            (result[i] if i < len(result) else 0.0) + alpha * direction[i]
            for i in range(len(direction))
        ]
        if iteration == 2:
            break
        image = (
            [direction[0]]
            + [direction[i] - direction[i - 1] for i in range(1, len(direction))]
            + [-direction[-1]]
        )
        residual = [
            (residual[i] if i < len(residual) else 0.0) - alpha * image[i]
            for i in range(len(image))
        ]
        rho_next = dot(residual, residual, False)
        beta = rho_next / rho
        rho = rho_next
        direction = [
            residual[i] + (beta * direction[i] if i < len(direction) else 0.0)
            for i in range(len(residual))
        ]
    return result


def final_kernel(
    curves_ref, dots_ref, part0_ref, part1_ref, part2_ref, part3_ref,
    table_high_ref, table_low_ref, modulus_ref, soil_ref,
    modulus_out_ref, strain_out_ref, spectra_ref,
):
    freq_group = lax.axis_index("freq")
    parts, freqs = 64, 32
    total = jnp.zeros((8, LANES), F32)
    for i in range(dots_ref.shape[0] // 8):
        total = total + dots_ref[8 * i : 8 * i + 8, :]
    square = jnp.concatenate([total, jnp.zeros((LANES - 8, LANES), F32)], 0)
    turned = jnp.transpose(square)
    beside = pltpu.roll(turned, 127, 1)
    h = [turned[freqs * i : freqs * (i + 1)] for i in range(4)]
    h += [beside[freqs * i : freqs * (i + 1)] for i in range(2)]
    coefs = coefficients(h)
    lanes = lane_ids(freqs)
    for step, part_ref in enumerate((part0_ref, part1_ref, part2_ref, part3_ref)):
        source = (freq_group + 4 - step) % 4
        weights = [
            jnp.sum(jnp.where(lanes == 2 * source, c, 0.0), axis=1, keepdims=True) for c in coefs
        ]

        def joined(base, per_stage):
            return sum(
                weights[j] * part_ref[base + j * per_stage : base + j * per_stage + freqs, :]
                for j in range(3)
            )

        rest = joined(3 * parts, freqs)
        for k in range(2):
            start = pl.multiple_of(source * parts + k * freqs, freqs)
            spectra_ref[pl.ds(start, freqs), :LANES] = joined(k * freqs, parts)
            side = pltpu.roll(rest, 64, 1) if k else rest
            spectra_ref[pl.ds(start, freqs), LANES:] = jnp.where(lanes < 64, side, 0.0)
    high, low = halves(spectra_ref[...])
    table_high, table_low = table_high_ref[...], table_low_ref[...]
    history = (
        jnp.dot(table_high, low, preferred_element_type=F32)
        + jnp.dot(table_low, high, preferred_element_type=F32)
        + jnp.dot(table_high, high, preferred_element_type=F32)
    )
    squares = history[:, :LANES] ** 2 + history[:, LANES:] ** 2
    squares = squares + pltpu.roll(squares, 64, 1)
    squares = squares + pltpu.roll(squares, 32, 1)
    peak = jnp.max(squares, axis=0, keepdims=True)[:, : LANES // 4] * (1.0 / (4 * freqs))
    peak_strain = STRAIN_FACTOR * jnp.sqrt(peak + EPSILON)
    position = (jnp.log(peak_strain) * (1.0 / np.log(10.0)) - LOG_LOW) / LOG_STEP
    soil = soil_ref[...]
    ratio = jnp.zeros_like(position)
    for level in range(curves_ref.shape[1]):
        value = jnp.where(soil == 0, curves_ref[0, level], 0.0)
        for kind in range(1, curves_ref.shape[0]):
            value = jnp.where(soil == kind, curves_ref[kind, level], value)
        ratio = ratio + value * jnp.maximum(0.0, 1.0 - jnp.abs(position - level))
    own = pltpu.roll(modulus_ref[...], (LANES - LANES // 4 * freq_group) % LANES, 1)
    modulus_out_ref[...] = own[:, : LANES // 4] * ratio
    strain_out_ref[...] = peak_strain


def time_table(total_freq):
    order = np.arange(1, total_freq + 1)
    phase = (np.arange(NT)[:, None] * order[None, :] % NT) * (2.0 * np.pi / NT)
    waves = np.stack([np.cos(phase), -np.sin(phase)], 1)
    table = waves.reshape(NT, 2, 4, total_freq // 4).transpose(0, 2, 1, 3).reshape(NT, -1)
    high = table.astype(np.float32).astype(jnp.bfloat16)
    low = (table - high.astype(np.float64)).astype(np.float32).astype(jnp.bfloat16)
    return high, low


def per_device(
    load, stiffness, mass_template, modulus, element_mass, strain_map, curves, soil_type
):
    half, freq_dev, _, nodes = load.shape
    parts = 2 * freq_dev
    groups = lax.axis_size("freq")
    slabs = lax.axis_size("elem")
    rows = load.reshape(half * parts, nodes)
    modulus_row, mass_row = modulus.reshape(1, nodes), element_mass.reshape(1, nodes)
    edge_up, edge_down, edge_own, lhs, cols = pl.pallas_call(
        edges_kernel,
        out_shape=[
            pltpu.VMEM((UP_ROWS, LANES), F32),
            pltpu.VMEM((DOWN_ROWS, LANES), F32),
            pltpu.VMEM((UP_ROWS, LANES), F32),
            pltpu.VMEM((4 * half + 16, 2 * LANES), BF16),
            pltpu.VMEM((half, LANES), F32),
        ],
        in_specs=[HBM] * 3 + [VMEM] * 3,
        out_specs=[VMEM] * 5,
        scratch_shapes=[
            pltpu.VMEM((half * parts, LANES), F32),
            pltpu.VMEM((LANES, LANES), F32),
            pltpu.VMEM((LANES, LANES), F32),
            pltpu.VMEM((LANES, LANES), F32),
            pltpu.VMEM((2, 1, LANES), F32),
            pltpu.SemaphoreType.DMA((5,)),
        ],
        name="edges",
    )(rows, modulus_row, mass_row, stiffness, mass_template.reshape(1, -1), strain_map)
    from_left = lax.ppermute(edge_up, "elem", [(i, i + 1) for i in range(slabs - 1)])
    from_right = lax.ppermute(edge_down, "elem", [(i + 1, i) for i in range(slabs - 1)])
    packed = 9 * freq_dev
    outs = pl.pallas_call(
        main_kernel,
        out_shape=[jax.ShapeDtypeStruct((packed, LANES), F32)] * 4
        + [jax.ShapeDtypeStruct((2 * slabs * groups, LANES), F32)],
        in_specs=[VMEM] * 6,
        out_specs=[VMEM] * 5,
        scratch_shapes=[
            pltpu.VMEM((3 * parts * 8, LANES), F32),
            pltpu.VMEM((parts, half, LANES), F32),
            pltpu.VMEM((freq_dev, half, LANES), F32),
            pltpu.VMEM((3, half + 8, LANES), F32),
            pltpu.VMEM((256, LANES), F32),
        ],
        compiler_params=pltpu.CompilerParams(vmem_limit_bytes=32 * 1024 * 1024),
        name="krylov",
    )(rows, edge_own, from_left, from_right, lhs, cols)
    received = [outs[0]] + [
        lax.ppermute(outs[step], "freq", [(i, (i + step) % groups) for i in range(groups)])
        for step in range(1, groups)
    ]
    dots = lax.all_to_all(
        outs[4].reshape(slabs * groups, 2, LANES), ("elem", "freq"), 0, 0
    ).reshape(-1, LANES)
    table_high, table_low = time_table(freq_dev * groups)
    quarter = nodes // groups
    new_modulus, peak_strain = pl.pallas_call(
        final_kernel,
        out_shape=[jax.ShapeDtypeStruct((1, quarter), F32)] * 2,
        in_specs=[SMEM] + [VMEM] * 9,
        out_specs=[VMEM] * 2,
        scratch_shapes=[pltpu.VMEM((groups * parts, 2 * LANES), F32)],
        compiler_params=pltpu.CompilerParams(vmem_limit_bytes=32 * 1024 * 1024),
        name="response",
    )(curves, dots, *received, jnp.asarray(table_high), jnp.asarray(table_low),
      modulus_row, soil_type.reshape(1, quarter))
    return new_modulus.reshape(quarter), peak_strain.reshape(quarter)


def solution(mesh):
    in_specs = (
        P(None, "freq", None, "elem"),
        P(),
        P(),
        P("elem"),
        P("elem"),
        P(),
        P(),
        P(("elem", "freq")),
    )
    out_specs = (P(("elem", "freq")), P(("elem", "freq")))
    return jax.shard_map(
        per_device, mesh=mesh, in_specs=in_specs, out_specs=out_specs, check_vma=False
    )
```

```python
import jax
import jax.numpy as jnp
import numpy as np
from jax import lax
from jax.experimental import pallas as pl
from jax.experimental.pallas import tpu as pltpu
from jax.sharding import PartitionSpec as P

NT = 512
MASS_COEF = 0.5
LOG_LOW = -1.5
LOG_STEP = 0.2
STRAIN_FACTOR = 0.65
EPSILON = 1e-06
LANES = 128
SLOT = 8
DEPTH = 176
UNROLL = 32
DOTS = 6
F32 = jnp.float32
BF16 = jnp.bfloat16
VMEM = pl.BlockSpec(memory_space=pltpu.VMEM)
SMEM = pl.BlockSpec(memory_space=pltpu.SMEM)
HBM = pl.BlockSpec(memory_space=pltpu.HBM)
OWN_ROWS, OWN_AT = 104, 96
SENT_ROWS, SENT_AT = 80, 72


def lane_ids(rows=1):
    return lax.broadcasted_iota(jnp.int32, (rows, LANES), 1)


def later(x):
    return pltpu.roll(x, 127, 1)


def earlier(x):
    return pltpu.roll(x, 1, 1)


def halves(x):
    high = x.astype(BF16)
    return high, (x - high.astype(F32)).astype(BF16)


def edges_kernel(
    load_ref, modulus_ref, mass_ref, stiffness_ref, template_ref, strain_map_ref,
    first_ref, second_ref, own_ref, lhs_ref, cols_ref, buffer_ref,
    slots_ref, turned_ref, square_ref, small_ref, third_ref, copied,
):
    half, parts, chunks = 48, 64, 3
    per = half // chunks
    length = per * parts
    full = 2 * half
    comps = strain_map_ref.shape[0]
    copies = [
        pltpu.make_async_copy(
            load_ref.at[pl.ds(i * length, length)], buffer_ref.at[pl.ds(i * length, length)],
            copied.at[i],
        )
        for i in range(chunks)
    ]
    smalls = [
        pltpu.make_async_copy(source, target, copied.at[chunks + i])
        for i, (source, target) in enumerate((
            (modulus_ref, small_ref.at[0]), (mass_ref, small_ref.at[1]),
        ))
    ]
    for copy in copies + smalls:
        copy.start()
    square_ref[...] = jnp.zeros(square_ref.shape, F32)

    square_ref[:full, :full] = stiffness_ref[...]
    square_ref[full : full + comps, :full] = strain_map_ref[...]
    square_ref[full + 8 : full + 9, :full] = template_ref[...]
    stiff = square_ref[:full, :]
    same = lax.broadcasted_iota(jnp.int32, (full, LANES), 0) == lane_ids(full)
    kdiag = jnp.sum(jnp.where(same, stiff, 0.0), axis=1, keepdims=True)
    template = jnp.sum(
        jnp.where(same, square_ref[full + 8 : full + 9, :], 0.0), axis=1, keepdims=True
    )
    lane = lane_ids(half)
    columns = jnp.zeros((half, LANES), F32)
    for i, col in enumerate((kdiag[:half], kdiag[half:], template[:half], template[half:])):
        columns = jnp.where(lane == i, col, columns)
    cols_ref[...] = columns
    off = jnp.where(same, 0.0, stiff)
    strain_rows = square_ref[full : full + 8, :]
    moved = pltpu.roll(off, LANES - half, 1)
    moved_rows = pltpu.roll(strain_rows, LANES - half, 1)
    stacked = jnp.concatenate(
        [off[:half], moved[half:], moved[:half], off[half:], strain_rows, moved_rows], 0
    )
    rows = stacked.shape[0]
    lane = lane_ids(rows)
    stacked = jnp.where(lane < half, stacked, 0.0)
    high, low = halves(stacked)
    high = high.astype(F32)
    lhs_ref[:, :LANES] = (high + pltpu.roll(high, half, 1)).astype(BF16)
    lhs_ref[:, LANES:] = low

    slot = lane_ids(parts) // SLOT
    for chunk in range(chunks):
        copies[chunk].wait()
        held = jnp.zeros((parts, LANES), F32)
        for i in range(per):
            start = (chunk * per + i) * parts
            moved = pltpu.roll(buffer_ref[start : start + parts, :], 2 + SLOT * i, 1)
            held = jnp.where(slot == i, moved, held)
        at = chunk * per
        for turn, shift in enumerate((LANES - 1, LANES - 3)):
            slots_ref[pl.ds(0, parts, stride=2), :] = held
            slots_ref[pl.ds(1, parts, stride=2), :] = pltpu.roll(held, shift, 1)
            turned_ref[...] = jnp.transpose(slots_ref[...])
            if turn == 0:
                own_ref[at : at + per, :] = turned_ref[pl.ds(1, per, stride=SLOT), :]
            else:
                own_ref[half + at : half + at + per, :] = turned_ref[pl.ds(0, per, stride=SLOT), :]
                third_ref[at : at + per, :] = turned_ref[pl.ds(1, per, stride=SLOT), :]
    for copy in smalls:
        copy.wait()
    own_ref[OWN_AT : OWN_AT + 1, :] = small_ref[0]
    own_ref[OWN_AT + 1 : OWN_AT + 2, :] = small_ref[1]
    own_ref[OWN_AT + 2 :, :] = jnp.zeros((OWN_ROWS - OWN_AT - 2, LANES), F32)
    even = lane_ids() % 2 == 0
    outer, inner = own_ref[:half, :], own_ref[half : 2 * half, :]
    third = third_ref[...]
    up = [jnp.where(even, outer, earlier(inner)), jnp.zeros((half // 2, LANES), F32)]
    down = [
        jnp.where(even, later(inner), outer),
        jnp.where(even, later(third[half // 2 :]), third[: half // 2]),
    ]
    even_device = lax.axis_index("elem") % 2 == 0
    for ref, ahead in ((first_ref, even_device), (second_ref, jnp.logical_not(even_device))):
        ref[:half, :] = jnp.where(ahead, up[0], down[0])
        ref[half:SENT_AT, :] = jnp.where(ahead, up[1], down[1])
        ref[SENT_AT:, :] = own_ref[OWN_AT:, :]


def main_kernel(
    load_ref, own_ref, first_ref, second_ref, lhs_ref, cols_ref,
    out0_ref, out1_ref, out2_ref, out3_ref, dots_out_ref,
    strain_ref, field_ref, inv_ref, border_ref, dots_ref,
):
    half, parts = 48, 64
    freqs = parts // 2
    freq_group = lax.axis_index("freq")
    slab = lax.axis_index("elem")
    is_last = slab == lax.axis_size("elem") - 1
    ahead = slab % 2 == 0
    met_first, met_second = first_ref[...], second_ref[...]
    from_right = jnp.where(ahead, met_first, met_second)
    from_left = jnp.where(ahead, met_second, met_first)
    first_order = (freq_group * freqs + 1).astype(F32)
    lanes = lane_ids()
    even = lanes % 2 == 0

    def shift_of(order):
        return MASS_COEF * (order * (1.0 / (4 * freqs))) ** 2

    cols = cols_ref[...]
    kd_top, kd_low, mt_top, mt_low = (cols[:, i : i + 1] for i in range(4))

    def rows_of(at):
        own = own_ref[OWN_AT + at : OWN_AT + at + 1, :]
        left, right = (r[SENT_AT + at : SENT_AT + at + 1] for r in (from_left, from_right))
        prev = jnp.where(lanes == 0, earlier(left), earlier(own))

        def sides(*upper_lower):
            (upper, i), (lower, j) = upper_lower
            upper, lower = upper[:, i : i + 1], lower[:, j : j + 1]
            return jnp.where(even, upper, lower)

        zero = jnp.zeros_like(own)
        pairs = [
            (sides((own, 126), (own, 1)), sides((own, 125), (own, 0))),
            (sides((own, 127), (own, 0)), sides((own, 126), (left, 127))),
            (sides((right, 0), (left, 127)), sides((own, 127), (left, 126))),
            (sides((right, 1), (left, 126)), sides((right, 0), (left, 125))),
            (sides((right, 2), (zero, 0)), sides((right, 1), (zero, 0))),
        ]
        return (own, prev), pairs

    mod_main, mod_pairs = rows_of(0)
    mass_main, mass_pairs = rows_of(1)

    def diagonals(mod, mass):
        return kd_top * mod[0] + kd_low * mod[1], mt_top * mass[0] + mt_low * mass[1]

    lhs = lhs_ref[:, :DEPTH]
    blank = jnp.zeros((DEPTH - 3 * half, 2 * LANES), BF16)

    def products(*fields):
        split = [halves(field) for field in fields]
        high = jnp.concatenate([h for h, _ in split], 1)
        low = jnp.concatenate([l for _, l in split], 1)
        gap = blank[:, : high.shape[1]]
        result = jnp.dot(
            lhs, jnp.concatenate([high, low, gap, high], 0), preferred_element_type=F32
        )
        cut = [half * i for i in range(5)] + [4 * half + 8, 4 * half + 16]
        return [
            [result[cut[i] : cut[i + 1], LANES * k : LANES * (k + 1)] for i in range(6)]
            for k in range(len(fields))
        ]

    order = first_order + (lanes // 4).astype(F32)
    beyond = jnp.logical_and(even, is_last)
    inverses = []
    for i, (mod, mass) in enumerate(zip(mod_pairs, mass_pairs)):
        stiff, weight = diagonals(mod, mass)
        diag = stiff + shift_of(order) * weight
        good = diag > 0
        if i >= 2:
            good = jnp.logical_and(good, jnp.logical_not(beyond))
        inverses.append(jnp.where(good, 1.0 / diag, 0.0))

    third = from_right[half:SENT_AT]
    rims = [
        own_ref[half : 2 * half, :],
        own_ref[:half, :],
        jnp.where(even, later(from_right[:half]), earlier(from_left[:half])),
        jnp.where(even, from_right[:half], from_left[:half]),
        jnp.where(even, jnp.concatenate([later(third), third], 0), 0.0),
    ]
    rims = [field * inv for field, inv in zip(rims, inverses)]

    def rim_stage(stage, rims):
        first = stage
        z = {}
        for i in range(first, len(rims), 2):
            names = list(range(i, min(i + 2, len(rims))))
            for name, value in zip(names, products(*(rims[name] for name in names))):
                z[name] = value
        at_edge = mod_pairs[1]
        outer = z[2]
        if stage < 2:
            border = jnp.where(even, at_edge[0] * outer[2], at_edge[1] * outer[3])
            tail = outer[5]
        else:
            border = jnp.where(even, at_edge[0] * outer[2], 0.0)
            energy = jnp.sum(at_edge[0] * rims[2] * outer[1], axis=0, keepdims=True)
            row = lax.broadcasted_iota(jnp.int32, (8, LANES), 0)
            tail = jnp.where(row == 6, energy, outer[5])
        border_ref[stage, :half, :] = border
        border_ref[stage, half:, :] = jnp.where(even, tail, 0.0)
        nexts = [None] * len(rims)
        for i in range(first + 1, len(rims) - 1):
            above = jnp.where(even, z[i + 1][2], z[i - 1][2])
            below = jnp.where(even, z[i - 1][3], z[i + 1][3])
            top, low = mod_pairs[i]
            nexts[i] = -inverses[i] * (top * (z[i][0] + above) + low * (z[i][1] + below))
        return nexts[: len(rims) - 1]

    stiff_main, mass_diag_main = diagonals(mod_main, mass_main)
    mod_own, mod_prev = mod_main
    mod_sent_up = jnp.where(lanes == 127, 0.0, mod_own)
    mod_sent_down = jnp.where(lanes == 0, 0.0, mod_prev)
    rim = jnp.logical_or(lanes == 0, lanes == 127)

    def borders(stage, f, k):
        moved = pltpu.roll(border_ref[stage], LANES - 1 - 2 * (2 * f + k), 1)
        moved = jnp.where(rim, moved, 0.0)
        return moved[:half], moved[half:]

    def strain_of(top, low, added):
        return top + jnp.where(lanes == 127, 0.0, later(low)) + added

    def put_dot(which, f, pairs):
        total = sum(a * b for a, b in pairs)
        dots_ref[pl.ds(which * freqs + f, 1), :] = jnp.sum(total, axis=0, keepdims=True)

    def put_strain(stage, f, k, value):
        start = ((stage * 2 + k) * freqs + f) * 8
        strain_ref[pl.ds(pl.multiple_of(start, 8), 8), :] = value

    def images(f, stage, fields):
        result = []
        for k, z in enumerate(products(*fields)):
            z11, z22, z12, z21, s_top, s_low = z
            added, added_strain = borders(stage, f, k)
            image = (
                mod_own * z11 + mod_prev * z22 + later(mod_sent_down * z12)
                + earlier(mod_sent_up * z21) + added
            )
            put_strain(stage, f, k, strain_of(s_top, s_low, added_strain))
            result.append(-image)
        return result

    def first(f, carry):
        inv = 1.0 / (stiff_main + shift_of(first_order + f.astype(F32)) * mass_diag_main)
        inv_ref[f] = inv
        loads = [load_ref[pl.ds(2 * f + k, half, stride=parts), :] for k in range(2)]
        fields = [inv * b for b in loads]
        image = images(f, 0, fields)
        nexts = [inv * t for t in image]
        for k in range(2):
            field_ref[2 * f + k] = nexts[k]
        put_dot(0, f, zip(fields, loads))
        put_dot(1, f, zip(fields, image))
        put_dot(2, f, zip(nexts, image))
        return carry

    def second(f, carry):
        inv = inv_ref[f]
        fields = [field_ref[2 * f + k] for k in range(2)]
        image = images(f, 1, fields)
        nexts = [inv * t for t in image]
        for k in range(2):
            field_ref[2 * f + k] = nexts[k]
        put_dot(3, f, zip(fields, image))
        put_dot(4, f, zip(nexts, image))
        return carry

    def third(f, carry):
        fields = [field_ref[2 * f + k] for k in range(2)]
        total, extra = 0.0, 0.0
        for k, z in enumerate(products(*fields)):
            z11, z22, z12, _, s_top, s_low = z
            added, added_strain = borders(2, f, k)
            twice = 2.0 * (later(mod_sent_down * z12) + added)
            total = total + fields[k] * (mod_own * z11 + mod_sent_down * z22 + twice)
            strain = strain_of(s_top, s_low, added_strain)
            put_strain(2, f, k, strain)
            extra = extra + strain[6:7]
        dots_ref[pl.ds(5 * freqs + f, 1), :] = -(jnp.sum(total, axis=0, keepdims=True) + extra)
        return carry

    quarter = LANES // 4
    cell = lane_ids(8) // quarter
    outs = (out0_ref, out1_ref, out2_ref, out3_ref)

    def pack(stage, block):
        def comp(k, c):
            start = (((stage * 2 + k) * freqs) + block * 8) * 8 + c
            return strain_ref[pl.ds(start, 8, stride=8), :]

        comps = {(k, c): comp(k, c) for k in range(2) for c in range(6)}
        places = [
            (stage * parts + k * freqs, [(k, c) for c in range(4)]) for k in range(2)
        ] + [(3 * parts + stage * freqs, [(0, 4), (0, 5), (1, 4), (1, 5)])]
        for step in range(4):
            dest = lax.bitwise_xor(freq_group, step)
            for row, names in places:
                held = None
                for i, name in enumerate(names):
                    moved = pltpu.roll(comps[name], quarter * ((i + 4 - dest) % 4), 1)
                    held = moved if held is None else jnp.where(cell == i, moved, held)
                outs[step][row + block * 8 : row + block * 8 + 8, :] = held

    for stage, step in enumerate((first, second, third)):
        rims = rim_stage(stage, rims)
        lax.fori_loop(0, freqs, step, 0, unroll=UNROLL)
        for block in range(freqs // 8):
            pack(stage, block)

    dots_ref[DOTS * freqs :, :] = jnp.zeros((256 - DOTS * freqs, LANES), F32)
    sums = lax.dot_general(
        jnp.ones((8, LANES), F32), dots_ref[...], (((1,), (1,)), ((), ())),
        precision=lax.Precision.HIGHEST, preferred_element_type=F32,
    )
    row = lax.broadcasted_iota(jnp.int32, (8, LANES), 0)
    pair = jnp.where(row % 2 == 0, sums[:, :LANES], sums[:, LANES:])
    for i in range(dots_out_ref.shape[0] // 8):
        dots_out_ref[8 * i : 8 * i + 8, :] = pair


def coefficients(h):
    def dot(a, b, energy):
        total = None
        for i, x in enumerate(a):
            for j, y in enumerate(b):
                weight = h[i + j] - h[i + j + 1] if energy else h[i + j]
                term = x * y * weight
                total = term if total is None else total + term
        return total

    one = jnp.ones_like(h[0])
    residual, direction = [one], [one]
    rho = h[0]
    result = []
    for iteration in range(3):
        alpha = rho / dot(direction, direction, True)
        result = [
            (result[i] if i < len(result) else 0.0) + alpha * direction[i]
            for i in range(len(direction))
        ]
        if iteration == 2:
            break
        image = (
            [direction[0]]
            + [direction[i] - direction[i - 1] for i in range(1, len(direction))]
            + [-direction[-1]]
        )
        residual = [
            (residual[i] if i < len(residual) else 0.0) - alpha * image[i]
            for i in range(len(image))
        ]
        rho_next = dot(residual, residual, False)
        beta = rho_next / rho
        rho = rho_next
        direction = [
            residual[i] + (beta * direction[i] if i < len(direction) else 0.0)
            for i in range(len(residual))
        ]
    return result


def final_kernel(
    curves_ref, dots_ref, part0_ref, part1_ref, part2_ref, part3_ref,
    table_high_ref, table_low_ref, modulus_ref, soil_ref,
    modulus_out_ref, strain_out_ref, spectra_ref,
):
    freq_group = lax.axis_index("freq")
    parts, freqs = 64, 32
    total = jnp.zeros((8, LANES), F32)
    for i in range(dots_ref.shape[0] // 8):
        total = total + dots_ref[8 * i : 8 * i + 8, :]
    square = jnp.concatenate([total, jnp.zeros((LANES - 8, LANES), F32)], 0)
    turned = jnp.transpose(square)
    beside = pltpu.roll(turned, 127, 1)
    h = [turned[freqs * i : freqs * (i + 1)] for i in range(4)]
    h += [beside[freqs * i : freqs * (i + 1)] for i in range(2)]
    coefs = coefficients(h)
    lanes = lane_ids(freqs)
    for step, part_ref in enumerate((part0_ref, part1_ref, part2_ref, part3_ref)):
        source = lax.bitwise_xor(freq_group, step)
        weights = [
            jnp.sum(jnp.where(lanes == 2 * source, c, 0.0), axis=1, keepdims=True) for c in coefs
        ]

        def joined(base, per_stage):
            return sum(
                weights[j] * part_ref[base + j * per_stage : base + j * per_stage + freqs, :]
                for j in range(3)
            )

        rest = joined(3 * parts, freqs)
        for k in range(2):
            start = pl.multiple_of(source * parts + k * freqs, freqs)
            spectra_ref[pl.ds(start, freqs), :LANES] = joined(k * freqs, parts)
            side = pltpu.roll(rest, 64, 1) if k else rest
            spectra_ref[pl.ds(start, freqs), LANES:] = jnp.where(lanes < 64, side, 0.0)
    high, low = halves(spectra_ref[...])
    table_high, table_low = table_high_ref[...], table_low_ref[...]
    history = (
        jnp.dot(table_high, low, preferred_element_type=F32)
        + jnp.dot(table_low, high, preferred_element_type=F32)
        + jnp.dot(table_high, high, preferred_element_type=F32)
    )
    squares = history[:, :LANES] ** 2 + history[:, LANES:] ** 2
    squares = squares + pltpu.roll(squares, 64, 1)
    squares = squares + pltpu.roll(squares, 32, 1)
    peak = jnp.max(squares, axis=0, keepdims=True)[:, : LANES // 4] * (1.0 / (4 * freqs))
    peak_strain = STRAIN_FACTOR * jnp.sqrt(peak + EPSILON)
    position = (jnp.log(peak_strain) * (1.0 / np.log(10.0)) - LOG_LOW) / LOG_STEP
    soil = soil_ref[...]
    ratio = jnp.zeros_like(position)
    for level in range(curves_ref.shape[1]):
        value = jnp.where(soil == 0, curves_ref[0, level], 0.0)
        for kind in range(1, curves_ref.shape[0]):
            value = jnp.where(soil == kind, curves_ref[kind, level], value)
        ratio = ratio + value * jnp.maximum(0.0, 1.0 - jnp.abs(position - level))
    own = pltpu.roll(modulus_ref[...], (LANES - LANES // 4 * freq_group) % LANES, 1)
    modulus_out_ref[...] = own[:, : LANES // 4] * ratio
    strain_out_ref[...] = peak_strain


def time_table(total_freq):
    order = np.arange(1, total_freq + 1)
    phase = (np.arange(NT)[:, None] * order[None, :] % NT) * (2.0 * np.pi / NT)
    waves = np.stack([np.cos(phase), -np.sin(phase)], 1)
    table = waves.reshape(NT, 2, 4, total_freq // 4).transpose(0, 2, 1, 3).reshape(NT, -1)
    high = table.astype(np.float32).astype(jnp.bfloat16)
    low = (table - high.astype(np.float64)).astype(np.float32).astype(jnp.bfloat16)
    return high, low


def per_device(
    load, stiffness, mass_template, modulus, element_mass, strain_map, curves, soil_type
):
    half, freq_dev, _, nodes = load.shape
    parts = 2 * freq_dev
    groups = lax.axis_size("freq")
    slabs = lax.axis_size("elem")
    rows = load.reshape(half * parts, nodes)
    modulus_row, mass_row = modulus.reshape(1, nodes), element_mass.reshape(1, nodes)
    first, second, own, lhs, cols, rows = pl.pallas_call(
        edges_kernel,
        out_shape=[
            pltpu.VMEM((SENT_ROWS, LANES), F32),
            pltpu.VMEM((SENT_ROWS, LANES), F32),
            pltpu.VMEM((OWN_ROWS, LANES), F32),
            pltpu.VMEM((4 * half + 16, 2 * LANES), BF16),
            pltpu.VMEM((half, LANES), F32),
            pltpu.VMEM((half * parts, LANES), F32),
        ],
        in_specs=[HBM] * 3 + [VMEM] * 3,
        out_specs=[VMEM] * 6,
        scratch_shapes=[
            pltpu.VMEM((LANES, LANES), F32),
            pltpu.VMEM((LANES, LANES), F32),
            pltpu.VMEM((LANES, LANES), F32),
            pltpu.VMEM((2, 1, LANES), F32),
            pltpu.VMEM((half, LANES), F32),
            pltpu.SemaphoreType.DMA((5,)),
        ],
        name="edges",
    )(rows, modulus_row, mass_row, stiffness, mass_template.reshape(1, -1), strain_map)
    met_first = lax.ppermute(first, "elem", [(i, i ^ 1) for i in range(slabs)])
    met_second = lax.ppermute(
        second, "elem", [(i, i + 1 if i % 2 else i - 1) for i in range(1, slabs - 1)]
    )
    packed = 9 * freq_dev
    outs = pl.pallas_call(
        main_kernel,
        out_shape=[jax.ShapeDtypeStruct((packed, LANES), F32)] * 4
        + [jax.ShapeDtypeStruct((2 * slabs * groups, LANES), F32)],
        in_specs=[VMEM] * 6,
        out_specs=[VMEM] * 5,
        scratch_shapes=[
            pltpu.VMEM((3 * parts * 8, LANES), F32),
            pltpu.VMEM((parts, half, LANES), F32),
            pltpu.VMEM((freq_dev, half, LANES), F32),
            pltpu.VMEM((3, half + 8, LANES), F32),
            pltpu.VMEM((256, LANES), F32),
        ],
        compiler_params=pltpu.CompilerParams(vmem_limit_bytes=32 * 1024 * 1024),
        name="krylov",
    )(rows, own, met_first, met_second, lhs, cols)
    received = [outs[0]] + [
        lax.ppermute(outs[step], "freq", [(i, i ^ step) for i in range(groups)])
        for step in range(1, groups)
    ]
    dots = lax.all_to_all(
        outs[4].reshape(slabs * groups, 2, LANES), ("elem", "freq"), 0, 0
    ).reshape(-1, LANES)
    table_high, table_low = time_table(freq_dev * groups)
    quarter = nodes // groups
    new_modulus, peak_strain = pl.pallas_call(
        final_kernel,
        out_shape=[jax.ShapeDtypeStruct((1, quarter), F32)] * 2,
        in_specs=[SMEM] + [VMEM] * 9,
        out_specs=[VMEM] * 2,
        scratch_shapes=[pltpu.VMEM((groups * parts, 2 * LANES), F32)],
        compiler_params=pltpu.CompilerParams(vmem_limit_bytes=32 * 1024 * 1024),
        name="response",
    )(curves, dots, *received, jnp.asarray(table_high), jnp.asarray(table_low),
      modulus_row, soil_type.reshape(1, quarter))
    return new_modulus.reshape(quarter), peak_strain.reshape(quarter)


def solution(mesh):
    in_specs = (
        P(None, "freq", None, "elem"),
        P(),
        P(),
        P("elem"),
        P("elem"),
        P(),
        P(),
        P(("elem", "freq")),
    )
    out_specs = (P(("elem", "freq")), P(("elem", "freq")))
    return jax.shard_map(
        per_device, mesh=mesh, in_specs=in_specs, out_specs=out_specs, check_vma=False
    )
```

```python
import jax
import jax.numpy as jnp
import numpy as np
from jax import lax
from jax.experimental import pallas as pl
from jax.experimental.pallas import tpu as pltpu
from jax.sharding import PartitionSpec as P

NT = 512
MASS_COEF = 0.5
LOG_LOW = -1.5
LOG_STEP = 0.2
STRAIN_FACTOR = 0.65
EPSILON = 1e-06
LANES = 128
SLOT = 8
DEPTH = 176
UNROLL = 32
DOTS = 6
F32 = jnp.float32
BF16 = jnp.bfloat16
VMEM = pl.BlockSpec(memory_space=pltpu.VMEM)
SMEM = pl.BlockSpec(memory_space=pltpu.SMEM)
HBM = pl.BlockSpec(memory_space=pltpu.HBM)
OWN_ROWS, OWN_AT = 104, 96
SENT_ROWS, SENT_AT = 80, 72


def lane_ids(rows=1):
    return lax.broadcasted_iota(jnp.int32, (rows, LANES), 1)


def later(x):
    return pltpu.roll(x, 127, 1)


def earlier(x):
    return pltpu.roll(x, 1, 1)


def halves(x):
    high = x.astype(BF16)
    return high, (x - high.astype(F32)).astype(BF16)


def edges_kernel(
    load_ref, modulus_ref, mass_ref, stiffness_ref, template_ref, strain_map_ref,
    first_ref, second_ref, own_ref, lhs_ref, cols_ref, buffer_ref,
    slots_ref, turned_ref, square_ref, small_ref, third_ref, small_template_ref, small_stiff_ref, small_map_ref, copied,
):
    half, parts, chunks = 48, 64, 3
    per = half // chunks
    pieces = 3
    piece = half * parts // pieces
    full = 2 * half
    comps = strain_map_ref.shape[0]
    copies = [
        pltpu.make_async_copy(
            load_ref.at[pl.ds(i * piece, piece)], buffer_ref.at[pl.ds(i * piece, piece)],
            copied.at[i],
        )
        for i in range(pieces)
    ]
    smalls = [
        pltpu.make_async_copy(source, target, copied.at[pieces + i])
        for i, (source, target) in enumerate((
            (modulus_ref, small_ref.at[0]), (mass_ref, small_ref.at[1]),
            (template_ref, small_template_ref), (stiffness_ref, small_stiff_ref), (strain_map_ref, small_map_ref),
        ))
    ]
    for copy in smalls[2:] + copies + smalls[:2]:
        copy.start()
    square_ref[...] = jnp.zeros(square_ref.shape, F32)

    for copy in smalls[2:]:
        copy.wait()
    square_ref[:full, :full] = small_stiff_ref[...]
    square_ref[full : full + comps, :full] = small_map_ref[...]
    square_ref[full + 8 : full + 9, :full] = small_template_ref[...]
    stiff = square_ref[:full, :]
    same = lax.broadcasted_iota(jnp.int32, (full, LANES), 0) == lane_ids(full)
    kdiag = jnp.sum(jnp.where(same, stiff, 0.0), axis=1, keepdims=True)
    template = jnp.sum(
        jnp.where(same, square_ref[full + 8 : full + 9, :], 0.0), axis=1, keepdims=True
    )
    lane = lane_ids(half)
    columns = jnp.zeros((half, LANES), F32)
    for i, col in enumerate((kdiag[:half], kdiag[half:], template[:half], template[half:])):
        columns = jnp.where(lane == i, col, columns)
    cols_ref[...] = columns
    off = jnp.where(same, 0.0, stiff)
    strain_rows = square_ref[full : full + 8, :]
    moved = pltpu.roll(off, LANES - half, 1)
    moved_rows = pltpu.roll(strain_rows, LANES - half, 1)
    stacked = jnp.concatenate(
        [off[:half], moved[half:], moved[:half], off[half:], strain_rows, moved_rows], 0
    )
    rows = stacked.shape[0]
    lane = lane_ids(rows)
    stacked = jnp.where(lane < half, stacked, 0.0)
    high, low = halves(stacked)
    high = high.astype(F32)
    lhs_ref[:, :LANES] = (high + pltpu.roll(high, half, 1)).astype(BF16)
    lhs_ref[:, LANES:] = low

    slot = lane_ids(parts) // SLOT
    for chunk in range(chunks):
        for copy in copies[chunk * pieces // chunks : (chunk + 1) * pieces // chunks]:
            copy.wait()
        held = jnp.zeros((parts, LANES), F32)
        for i in range(per):
            start = (chunk * per + i) * parts
            moved = pltpu.roll(buffer_ref[start : start + parts, :], 2 + SLOT * i, 1)
            held = jnp.where(slot == i, moved, held)
        at = chunk * per
        for turn, shift in enumerate((LANES - 1, LANES - 3)):
            slots_ref[pl.ds(0, parts, stride=2), :] = held
            slots_ref[pl.ds(1, parts, stride=2), :] = pltpu.roll(held, shift, 1)
            turned_ref[...] = jnp.transpose(slots_ref[...])
            if turn == 0:
                own_ref[at : at + per, :] = turned_ref[pl.ds(1, per, stride=SLOT), :]
            else:
                own_ref[half + at : half + at + per, :] = turned_ref[pl.ds(0, per, stride=SLOT), :]
                third_ref[at : at + per, :] = turned_ref[pl.ds(1, per, stride=SLOT), :]
    for copy in smalls[:2]:
        copy.wait()
    own_ref[OWN_AT : OWN_AT + 1, :] = small_ref[0]
    own_ref[OWN_AT + 1 : OWN_AT + 2, :] = small_ref[1]
    own_ref[OWN_AT + 2 :, :] = jnp.zeros((OWN_ROWS - OWN_AT - 2, LANES), F32)
    even = lane_ids() % 2 == 0
    outer, inner = own_ref[:half, :], own_ref[half : 2 * half, :]
    third = third_ref[...]
    up = [jnp.where(even, outer, earlier(inner)), jnp.zeros((half // 2, LANES), F32)]
    down = [
        jnp.where(even, later(inner), outer),
        jnp.where(even, later(third[half // 2 :]), third[: half // 2]),
    ]
    even_device = lax.axis_index("elem") % 2 == 0
    for ref, ahead in ((first_ref, even_device), (second_ref, jnp.logical_not(even_device))):
        ref[:half, :] = jnp.where(ahead, up[0], down[0])
        ref[half:SENT_AT, :] = jnp.where(ahead, up[1], down[1])
        ref[SENT_AT:, :] = own_ref[OWN_AT:, :]


def shift_of(order, total):
    return MASS_COEF * (order * (1.0 / total)) ** 2


def columns_of(cols):
    return [cols[:, i : i + 1] for i in range(4)]


def diagonals(columns, mod, mass):
    kd_top, kd_low, mt_top, mt_low = columns
    return kd_top * mod[0] + kd_low * mod[1], mt_top * mass[0] + mt_low * mass[1]


def products(lhs, *fields):
    half = fields[0].shape[0]
    split = [halves(field) for field in fields]
    high = jnp.concatenate([h for h, _ in split], 1)
    low = jnp.concatenate([l for _, l in split], 1)
    gap = jnp.zeros((DEPTH - 3 * half, high.shape[1]), BF16)
    result = jnp.dot(lhs, jnp.concatenate([high, low, gap, high], 0), preferred_element_type=F32)
    cut = [half * i for i in range(5)] + [4 * half + 8, 4 * half + 16]
    return [
        [result[cut[i] : cut[i + 1], LANES * k : LANES * (k + 1)] for i in range(6)]
        for k in range(len(fields))
    ]


def image_of(mod, z):
    lanes = lane_ids()
    own, prev = mod
    up = jnp.where(lanes == 127, 0.0, own)
    down = jnp.where(lanes == 0, 0.0, prev)
    return own * z[0] + prev * z[1] + later(down * z[2]) + earlier(up * z[3])


def strain_of(z):
    return z[4] + jnp.where(lane_ids() == 127, 0.0, later(z[5]))


def inner_kernel(
    load_ref, own_ref, lhs_ref, cols_ref, image_ref, field_ref, inv_ref, strain_ref
):
    half, parts = 48, 64
    freqs = parts // 2
    first_order = (lax.axis_index("freq") * freqs + 1).astype(F32)
    lanes = lane_ids()

    def row(at):
        own = own_ref[OWN_AT + at : OWN_AT + at + 1, :]
        return own, jnp.where(lanes == 0, 0.0, earlier(own))

    mod, mass = row(0), row(1)
    stiff, weight = diagonals(columns_of(cols_ref[...]), mod, mass)
    lhs = lhs_ref[:, :DEPTH]

    def step(f, carry):
        shift = shift_of(first_order + f.astype(F32), 4 * freqs)
        inv = jnp.where(lanes == 0, 0.0, 1.0 / (stiff + shift * weight))
        inv_ref[f] = inv
        loads = [load_ref[pl.ds(2 * f + k, half, stride=parts), :] for k in range(2)]
        for k, z in enumerate(products(lhs, *(inv * b for b in loads))):
            field_ref[2 * f + k] = loads[k]
            image_ref[2 * f + k] = image_of(mod, z)
            start = pl.multiple_of((k * freqs + f) * 8, 8)
            strain_ref[pl.ds(start, 8), :] = strain_of(z)
        return carry

    lax.fori_loop(0, freqs, step, 0, unroll=UNROLL)


def main_kernel(
    image_ref, load_ref, inner_inv_ref, inner_strain_ref,
    own_ref, first_ref, second_ref, lhs_ref, cols_ref,
    out0_ref, out1_ref, out2_ref, out3_ref, dots_out_ref,
    strain_ref, field_ref, inv_ref, border_ref, dots_ref,
):
    half, parts = 48, 64
    freqs = parts // 2
    freq_group = lax.axis_index("freq")
    slab = lax.axis_index("elem")
    is_last = slab == lax.axis_size("elem") - 1
    ahead = slab % 2 == 0
    met_first, met_second = first_ref[...], second_ref[...]
    from_right = jnp.where(ahead, met_first, met_second)
    from_left = jnp.where(ahead, met_second, met_first)
    first_order = (freq_group * freqs + 1).astype(F32)
    lanes = lane_ids()
    even = lanes % 2 == 0

    columns = columns_of(cols_ref[...])
    def rows_of(at):
        own = own_ref[OWN_AT + at : OWN_AT + at + 1, :]
        left, right = (r[SENT_AT + at : SENT_AT + at + 1] for r in (from_left, from_right))
        prev = jnp.where(lanes == 0, earlier(left), earlier(own))

        def sides(*upper_lower):
            (upper, i), (lower, j) = upper_lower
            upper, lower = upper[:, i : i + 1], lower[:, j : j + 1]
            return jnp.where(even, upper, lower)

        zero = jnp.zeros_like(own)
        pairs = [
            (sides((own, 126), (own, 1)), sides((own, 125), (own, 0))),
            (sides((own, 127), (own, 0)), sides((own, 126), (left, 127))),
            (sides((right, 0), (left, 127)), sides((own, 127), (left, 126))),
            (sides((right, 1), (left, 126)), sides((right, 0), (left, 125))),
            (sides((right, 2), (zero, 0)), sides((right, 1), (zero, 0))),
        ]
        return (own, prev), pairs

    mod_main, mod_pairs = rows_of(0)
    mass_main, mass_pairs = rows_of(1)

    lhs = lhs_ref[:, :DEPTH]

    order = first_order + (lanes // 4).astype(F32)
    beyond = jnp.logical_and(even, is_last)
    inverses = []
    for i, (mod, mass) in enumerate(zip(mod_pairs, mass_pairs)):
        stiff, weight = diagonals(columns, mod, mass)
        diag = stiff + shift_of(order, 4 * freqs) * weight
        good = diag > 0
        if i >= 2:
            good = jnp.logical_and(good, jnp.logical_not(beyond))
        inverses.append(jnp.where(good, 1.0 / diag, 0.0))

    third = from_right[half:SENT_AT]
    rims = [
        own_ref[half : 2 * half, :],
        own_ref[:half, :],
        jnp.where(even, later(from_right[:half]), earlier(from_left[:half])),
        jnp.where(even, from_right[:half], from_left[:half]),
        jnp.where(even, jnp.concatenate([later(third), third], 0), 0.0),
    ]
    rims = [field * inv for field, inv in zip(rims, inverses)]

    def rim_stage(stage, rims):
        first = stage
        z = {}
        for i in range(first, len(rims), 2):
            names = list(range(i, min(i + 2, len(rims))))
            for name, value in zip(names, products(lhs, *(rims[name] for name in names))):
                z[name] = value
        at_edge = mod_pairs[1]
        outer = z[2]
        if stage == 0:
            node = z[1]
            own_part = at_edge[0] * node[0] + at_edge[1] * (node[1] + outer[3])
            border = jnp.where(even, at_edge[0] * outer[2], own_part)
            border_ref[3, :half, :] = at_edge[0] * node[3]
            border_ref[4, :half, :] = inverses[1]
            tail = outer[5]
        elif stage == 1:
            border = jnp.where(even, at_edge[0] * outer[2], at_edge[1] * outer[3])
            tail = outer[5]
        else:
            border = jnp.where(even, at_edge[0] * outer[2], 0.0)
            energy = jnp.sum(at_edge[0] * rims[2] * outer[1], axis=0, keepdims=True)
            row = lax.broadcasted_iota(jnp.int32, (8, LANES), 0)
            tail = jnp.where(row == 6, energy, outer[5])
        border_ref[stage, :half, :] = border
        border_ref[stage, half:, :] = jnp.where(even, tail, z[1][4] if stage == 0 else 0.0)
        nexts = [None] * len(rims)
        for i in range(first + 1, len(rims) - 1):
            above = jnp.where(even, z[i + 1][2], z[i - 1][2])
            below = jnp.where(even, z[i - 1][3], z[i + 1][3])
            top, low = mod_pairs[i]
            nexts[i] = -inverses[i] * (top * (z[i][0] + above) + low * (z[i][1] + below))
        return nexts[: len(rims) - 1]

    mod_own, mod_prev = mod_main
    mod_sent_down = jnp.where(lanes == 0, 0.0, mod_prev)
    rim = jnp.logical_or(lanes == 0, lanes == 127)

    def borders(stage, f, k):
        moved = pltpu.roll(border_ref[stage], LANES - 1 - 2 * (2 * f + k), 1)
        moved = jnp.where(rim, moved, 0.0)
        return moved[:half], moved[half:]

    def put_dot(which, f, pairs):
        total = sum(a * b for a, b in pairs)
        dots_ref[pl.ds(which * freqs + f, 1), :] = jnp.sum(total, axis=0, keepdims=True)

    def put_strain(stage, f, k, value):
        start = ((stage * 2 + k) * freqs + f) * 8
        strain_ref[pl.ds(pl.multiple_of(start, 8), 8), :] = value

    def moved_to(which, lane, place, f, k):
        shift = (lane + 2 * LANES - 1 - 2 * (2 * f + k)) % LANES
        return jnp.where(lanes == lane, pltpu.roll(border_ref[which, :half, :], shift, 1), place)

    def images(f, stage, fields):
        result = []
        for k, z in enumerate(products(lhs, *fields)):
            added, added_strain = borders(stage, f, k)
            put_strain(stage, f, k, strain_of(z) + added_strain)
            result.append(-(image_of(mod_main, z) + added))
        return result

    def first(f, carry):
        inv = moved_to(4, 0, inner_inv_ref[f], f, 0)
        inv_ref[f] = inv
        loads = [load_ref[2 * f + k] for k in range(2)]
        fields = [inv * b for b in loads]
        image = []
        for k in range(2):
            added, added_strain = borders(0, f, k)
            added = added + moved_to(3, 1, 0.0, f, k)
            image.append(-(image_ref[2 * f + k] + added))
            start = pl.multiple_of((k * freqs + f) * 8, 8)
            put_strain(0, f, k, inner_strain_ref[pl.ds(start, 8), :] + added_strain)
        nexts = [inv * t for t in image]
        for k in range(2):
            field_ref[2 * f + k] = nexts[k]
        put_dot(0, f, zip(fields, loads))
        put_dot(1, f, zip(fields, image))
        put_dot(2, f, zip(nexts, image))
        return carry

    def second(f, carry):
        inv = inv_ref[f]
        fields = [field_ref[2 * f + k] for k in range(2)]
        image = images(f, 1, fields)
        nexts = [inv * t for t in image]
        for k in range(2):
            field_ref[2 * f + k] = nexts[k]
        put_dot(3, f, zip(fields, image))
        put_dot(4, f, zip(nexts, image))
        return carry

    def third(f, carry):
        fields = [field_ref[2 * f + k] for k in range(2)]
        total, extra = 0.0, 0.0
        for k, z in enumerate(products(lhs, *fields)):
            z11, z22, z12 = z[:3]
            added, added_strain = borders(2, f, k)
            twice = 2.0 * (later(mod_sent_down * z12) + added)
            total = total + fields[k] * (mod_own * z11 + mod_sent_down * z22 + twice)
            strain = strain_of(z) + added_strain
            put_strain(2, f, k, strain)
            extra = extra + strain[6:7]
        dots_ref[pl.ds(5 * freqs + f, 1), :] = -(jnp.sum(total, axis=0, keepdims=True) + extra)
        return carry

    quarter = LANES // 4
    cell = lane_ids(8) // quarter
    outs = (out0_ref, out1_ref, out2_ref, out3_ref)

    def pack(stage, block):
        def comp(k, c):
            start = (((stage * 2 + k) * freqs) + block * 8) * 8 + c
            return strain_ref[pl.ds(start, 8, stride=8), :]

        comps = {(k, c): comp(k, c) for k in range(2) for c in range(6)}
        places = [
            (stage * parts + k * freqs, [(k, c) for c in range(4)]) for k in range(2)
        ] + [(3 * parts + stage * freqs, [(0, 4), (0, 5), (1, 4), (1, 5)])]
        for step in range(4):
            dest = lax.bitwise_xor(freq_group, step)
            for row, names in places:
                held = None
                for i, name in enumerate(names):
                    moved = pltpu.roll(comps[name], quarter * ((i + 4 - dest) % 4), 1)
                    held = moved if held is None else jnp.where(cell == i, moved, held)
                outs[step][row + block * 8 : row + block * 8 + 8, :] = held

    for stage, step in enumerate((first, second, third)):
        rims = rim_stage(stage, rims)
        lax.fori_loop(0, freqs, step, 0, unroll=UNROLL)
        for block in range(freqs // 8):
            pack(stage, block)

    dots_ref[DOTS * freqs :, :] = jnp.zeros((256 - DOTS * freqs, LANES), F32)
    sums = lax.dot_general(
        jnp.ones((8, LANES), F32), dots_ref[...], (((1,), (1,)), ((), ())),
        precision=lax.Precision.HIGHEST, preferred_element_type=F32,
    )
    row = lax.broadcasted_iota(jnp.int32, (8, LANES), 0)
    pair = jnp.where(row % 2 == 0, sums[:, :LANES], sums[:, LANES:])
    for i in range(dots_out_ref.shape[0] // 8):
        dots_out_ref[8 * i : 8 * i + 8, :] = pair


def coefficients(h):
    def dot(a, b, energy):
        total = None
        for i, x in enumerate(a):
            for j, y in enumerate(b):
                weight = h[i + j] - h[i + j + 1] if energy else h[i + j]
                term = x * y * weight
                total = term if total is None else total + term
        return total

    one = jnp.ones_like(h[0])
    residual, direction = [one], [one]
    rho = h[0]
    result = []
    for iteration in range(3):
        alpha = rho / dot(direction, direction, True)
        result = [
            (result[i] if i < len(result) else 0.0) + alpha * direction[i]
            for i in range(len(direction))
        ]
        if iteration == 2:
            break
        image = (
            [direction[0]]
            + [direction[i] - direction[i - 1] for i in range(1, len(direction))]
            + [-direction[-1]]
        )
        residual = [
            (residual[i] if i < len(residual) else 0.0) - alpha * image[i]
            for i in range(len(image))
        ]
        rho_next = dot(residual, residual, False)
        beta = rho_next / rho
        rho = rho_next
        direction = [
            residual[i] + (beta * direction[i] if i < len(direction) else 0.0)
            for i in range(len(residual))
        ]
    return result


def final_kernel(
    curves_ref, dots_ref, part0_ref, part1_ref, part2_ref, part3_ref,
    table_high_ref, table_low_ref, modulus_ref, soil_ref,
    modulus_out_ref, strain_out_ref, spectra_ref,
):
    freq_group = lax.axis_index("freq")
    parts, freqs = 64, 32
    total = jnp.zeros((8, LANES), F32)
    for i in range(dots_ref.shape[0] // 8):
        total = total + dots_ref[8 * i : 8 * i + 8, :]
    square = jnp.concatenate([total, jnp.zeros((LANES - 8, LANES), F32)], 0)
    turned = jnp.transpose(square)
    beside = pltpu.roll(turned, 127, 1)
    h = [turned[freqs * i : freqs * (i + 1)] for i in range(4)]
    h += [beside[freqs * i : freqs * (i + 1)] for i in range(2)]
    coefs = coefficients(h)
    lanes = lane_ids(freqs)
    for step, part_ref in enumerate((part0_ref, part1_ref, part2_ref, part3_ref)):
        source = lax.bitwise_xor(freq_group, step)
        weights = [
            jnp.sum(jnp.where(lanes == 2 * source, c, 0.0), axis=1, keepdims=True) for c in coefs
        ]

        def joined(base, per_stage):
            return sum(
                weights[j] * part_ref[base + j * per_stage : base + j * per_stage + freqs, :]
                for j in range(3)
            )

        rest = joined(3 * parts, freqs)
        for k in range(2):
            start = pl.multiple_of(source * parts + k * freqs, freqs)
            spectra_ref[pl.ds(start, freqs), :LANES] = joined(k * freqs, parts)
            side = pltpu.roll(rest, 64, 1) if k else rest
            spectra_ref[pl.ds(start, freqs), LANES:] = jnp.where(lanes < 64, side, 0.0)
    high, low = halves(spectra_ref[...])
    table_high, table_low = table_high_ref[...], table_low_ref[...]
    history = (
        jnp.dot(table_high, low, preferred_element_type=F32)
        + jnp.dot(table_low, high, preferred_element_type=F32)
        + jnp.dot(table_high, high, preferred_element_type=F32)
    )
    squares = history[:, :LANES] ** 2 + history[:, LANES:] ** 2
    squares = squares + pltpu.roll(squares, 64, 1)
    squares = squares + pltpu.roll(squares, 32, 1)
    peak = jnp.max(squares, axis=0, keepdims=True)[:, : LANES // 4] * (1.0 / (4 * freqs))
    peak_strain = STRAIN_FACTOR * jnp.sqrt(peak + EPSILON)
    position = (jnp.log(peak_strain) * (1.0 / np.log(10.0)) - LOG_LOW) / LOG_STEP
    soil = soil_ref[...]
    ratio = jnp.zeros_like(position)
    for level in range(curves_ref.shape[1]):
        value = jnp.where(soil == 0, curves_ref[0, level], 0.0)
        for kind in range(1, curves_ref.shape[0]):
            value = jnp.where(soil == kind, curves_ref[kind, level], value)
        ratio = ratio + value * jnp.maximum(0.0, 1.0 - jnp.abs(position - level))
    own = pltpu.roll(modulus_ref[...], (LANES - LANES // 4 * freq_group) % LANES, 1)
    modulus_out_ref[...] = own[:, : LANES // 4] * ratio
    strain_out_ref[...] = peak_strain


def time_table(total_freq):
    order = np.arange(1, total_freq + 1)
    phase = (np.arange(NT)[:, None] * order[None, :] % NT) * (2.0 * np.pi / NT)
    waves = np.stack([np.cos(phase), -np.sin(phase)], 1)
    table = waves.reshape(NT, 2, 4, total_freq // 4).transpose(0, 2, 1, 3).reshape(NT, -1)
    high = table.astype(np.float32).astype(jnp.bfloat16)
    low = (table - high.astype(np.float64)).astype(np.float32).astype(jnp.bfloat16)
    return high, low


def per_device(
    load, stiffness, mass_template, modulus, element_mass, strain_map, curves, soil_type
):
    half, freq_dev, _, nodes = load.shape
    parts = 2 * freq_dev
    groups = lax.axis_size("freq")
    slabs = lax.axis_size("elem")
    rows = load.reshape(half * parts, nodes)
    modulus_row, mass_row = modulus.reshape(1, nodes), element_mass.reshape(1, nodes)
    first, second, own, lhs, cols, rows = pl.pallas_call(
        edges_kernel,
        out_shape=[
            pltpu.VMEM((SENT_ROWS, LANES), F32),
            pltpu.VMEM((SENT_ROWS, LANES), F32),
            pltpu.VMEM((OWN_ROWS, LANES), F32),
            pltpu.VMEM((4 * half + 16, 2 * LANES), BF16),
            pltpu.VMEM((half, LANES), F32),
            pltpu.VMEM((half * parts, LANES), F32),
        ],
        in_specs=[HBM] * 6,
        out_specs=[VMEM] * 6,
        scratch_shapes=[
            pltpu.VMEM((LANES, LANES), F32),
            pltpu.VMEM((LANES, LANES), F32),
            pltpu.VMEM((LANES, LANES), F32),
            pltpu.VMEM((2, 1, LANES), F32),
            pltpu.VMEM((half, LANES), F32),
            pltpu.VMEM((1, 2 * half), F32),
            pltpu.VMEM((2 * half, 2 * half), F32),
            pltpu.VMEM(strain_map.shape, F32),
            pltpu.SemaphoreType.DMA((3+6,)),
        ],
        name="edges",
    )(rows, modulus_row, mass_row, stiffness, mass_template.reshape(1, -1), strain_map)
    met_first = lax.ppermute(first, "elem", [(i, i ^ 1) for i in range(slabs)])
    met_second = lax.ppermute(
        second, "elem", [(i, i + 1 if i % 2 else i - 1) for i in range(1, slabs - 1)]
    )
    inner = pl.pallas_call(
        inner_kernel,
        out_shape=[
            pltpu.VMEM((parts, half, LANES), F32),
            pltpu.VMEM((parts, half, LANES), F32),
            pltpu.VMEM((freq_dev, half, LANES), F32),
            pltpu.VMEM((parts * 8, LANES), F32),
        ],
        in_specs=[VMEM] * 4,
        out_specs=[VMEM] * 4,
        compiler_params=pltpu.CompilerParams(vmem_limit_bytes=32 * 1024 * 1024),
        name="inner",
    )(rows, own, lhs, cols)
    packed = 9 * freq_dev
    outs = pl.pallas_call(
        main_kernel,
        out_shape=[jax.ShapeDtypeStruct((packed, LANES), F32)] * 4
        + [jax.ShapeDtypeStruct((2 * slabs * groups, LANES), F32)],
        in_specs=[VMEM] * 9,
        out_specs=[VMEM] * 5,
        scratch_shapes=[
            pltpu.VMEM((3 * parts * 8, LANES), F32),
            pltpu.VMEM((parts, half, LANES), F32),
            pltpu.VMEM((freq_dev, half, LANES), F32),
            pltpu.VMEM((5, half + 8, LANES), F32),
            pltpu.VMEM((256, LANES), F32),
        ],
        compiler_params=pltpu.CompilerParams(vmem_limit_bytes=32 * 1024 * 1024),
        name="krylov",
    )(*inner, own, met_first, met_second, lhs, cols)
    received = [outs[0]] + [
        lax.ppermute(outs[step], "freq", [(i, i ^ step) for i in range(groups)])
        for step in range(1, groups)
    ]
    dots = lax.all_to_all(
        outs[4].reshape(slabs * groups, 2, LANES), ("elem", "freq"), 0, 0
    ).reshape(-1, LANES)
    table_high, table_low = time_table(freq_dev * groups)
    quarter = nodes // groups
    new_modulus, peak_strain = pl.pallas_call(
        final_kernel,
        out_shape=[jax.ShapeDtypeStruct((1, quarter), F32)] * 2,
        in_specs=[SMEM] + [VMEM] * 9,
        out_specs=[VMEM] * 2,
        scratch_shapes=[pltpu.VMEM((groups * parts, 2 * LANES), F32)],
        compiler_params=pltpu.CompilerParams(vmem_limit_bytes=32 * 1024 * 1024),
        name="response",
    )(curves, dots, *received, jnp.asarray(table_high), jnp.asarray(table_low),
      modulus_row, soil_type.reshape(1, quarter))
    return new_modulus.reshape(quarter), peak_strain.reshape(quarter)


def solution(mesh):
    in_specs = (
        P(None, "freq", None, "elem"),
        P(),
        P(),
        P("elem"),
        P("elem"),
        P(),
        P(),
        P(("elem", "freq")),
    )
    out_specs = (P(("elem", "freq")), P(("elem", "freq")))
    return jax.shard_map(
        per_device, mesh=mesh, in_specs=in_specs, out_specs=out_specs, check_vma=False
    )
```

```python
import jax
import jax.numpy as jnp
import numpy as np
from jax import lax
from jax.experimental import pallas as pl
from jax.experimental.pallas import tpu as pltpu
from jax.sharding import PartitionSpec as P

NT = 512
MASS_COEF = 0.5
LOG_LOW = -1.5
LOG_STEP = 0.2
STRAIN_FACTOR = 0.65
EPSILON = 1e-06
LANES = 128
SLOT = 8
DEPTH = 176
UNROLL = 32
STEPS = (0, 1, 3, 2)
DOTS = 6
F32 = jnp.float32
BF16 = jnp.bfloat16
VMEM = pl.BlockSpec(memory_space=pltpu.VMEM)
SMEM = pl.BlockSpec(memory_space=pltpu.SMEM)
HBM = pl.BlockSpec(memory_space=pltpu.HBM)
OWN_ROWS, OWN_AT = 104, 96
SENT_ROWS, SENT_AT = 80, 72


def lane_ids(rows=1):
    return lax.broadcasted_iota(jnp.int32, (rows, LANES), 1)


def later(x):
    return pltpu.roll(x, 127, 1)


def earlier(x):
    return pltpu.roll(x, 1, 1)


def halves(x):
    high = x.astype(BF16)
    return high, (x - high.astype(F32)).astype(BF16)


def edges_kernel(
    load_ref, modulus_ref, mass_ref, stiffness_ref, template_ref, strain_map_ref,
    first_ref, second_ref, own_ref, lhs_ref, cols_ref, buffer_ref,
    slots_ref, turned_ref, square_ref, small_ref, third_ref, small_template_ref, small_stiff_ref, small_map_ref, copied,
):
    half, parts, chunks = 48, 64, 3
    per = half // chunks
    pieces = 3
    piece = half * parts // pieces
    full = 2 * half
    comps = strain_map_ref.shape[0]
    copies = [
        pltpu.make_async_copy(
            load_ref.at[pl.ds(i * piece, piece)], buffer_ref.at[pl.ds(i * piece, piece)],
            copied.at[i],
        )
        for i in range(pieces)
    ]
    smalls = [
        pltpu.make_async_copy(source, target, copied.at[pieces + i])
        for i, (source, target) in enumerate((
            (modulus_ref, small_ref.at[0]), (mass_ref, small_ref.at[1]),
            (template_ref, small_template_ref), (stiffness_ref, small_stiff_ref), (strain_map_ref, small_map_ref),
        ))
    ]
    for copy in smalls[2:] + copies + smalls[:2]:
        copy.start()
    square_ref[...] = jnp.zeros(square_ref.shape, F32)

    for copy in smalls[2:]:
        copy.wait()
    square_ref[:full, :full] = small_stiff_ref[...]
    square_ref[full : full + comps, :full] = small_map_ref[...]
    square_ref[full + 8 : full + 9, :full] = small_template_ref[...]
    stiff = square_ref[:full, :]
    same = lax.broadcasted_iota(jnp.int32, (full, LANES), 0) == lane_ids(full)
    kdiag = jnp.sum(jnp.where(same, stiff, 0.0), axis=1, keepdims=True)
    template = jnp.sum(
        jnp.where(same, square_ref[full + 8 : full + 9, :], 0.0), axis=1, keepdims=True
    )
    lane = lane_ids(half)
    columns = jnp.zeros((half, LANES), F32)
    for i, col in enumerate((kdiag[:half], kdiag[half:], template[:half], template[half:])):
        columns = jnp.where(lane == i, col, columns)
    cols_ref[...] = columns
    off = jnp.where(same, 0.0, stiff)
    strain_rows = square_ref[full : full + 8, :]
    moved = pltpu.roll(off, LANES - half, 1)
    moved_rows = pltpu.roll(strain_rows, LANES - half, 1)
    stacked = jnp.concatenate(
        [off[:half], moved[half:], moved[:half], strain_rows, moved_rows, off[half:]], 0
    )
    rows = stacked.shape[0]
    lane = lane_ids(rows)
    stacked = jnp.where(lane < half, stacked, 0.0)
    high, low = halves(stacked)
    high = high.astype(F32)
    lhs_ref[:, :LANES] = (high + pltpu.roll(high, half, 1)).astype(BF16)
    lhs_ref[:, LANES:] = low

    slot = lane_ids(parts) // SLOT
    for chunk in range(chunks):
        for copy in copies[chunk * pieces // chunks : (chunk + 1) * pieces // chunks]:
            copy.wait()
        held = jnp.zeros((parts, LANES), F32)
        for i in range(per):
            start = (chunk * per + i) * parts
            moved = pltpu.roll(buffer_ref[start : start + parts, :], 2 + SLOT * i, 1)
            held = jnp.where(slot == i, moved, held)
        at = chunk * per
        for turn, shift in enumerate((LANES - 1, LANES - 3)):
            slots_ref[pl.ds(0, parts, stride=2), :] = held
            slots_ref[pl.ds(1, parts, stride=2), :] = pltpu.roll(held, shift, 1)
            turned_ref[...] = jnp.transpose(slots_ref[...])
            if turn == 0:
                own_ref[at : at + per, :] = turned_ref[pl.ds(1, per, stride=SLOT), :]
            else:
                own_ref[half + at : half + at + per, :] = turned_ref[pl.ds(0, per, stride=SLOT), :]
                third_ref[at : at + per, :] = turned_ref[pl.ds(1, per, stride=SLOT), :]
    for copy in smalls[:2]:
        copy.wait()
    own_ref[OWN_AT : OWN_AT + 1, :] = small_ref[0]
    own_ref[OWN_AT + 1 : OWN_AT + 2, :] = small_ref[1]
    own_ref[OWN_AT + 2 :, :] = jnp.zeros((OWN_ROWS - OWN_AT - 2, LANES), F32)
    even = lane_ids() % 2 == 0
    outer, inner = own_ref[:half, :], own_ref[half : 2 * half, :]
    third = third_ref[...]
    up = [jnp.where(even, outer, earlier(inner)), jnp.zeros((half // 2, LANES), F32)]
    down = [
        jnp.where(even, later(inner), outer),
        jnp.where(even, later(third[half // 2 :]), third[: half // 2]),
    ]
    even_device = lax.axis_index("elem") % 2 == 0
    for ref, ahead in ((first_ref, even_device), (second_ref, jnp.logical_not(even_device))):
        ref[:half, :] = jnp.where(ahead, up[0], down[0])
        ref[half:SENT_AT, :] = jnp.where(ahead, up[1], down[1])
        ref[SENT_AT:, :] = own_ref[OWN_AT:, :]


def shift_of(order, total):
    return MASS_COEF * (order * (1.0 / total)) ** 2


def columns_of(cols):
    return [cols[:, i : i + 1] for i in range(4)]


def diagonals(columns, mod, mass):
    kd_top, kd_low, mt_top, mt_low = columns
    return kd_top * mod[0] + kd_low * mod[1], mt_top * mass[0] + mt_low * mass[1]


def products(lhs, *fields):
    half = fields[0].shape[0]
    split = [halves(field) for field in fields]
    high = jnp.concatenate([h for h, _ in split], 1)
    low = jnp.concatenate([l for _, l in split], 1)
    gap = jnp.zeros((DEPTH - 3 * half, high.shape[1]), BF16)
    result = jnp.dot(lhs, jnp.concatenate([high, low, gap, high], 0), preferred_element_type=F32)
    cut = [0, half, 2 * half, 3 * half, 3 * half + 8, 3 * half + 16, lhs.shape[0]]
    return [
        [result[cut[i] : cut[i + 1], LANES * k : LANES * (k + 1)] for i in (0, 1, 2, 5, 3, 4)]
        for k in range(len(fields))
    ]


def image_of(mod, z):
    lanes = lane_ids()
    own, prev = mod
    up = jnp.where(lanes == 127, 0.0, own)
    down = jnp.where(lanes == 0, 0.0, prev)
    return own * z[0] + prev * z[1] + later(down * z[2]) + earlier(up * z[3])


def strain_of(z):
    return z[4] + jnp.where(lane_ids() == 127, 0.0, later(z[5]))


def inner_kernel(
    load_ref, own_ref, lhs_ref, cols_ref, image_ref, field_ref, inv_ref, strain_ref
):
    half, parts = 48, 64
    freqs = parts // 2
    first_order = (lax.axis_index("freq") * freqs + 1).astype(F32)
    lanes = lane_ids()

    def row(at):
        own = own_ref[OWN_AT + at : OWN_AT + at + 1, :]
        return own, jnp.where(lanes == 0, 0.0, earlier(own))

    mod, mass = row(0), row(1)
    stiff, weight = diagonals(columns_of(cols_ref[...]), mod, mass)
    lhs = lhs_ref[:, :DEPTH]

    def step(f, carry):
        shift = shift_of(first_order + f.astype(F32), 4 * freqs)
        inv = jnp.where(lanes == 0, 0.0, 1.0 / (stiff + shift * weight))
        inv_ref[f] = inv
        loads = [load_ref[pl.ds(2 * f + k, half, stride=parts), :] for k in range(2)]
        for k, z in enumerate(products(lhs, *(inv * b for b in loads))):
            field_ref[2 * f + k] = loads[k]
            image_ref[2 * f + k] = image_of(mod, z)
            start = pl.multiple_of((k * freqs + f) * 8, 8)
            strain_ref[pl.ds(start, 8), :] = strain_of(z)
        return carry

    lax.fori_loop(0, freqs, step, 0, unroll=UNROLL)


def main_kernel(
    image_ref, load_ref, inner_inv_ref, inner_strain_ref,
    own_ref, second_ref, first_ref, lhs_ref, cols_ref,
    out0_ref, out1_ref, out2_ref, out3_ref, dots_out_ref,
    strain_ref, field_ref, inv_ref, border_ref, dots_ref,
):
    half, parts = 48, 64
    freqs = parts // 2
    freq_group = lax.axis_index("freq")
    slab = lax.axis_index("elem")
    is_last = slab == lax.axis_size("elem") - 1
    ahead = slab % 2 == 0
    met_first, met_second = first_ref[...], second_ref[...]
    from_right = jnp.where(ahead, met_first, met_second)
    from_left = jnp.where(ahead, met_second, met_first)
    first_order = (freq_group * freqs + 1).astype(F32)
    lanes = lane_ids()
    even = lanes % 2 == 0

    columns = columns_of(cols_ref[...])
    def rows_of(at):
        own = own_ref[OWN_AT + at : OWN_AT + at + 1, :]
        left, right = (r[SENT_AT + at : SENT_AT + at + 1] for r in (from_left, from_right))
        prev = jnp.where(lanes == 0, earlier(left), earlier(own))

        def sides(*upper_lower):
            (upper, i), (lower, j) = upper_lower
            upper, lower = upper[:, i : i + 1], lower[:, j : j + 1]
            return jnp.where(even, upper, lower)

        zero = jnp.zeros_like(own)
        pairs = [
            (sides((own, 126), (own, 1)), sides((own, 125), (own, 0))),
            (sides((own, 127), (own, 0)), sides((own, 126), (left, 127))),
            (sides((right, 0), (left, 127)), sides((own, 127), (left, 126))),
            (sides((right, 1), (left, 126)), sides((right, 0), (left, 125))),
            (sides((right, 2), (zero, 0)), sides((right, 1), (zero, 0))),
        ]
        return (own, prev), pairs

    mod_main, mod_pairs = rows_of(0)
    mass_main, mass_pairs = rows_of(1)

    lhs = lhs_ref[:, :DEPTH]

    order = first_order + (lanes // 4).astype(F32)
    beyond = jnp.logical_and(even, is_last)
    inverses = []
    for i, (mod, mass) in enumerate(zip(mod_pairs, mass_pairs)):
        stiff, weight = diagonals(columns, mod, mass)
        diag = stiff + shift_of(order, 4 * freqs) * weight
        good = diag > 0
        if i >= 2:
            good = jnp.logical_and(good, jnp.logical_not(beyond))
        inverses.append(jnp.where(good, 1.0 / diag, 0.0))

    third = from_right[half:SENT_AT]
    rims = [
        own_ref[half : 2 * half, :],
        own_ref[:half, :],
        jnp.where(even, later(from_right[:half]), earlier(from_left[:half])),
        jnp.where(even, from_right[:half], from_left[:half]),
        jnp.where(even, jnp.concatenate([later(third), third], 0), 0.0),
    ]
    rims = [field * inv for field, inv in zip(rims, inverses)]

    def rim_stage(stage, rims):
        first = stage
        z = {}
        for i in range(first, len(rims), 2):
            names = list(range(i, min(i + 2, len(rims))))
            for name, value in zip(names, products(lhs, *(rims[name] for name in names))):
                z[name] = value
        at_edge = mod_pairs[1]
        outer = z[2]
        if stage == 0:
            node = z[1]
            own_part = at_edge[0] * node[0] + at_edge[1] * (node[1] + outer[3])
            border = jnp.where(even, at_edge[0] * outer[2], own_part)
            border_ref[3, :half, :] = at_edge[0] * node[3]
            border_ref[4, :half, :] = inverses[1]
            tail = outer[5]
        elif stage == 1:
            border = jnp.where(even, at_edge[0] * outer[2], at_edge[1] * outer[3])
            tail = outer[5]
        else:
            border = jnp.where(even, at_edge[0] * outer[2], 0.0)
            energy = jnp.sum(at_edge[0] * rims[2] * outer[1], axis=0, keepdims=True)
            row = lax.broadcasted_iota(jnp.int32, (8, LANES), 0)
            tail = jnp.where(row == 6, energy, outer[5])
        border_ref[stage, :half, :] = border
        border_ref[stage, half:, :] = jnp.where(even, tail, z[1][4] if stage == 0 else 0.0)
        nexts = [None] * len(rims)
        for i in range(first + 1, len(rims) - 1):
            above = jnp.where(even, z[i + 1][2], z[i - 1][2])
            below = jnp.where(even, z[i - 1][3], z[i + 1][3])
            top, low = mod_pairs[i]
            nexts[i] = -inverses[i] * (top * (z[i][0] + above) + low * (z[i][1] + below))
        return nexts[: len(rims) - 1]

    mod_own, mod_prev = mod_main
    mod_sent_down = jnp.where(lanes == 0, 0.0, mod_prev)
    rim = jnp.logical_or(lanes == 0, lanes == 127)

    def borders(stage, f, k):
        moved = pltpu.roll(border_ref[stage], LANES - 1 - 2 * (2 * f + k), 1)
        moved = jnp.where(rim, moved, 0.0)
        return moved[:half], moved[half:]

    def put_dot(which, f, pairs):
        total = sum(a * b for a, b in pairs)
        dots_ref[pl.ds(which * freqs + f, 1), :] = jnp.sum(total, axis=0, keepdims=True)

    def put_strain(stage, f, k, value):
        start = ((stage * 2 + k) * freqs + f) * 8
        strain_ref[pl.ds(pl.multiple_of(start, 8), 8), :] = value

    def moved_to(which, lane, place, f, k):
        shift = (lane + 2 * LANES - 1 - 2 * (2 * f + k)) % LANES
        return jnp.where(lanes == lane, pltpu.roll(border_ref[which, :half, :], shift, 1), place)

    def images(f, stage, fields):
        result = []
        for k, z in enumerate(products(lhs, *fields)):
            added, added_strain = borders(stage, f, k)
            put_strain(stage, f, k, strain_of(z) + added_strain)
            result.append(-(image_of(mod_main, z) + added))
        return result

    def first(f, carry):
        inv = moved_to(4, 0, inner_inv_ref[f], f, 0)
        inv_ref[f] = inv
        loads = [load_ref[2 * f + k] for k in range(2)]
        fields = [inv * b for b in loads]
        image = []
        for k in range(2):
            added, added_strain = borders(0, f, k)
            added = added + moved_to(3, 1, 0.0, f, k)
            image.append(-(image_ref[2 * f + k] + added))
            start = pl.multiple_of((k * freqs + f) * 8, 8)
            put_strain(0, f, k, inner_strain_ref[pl.ds(start, 8), :] + added_strain)
        nexts = [inv * t for t in image]
        for k in range(2):
            field_ref[2 * f + k] = nexts[k]
        put_dot(0, f, zip(fields, loads))
        put_dot(1, f, zip(fields, image))
        put_dot(2, f, zip(nexts, image))
        return carry

    def second(f, carry):
        inv = inv_ref[f]
        fields = [field_ref[2 * f + k] for k in range(2)]
        image = images(f, 1, fields)
        nexts = [inv * t for t in image]
        for k in range(2):
            field_ref[2 * f + k] = nexts[k]
        put_dot(3, f, zip(fields, image))
        put_dot(4, f, zip(nexts, image))
        return carry

    def third(f, carry):
        fields = [field_ref[2 * f + k] for k in range(2)]
        total, extra = 0.0, 0.0
        for k, z in enumerate(products(lhs[: 3 * half + 16], *fields)):
            z11, z22, z12 = z[:3]
            added, added_strain = borders(2, f, k)
            twice = 2.0 * (later(mod_sent_down * z12) + added)
            total = total + fields[k] * (mod_own * z11 + mod_sent_down * z22 + twice)
            strain = strain_of(z) + added_strain
            put_strain(2, f, k, strain)
            extra = extra + strain[6:7]
        dots_ref[pl.ds(5 * freqs + f, 1), :] = -(jnp.sum(total, axis=0, keepdims=True) + extra)
        return carry

    quarter = LANES // 4
    cell = lane_ids(8) // quarter
    outs = (out0_ref, out1_ref, out2_ref, out3_ref)

    def pack(stage, block):
        def comp(k, c):
            start = (((stage * 2 + k) * freqs) + block * 8) * 8 + c
            return strain_ref[pl.ds(start, 8, stride=8), :]

        comps = {(k, c): comp(k, c) for k in range(2) for c in range(6)}
        places = [
            (stage * parts + k * freqs, [(k, c) for c in range(4)]) for k in range(2)
        ] + [(3 * parts + stage * freqs, [(0, 4), (0, 5), (1, 4), (1, 5)])]
        for step in range(4):
            dest = lax.bitwise_xor(freq_group, STEPS[step])
            for row, names in places:
                held = None
                for i, name in enumerate(names):
                    moved = pltpu.roll(comps[name], quarter * ((i + 4 - dest) % 4), 1)
                    held = moved if held is None else jnp.where(cell == i, moved, held)
                outs[step][row + block * 8 : row + block * 8 + 8, :] = held

    for stage, step in enumerate((first, second, third)):
        rims = rim_stage(stage, rims)
        lax.fori_loop(0, freqs, step, 0, unroll=UNROLL)
        for block in range(freqs // 8):
            pack(stage, block)

    dots_ref[DOTS * freqs :, :] = jnp.zeros((256 - DOTS * freqs, LANES), F32)
    sums = lax.dot_general(
        jnp.ones((8, LANES), F32), dots_ref[...], (((1,), (1,)), ((), ())),
        precision=lax.Precision.HIGHEST, preferred_element_type=F32,
    )
    row = lax.broadcasted_iota(jnp.int32, (8, LANES), 0)
    pair = jnp.where(row % 2 == 0, sums[:, :LANES], sums[:, LANES:])
    for i in range(dots_out_ref.shape[0] // 8):
        dots_out_ref[8 * i : 8 * i + 8, :] = pair


def coefficients(h):
    def dot(a, b, energy):
        total = None
        for i, x in enumerate(a):
            for j, y in enumerate(b):
                weight = h[i + j] - h[i + j + 1] if energy else h[i + j]
                term = x * y * weight
                total = term if total is None else total + term
        return total

    one = jnp.ones_like(h[0])
    residual, direction = [one], [one]
    rho = h[0]
    result = []
    for iteration in range(3):
        alpha = rho / dot(direction, direction, True)
        result = [
            (result[i] if i < len(result) else 0.0) + alpha * direction[i]
            for i in range(len(direction))
        ]
        if iteration == 2:
            break
        image = (
            [direction[0]]
            + [direction[i] - direction[i - 1] for i in range(1, len(direction))]
            + [-direction[-1]]
        )
        residual = [
            (residual[i] if i < len(residual) else 0.0) - alpha * image[i]
            for i in range(len(image))
        ]
        rho_next = dot(residual, residual, False)
        beta = rho_next / rho
        rho = rho_next
        direction = [
            residual[i] + (beta * direction[i] if i < len(direction) else 0.0)
            for i in range(len(residual))
        ]
    return result


def final_kernel(
    curves_ref, dots_ref, part0_ref, part1_ref, part2_ref, part3_ref,
    table_high_ref, table_low_ref, modulus_ref, soil_ref,
    modulus_out_ref, strain_out_ref, spectra_ref,
):
    freq_group = lax.axis_index("freq")
    parts, freqs = 64, 32
    total = jnp.zeros((8, LANES), F32)
    for i in range(dots_ref.shape[0] // 8):
        total = total + dots_ref[8 * i : 8 * i + 8, :]
    square = jnp.concatenate([total, jnp.zeros((LANES - 8, LANES), F32)], 0)
    turned = jnp.transpose(square)
    beside = pltpu.roll(turned, 127, 1)
    h = [turned[freqs * i : freqs * (i + 1)] for i in range(4)]
    h += [beside[freqs * i : freqs * (i + 1)] for i in range(2)]
    coefs = coefficients(h)
    lanes = lane_ids(freqs)
    for step, part_ref in enumerate((part0_ref, part1_ref, part2_ref, part3_ref)):
        source = lax.bitwise_xor(freq_group, STEPS[step])
        weights = [
            jnp.sum(jnp.where(lanes == 2 * source, c, 0.0), axis=1, keepdims=True) for c in coefs
        ]

        def joined(base, per_stage):
            return sum(
                weights[j] * part_ref[base + j * per_stage : base + j * per_stage + freqs, :]
                for j in range(3)
            )

        rest = joined(3 * parts, freqs)
        for k in range(2):
            start = pl.multiple_of(source * parts + k * freqs, freqs)
            spectra_ref[pl.ds(start, freqs), :LANES] = joined(k * freqs, parts)
            side = pltpu.roll(rest, 64, 1) if k else rest
            spectra_ref[pl.ds(start, freqs), LANES:] = jnp.where(lanes < 64, side, 0.0)
    high, low = halves(spectra_ref[...])
    table_high, table_low = table_high_ref[...], table_low_ref[...]
    history = (
        jnp.dot(table_high, low, preferred_element_type=F32)
        + jnp.dot(table_low, high, preferred_element_type=F32)
        + jnp.dot(table_high, high, preferred_element_type=F32)
    )
    squares = history[:, :LANES] ** 2 + history[:, LANES:] ** 2
    squares = squares + pltpu.roll(squares, 64, 1)
    squares = squares + pltpu.roll(squares, 32, 1)
    peak = jnp.max(squares, axis=0, keepdims=True)[:, : LANES // 4] * (1.0 / (4 * freqs))
    peak_strain = STRAIN_FACTOR * jnp.sqrt(peak + EPSILON)
    position = (jnp.log(peak_strain) * (1.0 / np.log(10.0)) - LOG_LOW) / LOG_STEP
    soil = soil_ref[...]
    ratio = jnp.zeros_like(position)
    for level in range(curves_ref.shape[1]):
        value = jnp.where(soil == 0, curves_ref[0, level], 0.0)
        for kind in range(1, curves_ref.shape[0]):
            value = jnp.where(soil == kind, curves_ref[kind, level], value)
        ratio = ratio + value * jnp.maximum(0.0, 1.0 - jnp.abs(position - level))
    own = pltpu.roll(modulus_ref[...], (LANES - LANES // 4 * freq_group) % LANES, 1)
    modulus_out_ref[...] = own[:, : LANES // 4] * ratio
    strain_out_ref[...] = peak_strain


def time_table(total_freq):
    order = np.arange(1, total_freq + 1)
    phase = (np.arange(NT)[:, None] * order[None, :] % NT) * (2.0 * np.pi / NT)
    waves = np.stack([np.cos(phase), -np.sin(phase)], 1)
    table = waves.reshape(NT, 2, 4, total_freq // 4).transpose(0, 2, 1, 3).reshape(NT, -1)
    high = table.astype(np.float32).astype(jnp.bfloat16)
    low = (table - high.astype(np.float64)).astype(np.float32).astype(jnp.bfloat16)
    return high, low


def per_device(
    load, stiffness, mass_template, modulus, element_mass, strain_map, curves, soil_type
):
    half, freq_dev, _, nodes = load.shape
    parts = 2 * freq_dev
    groups = lax.axis_size("freq")
    slabs = lax.axis_size("elem")
    rows = load.reshape(half * parts, nodes)
    modulus_row, mass_row = modulus.reshape(1, nodes), element_mass.reshape(1, nodes)
    first, second, own, lhs, cols, rows = pl.pallas_call(
        edges_kernel,
        out_shape=[
            pltpu.VMEM((SENT_ROWS, LANES), F32),
            pltpu.VMEM((SENT_ROWS, LANES), F32),
            pltpu.VMEM((OWN_ROWS, LANES), F32),
            pltpu.VMEM((4 * half + 16, 2 * LANES), BF16),
            pltpu.VMEM((half, LANES), F32),
            pltpu.VMEM((half * parts, LANES), F32),
        ],
        in_specs=[HBM] * 6,
        out_specs=[VMEM] * 6,
        scratch_shapes=[
            pltpu.VMEM((LANES, LANES), F32),
            pltpu.VMEM((LANES, LANES), F32),
            pltpu.VMEM((LANES, LANES), F32),
            pltpu.VMEM((2, 1, LANES), F32),
            pltpu.VMEM((half, LANES), F32),
            pltpu.VMEM((1, 2 * half), F32),
            pltpu.VMEM((2 * half, 2 * half), F32),
            pltpu.VMEM(strain_map.shape, F32),
            pltpu.SemaphoreType.DMA((3+6,)),
        ],
        name="edges",
    )(rows, modulus_row, mass_row, stiffness, mass_template.reshape(1, -1), strain_map)
    met_first = lax.ppermute(first, "elem", [(i, i ^ 1) for i in range(slabs)])
    met_second = lax.ppermute(
        second, "elem", [(i, i + 1 if i % 2 else i - 1) for i in range(1, slabs - 1)]
    )
    inner = pl.pallas_call(
        inner_kernel,
        out_shape=[
            pltpu.VMEM((parts, half, LANES), F32),
            pltpu.VMEM((parts, half, LANES), F32),
            pltpu.VMEM((freq_dev, half, LANES), F32),
            pltpu.VMEM((parts * 8, LANES), F32),
        ],
        in_specs=[VMEM] * 4,
        out_specs=[VMEM] * 4,
        compiler_params=pltpu.CompilerParams(vmem_limit_bytes=32 * 1024 * 1024),
        name="inner",
    )(rows, own, lhs, cols)
    packed = 9 * freq_dev
    outs = pl.pallas_call(
        main_kernel,
        out_shape=[jax.ShapeDtypeStruct((packed, LANES), F32)] * 4
        + [jax.ShapeDtypeStruct((2 * slabs * groups, LANES), F32)],
        in_specs=[VMEM] * 9,
        out_specs=[VMEM] * 5,
        scratch_shapes=[
            pltpu.VMEM((3 * parts * 8, LANES), F32),
            pltpu.VMEM((parts, half, LANES), F32),
            pltpu.VMEM((freq_dev, half, LANES), F32),
            pltpu.VMEM((5, half + 8, LANES), F32),
            pltpu.VMEM((256, LANES), F32),
        ],
        compiler_params=pltpu.CompilerParams(vmem_limit_bytes=32 * 1024 * 1024),
        name="krylov",
    )(*inner, own, met_second, met_first, lhs, cols)
    received = [outs[0]] + [
        lax.ppermute(outs[step], "freq", [(i, i ^ STEPS[step]) for i in range(groups)])
        for step in range(1, groups)
    ]
    dots = lax.all_to_all(
        outs[4].reshape(slabs * groups, 2, LANES), ("elem", "freq"), 0, 0
    ).reshape(-1, LANES)
    table_high, table_low = time_table(freq_dev * groups)
    quarter = nodes // groups
    new_modulus, peak_strain = pl.pallas_call(
        final_kernel,
        out_shape=[jax.ShapeDtypeStruct((1, quarter), F32)] * 2,
        in_specs=[SMEM] + [VMEM] * 9,
        out_specs=[VMEM] * 2,
        scratch_shapes=[pltpu.VMEM((groups * parts, 2 * LANES), F32)],
        compiler_params=pltpu.CompilerParams(vmem_limit_bytes=32 * 1024 * 1024),
        name="response",
    )(curves, dots, *received, jnp.asarray(table_high), jnp.asarray(table_low),
      modulus_row, soil_type.reshape(1, quarter))
    return new_modulus.reshape(quarter), peak_strain.reshape(quarter)


def solution(mesh):
    in_specs = (
        P(None, "freq", None, "elem"),
        P(),
        P(),
        P("elem"),
        P("elem"),
        P(),
        P(),
        P(("elem", "freq")),
    )
    out_specs = (P(("elem", "freq")), P(("elem", "freq")))
    return jax.shard_map(
        per_device, mesh=mesh, in_specs=in_specs, out_specs=out_specs, check_vma=False
    )
```

```python
import jax
import jax.numpy as jnp
import numpy as np
from jax import lax
from jax.experimental import pallas as pl
from jax.experimental.pallas import tpu as pltpu
from jax.sharding import PartitionSpec as P

NT = 512
MASS_COEF = 0.5
LOG_LOW = -1.5
LOG_STEP = 0.2
STRAIN_FACTOR = 0.65
EPSILON = 1e-06
LANES = 128
SLOT = 8
DEPTH = 176
UNROLL = 32
STEPS = (0, 1, 3, 2)
DOTS = 6
F32 = jnp.float32
BF16 = jnp.bfloat16
VMEM = pl.BlockSpec(memory_space=pltpu.VMEM)
SMEM = pl.BlockSpec(memory_space=pltpu.SMEM)
HBM = pl.BlockSpec(memory_space=pltpu.HBM)
OWN_ROWS, OWN_AT = 104, 96
SENT_ROWS, SENT_AT = 80, 72


def lane_ids(rows=1):
    return lax.broadcasted_iota(jnp.int32, (rows, LANES), 1)


def later(x):
    return pltpu.roll(x, 127, 1)


def earlier(x):
    return pltpu.roll(x, 1, 1)


def halves(x):
    high = x.astype(BF16)
    return high, (x - high.astype(F32)).astype(BF16)


def edges_kernel(
    load_ref, modulus_ref, mass_ref, stiffness_ref, template_ref, strain_map_ref,
    first_ref, second_ref, own_ref, lhs_ref, cols_ref, buffer_ref,
    slots_ref, turned_ref, square_ref, small_ref, third_ref, small_template_ref, small_stiff_ref, small_map_ref, copied,
):
    half, parts, chunks = 48, 64, 3
    per = half // chunks
    pieces = 3
    piece = half * parts // pieces
    full = 2 * half
    comps = strain_map_ref.shape[0]
    copies = [
        pltpu.make_async_copy(
            load_ref.at[pl.ds(i * piece, piece)], buffer_ref.at[pl.ds(i * piece, piece)],
            copied.at[i],
        )
        for i in range(pieces)
    ]
    smalls = [
        pltpu.make_async_copy(source, target, copied.at[pieces + i])
        for i, (source, target) in enumerate((
            (modulus_ref, small_ref.at[0]), (mass_ref, small_ref.at[1]),
            (template_ref, small_template_ref), (stiffness_ref, small_stiff_ref), (strain_map_ref, small_map_ref),
        ))
    ]
    for copy in smalls[2:] + copies + smalls[:2]:
        copy.start()
    square_ref[...] = jnp.zeros(square_ref.shape, F32)

    for copy in smalls[2:]:
        copy.wait()
    square_ref[:full, :full] = small_stiff_ref[...]
    square_ref[full : full + comps, :full] = small_map_ref[...]
    square_ref[full + 8 : full + 9, :full] = small_template_ref[...]
    stiff = square_ref[:full, :]
    same = lax.broadcasted_iota(jnp.int32, (full, LANES), 0) == lane_ids(full)
    kdiag = jnp.sum(jnp.where(same, stiff, 0.0), axis=1, keepdims=True)
    template = jnp.sum(
        jnp.where(same, square_ref[full + 8 : full + 9, :], 0.0), axis=1, keepdims=True
    )
    lane = lane_ids(half)
    columns = jnp.zeros((half, LANES), F32)
    for i, col in enumerate((kdiag[:half], kdiag[half:], template[:half], template[half:])):
        columns = jnp.where(lane == i, col, columns)
    cols_ref[...] = columns
    off = jnp.where(same, 0.0, stiff)
    strain_rows = square_ref[full : full + 8, :]
    moved = pltpu.roll(off, LANES - half, 1)
    moved_rows = pltpu.roll(strain_rows, LANES - half, 1)
    stacked = jnp.concatenate(
        [off[:half], moved[half:], moved[:half], strain_rows, moved_rows, off[half:]], 0
    )
    rows = stacked.shape[0]
    lane = lane_ids(rows)
    stacked = jnp.where(lane < half, stacked, 0.0)
    high, low = halves(stacked)
    high = high.astype(F32)
    lhs_ref[:, :LANES] = (high + pltpu.roll(high, half, 1)).astype(BF16)
    lhs_ref[:, LANES:] = low

    slot = lane_ids(parts) // SLOT
    for chunk in range(chunks):
        for copy in copies[chunk * pieces // chunks : (chunk + 1) * pieces // chunks]:
            copy.wait()
        held = jnp.zeros((parts, LANES), F32)
        for i in range(per):
            start = (chunk * per + i) * parts
            moved = pltpu.roll(buffer_ref[start : start + parts, :], 2 + SLOT * i, 1)
            held = jnp.where(slot == i, moved, held)
        at = chunk * per
        for turn, shift in enumerate((LANES - 1, LANES - 3)):
            slots_ref[pl.ds(0, parts, stride=2), :] = held
            slots_ref[pl.ds(1, parts, stride=2), :] = pltpu.roll(held, shift, 1)
            turned_ref[...] = jnp.transpose(slots_ref[...])
            if turn == 0:
                own_ref[at : at + per, :] = turned_ref[pl.ds(1, per, stride=SLOT), :]
            else:
                own_ref[half + at : half + at + per, :] = turned_ref[pl.ds(0, per, stride=SLOT), :]
                third_ref[at : at + per, :] = turned_ref[pl.ds(1, per, stride=SLOT), :]
    for copy in smalls[:2]:
        copy.wait()
    own_ref[OWN_AT : OWN_AT + 1, :] = small_ref[0]
    own_ref[OWN_AT + 1 : OWN_AT + 2, :] = small_ref[1]
    own_ref[OWN_AT + 2 :, :] = jnp.zeros((OWN_ROWS - OWN_AT - 2, LANES), F32)
    even = lane_ids() % 2 == 0
    outer, inner = own_ref[:half, :], own_ref[half : 2 * half, :]
    third = third_ref[...]
    up = [jnp.where(even, outer, earlier(inner)), jnp.zeros((half // 2, LANES), F32)]
    down = [
        jnp.where(even, later(inner), outer),
        jnp.where(even, later(third[half // 2 :]), third[: half // 2]),
    ]
    even_device = lax.axis_index("elem") % 2 == 0
    for ref, ahead in ((first_ref, even_device), (second_ref, jnp.logical_not(even_device))):
        ref[:half, :] = jnp.where(ahead, up[0], down[0])
        ref[half:SENT_AT, :] = jnp.where(ahead, up[1], down[1])
        ref[SENT_AT:, :] = own_ref[OWN_AT:, :]


def shift_of(order, total):
    return MASS_COEF * (order * (1.0 / total)) ** 2


def columns_of(cols):
    return [cols[:, i : i + 1] for i in range(4)]


def diagonals(columns, mod, mass):
    kd_top, kd_low, mt_top, mt_low = columns
    return kd_top * mod[0] + kd_low * mod[1], mt_top * mass[0] + mt_low * mass[1]


def products(lhs, *fields):
    half = fields[0].shape[0]
    split = [halves(field) for field in fields]
    high = jnp.concatenate([h for h, _ in split], 1)
    low = jnp.concatenate([l for _, l in split], 1)
    gap = jnp.zeros((DEPTH - 3 * half, high.shape[1]), BF16)
    result = jnp.dot(lhs, jnp.concatenate([high, low, gap, high], 0), preferred_element_type=F32)
    cut = [0, half, 2 * half, 3 * half, 3 * half + 8, 3 * half + 16, lhs.shape[0]]
    return [
        [result[cut[i] : cut[i + 1], LANES * k : LANES * (k + 1)] for i in (0, 1, 2, 5, 3, 4)]
        for k in range(len(fields))
    ]


def image_of(mod, z):
    lanes = lane_ids()
    own, prev = mod
    up = jnp.where(lanes == 127, 0.0, own)
    down = jnp.where(lanes == 0, 0.0, prev)
    return own * z[0] + prev * z[1] + later(down * z[2]) + earlier(up * z[3])


def strain_of(z):
    return z[4] + jnp.where(lane_ids() == 127, 0.0, later(z[5]))


def inner_kernel(
    load_ref, own_ref, lhs_ref, cols_ref, image_ref, field_ref, inv_ref, strain_ref
):
    half, parts = 48, 64
    freqs = parts // 2
    first_order = (lax.axis_index("freq") * freqs + 1).astype(F32)
    lanes = lane_ids()

    def row(at):
        own = own_ref[OWN_AT + at : OWN_AT + at + 1, :]
        return own, jnp.where(lanes == 0, 0.0, earlier(own))

    mod, mass = row(0), row(1)
    stiff, weight = diagonals(columns_of(cols_ref[...]), mod, mass)
    lhs = lhs_ref[:, :DEPTH]

    def step(f, carry):
        shift = shift_of(first_order + f.astype(F32), 4 * freqs)
        inv = jnp.where(lanes == 0, 0.0, 1.0 / (stiff + shift * weight))
        inv_ref[f] = inv
        loads = [load_ref[pl.ds(2 * f + k, half, stride=parts), :] for k in range(2)]
        for k, z in enumerate(products(lhs, *(inv * b for b in loads))):
            field_ref[2 * f + k] = loads[k]
            image_ref[2 * f + k] = image_of(mod, z)
            start = pl.multiple_of((k * freqs + f) * 8, 8)
            strain_ref[pl.ds(start, 8), :] = strain_of(z)
        return carry

    lax.fori_loop(0, freqs, step, 0, unroll=UNROLL)


def main_kernel(
    image_ref, load_ref, inner_inv_ref, inner_strain_ref,
    own_ref, second_ref, first_ref, lhs_ref, cols_ref,
    out0_ref, out1_ref, out2_ref, out3_ref, dots_out_ref,
    strain_ref, field_ref, inv_ref, border_ref, dots_ref,
):
    half, parts = 48, 64
    freqs = parts // 2
    freq_group = lax.axis_index("freq")
    slab = lax.axis_index("elem")
    is_last = slab == lax.axis_size("elem") - 1
    ahead = slab % 2 == 0
    met_first, met_second = first_ref[...], second_ref[...]
    from_right = jnp.where(ahead, met_first, met_second)
    from_left = jnp.where(ahead, met_second, met_first)
    first_order = (freq_group * freqs + 1).astype(F32)
    lanes = lane_ids()
    even = lanes % 2 == 0

    columns = columns_of(cols_ref[...])
    def rows_of(at):
        own = own_ref[OWN_AT + at : OWN_AT + at + 1, :]
        left, right = (r[SENT_AT + at : SENT_AT + at + 1] for r in (from_left, from_right))
        prev = jnp.where(lanes == 0, earlier(left), earlier(own))

        def sides(*upper_lower):
            (upper, i), (lower, j) = upper_lower
            upper, lower = upper[:, i : i + 1], lower[:, j : j + 1]
            return jnp.where(even, upper, lower)

        zero = jnp.zeros_like(own)
        pairs = [
            (sides((own, 126), (own, 1)), sides((own, 125), (own, 0))),
            (sides((own, 127), (own, 0)), sides((own, 126), (left, 127))),
            (sides((right, 0), (left, 127)), sides((own, 127), (left, 126))),
            (sides((right, 1), (left, 126)), sides((right, 0), (left, 125))),
            (sides((right, 2), (zero, 0)), sides((right, 1), (zero, 0))),
        ]
        return (own, prev), pairs

    mod_main, mod_pairs = rows_of(0)
    mass_main, mass_pairs = rows_of(1)

    lhs = lhs_ref[:, :DEPTH]

    order = first_order + (lanes // 4).astype(F32)
    beyond = jnp.logical_and(even, is_last)
    inverses = []
    for i, (mod, mass) in enumerate(zip(mod_pairs, mass_pairs)):
        stiff, weight = diagonals(columns, mod, mass)
        diag = stiff + shift_of(order, 4 * freqs) * weight
        good = diag > 0
        if i >= 2:
            good = jnp.logical_and(good, jnp.logical_not(beyond))
        inverses.append(jnp.where(good, 1.0 / diag, 0.0))

    third = from_right[half:SENT_AT]
    rims = [
        own_ref[half : 2 * half, :],
        own_ref[:half, :],
        jnp.where(even, later(from_right[:half]), earlier(from_left[:half])),
        jnp.where(even, from_right[:half], from_left[:half]),
        jnp.where(even, jnp.concatenate([later(third), third], 0), 0.0),
    ]
    rims = [field * inv for field, inv in zip(rims, inverses)]

    def rim_stage(stage, rims):
        first = stage
        z = {}
        for i in range(first, len(rims), 2):
            names = list(range(i, min(i + 2, len(rims))))
            for name, value in zip(names, products(lhs, *(rims[name] for name in names))):
                z[name] = value
        at_edge = mod_pairs[1]
        outer = z[2]
        if stage == 0:
            node = z[1]
            own_part = at_edge[0] * node[0] + at_edge[1] * (node[1] + outer[3])
            border = jnp.where(even, at_edge[0] * outer[2], own_part)
            border_ref[3, :half, :] = at_edge[0] * node[3]
            border_ref[4, :half, :] = inverses[1]
            tail = outer[5]
        elif stage == 1:
            border = jnp.where(even, at_edge[0] * outer[2], at_edge[1] * outer[3])
            tail = outer[5]
        else:
            border = jnp.where(even, at_edge[0] * outer[2], 0.0)
            energy = jnp.sum(at_edge[0] * rims[2] * outer[1], axis=0, keepdims=True)
            row = lax.broadcasted_iota(jnp.int32, (8, LANES), 0)
            tail = jnp.where(row == 6, energy, outer[5])
        border_ref[stage, :half, :] = border
        border_ref[stage, half:, :] = jnp.where(even, tail, z[1][4] if stage == 0 else 0.0)
        nexts = [None] * len(rims)
        for i in range(first + 1, len(rims) - 1):
            above = jnp.where(even, z[i + 1][2], z[i - 1][2])
            below = jnp.where(even, z[i - 1][3], z[i + 1][3])
            top, low = mod_pairs[i]
            nexts[i] = -inverses[i] * (top * (z[i][0] + above) + low * (z[i][1] + below))
        return nexts[: len(rims) - 1]

    mod_own, mod_prev = mod_main
    mod_sent_down = jnp.where(lanes == 0, 0.0, mod_prev)
    rim = jnp.logical_or(lanes == 0, lanes == 127)

    def borders(stage, f, k):
        moved = pltpu.roll(border_ref[stage], LANES - 1 - 2 * (2 * f + k), 1)
        moved = jnp.where(rim, moved, 0.0)
        return moved[:half], moved[half:]

    def put_dot(which, f, pairs):
        total = sum(a * b for a, b in pairs)
        dots_ref[pl.ds(which * freqs + f, 1), :] = jnp.sum(total, axis=0, keepdims=True)

    def put_strain(stage, f, k, value):
        start = ((stage * 2 + k) * freqs + f) * 8
        strain_ref[pl.ds(pl.multiple_of(start, 8), 8), :] = value

    def moved_to(which, lane, place, f, k):
        shift = (lane + 2 * LANES - 1 - 2 * (2 * f + k)) % LANES
        return jnp.where(lanes == lane, pltpu.roll(border_ref[which, :half, :], shift, 1), place)

    def images(f, stage, fields):
        result = []
        for k, z in enumerate(products(lhs, *fields)):
            added, added_strain = borders(stage, f, k)
            put_strain(stage, f, k, strain_of(z) + added_strain)
            result.append(-(image_of(mod_main, z) + added))
        return result

    def first(f, carry):
        inv = moved_to(4, 0, inner_inv_ref[f], f, 0)
        inv_ref[f] = inv
        loads = [load_ref[2 * f + k] for k in range(2)]
        fields = [inv * b for b in loads]
        image = []
        for k in range(2):
            added, added_strain = borders(0, f, k)
            added = added + moved_to(3, 1, 0.0, f, k)
            image.append(-(image_ref[2 * f + k] + added))
            start = pl.multiple_of((k * freqs + f) * 8, 8)
            put_strain(0, f, k, inner_strain_ref[pl.ds(start, 8), :] + added_strain)
        nexts = [inv * t for t in image]
        for k in range(2):
            field_ref[2 * f + k] = nexts[k]
        put_dot(0, f, zip(fields, loads))
        put_dot(1, f, zip(fields, image))
        put_dot(2, f, zip(nexts, image))
        return carry

    def second(f, carry):
        inv = inv_ref[f]
        fields = [field_ref[2 * f + k] for k in range(2)]
        image = images(f, 1, fields)
        nexts = [inv * t for t in image]
        for k in range(2):
            field_ref[2 * f + k] = nexts[k]
        put_dot(3, f, zip(fields, image))
        put_dot(4, f, zip(nexts, image))
        return carry

    def third(f, carry):
        fields = [field_ref[2 * f + k] for k in range(2)]
        total, extra = 0.0, 0.0
        for k, z in enumerate(products(lhs[: 3 * half + 16], *fields)):
            z11, z22, z12 = z[:3]
            added, added_strain = borders(2, f, k)
            twice = 2.0 * (later(mod_sent_down * z12) + added)
            total = total + fields[k] * (mod_own * z11 + mod_sent_down * z22 + twice)
            strain = strain_of(z) + added_strain
            put_strain(2, f, k, strain)
            extra = extra + strain[6:7]
        dots_ref[pl.ds(5 * freqs + f, 1), :] = -(jnp.sum(total, axis=0, keepdims=True) + extra)
        return carry

    quarter = LANES // 4
    cell = lane_ids(8) // quarter
    outs = (out0_ref, out1_ref, out2_ref, out3_ref)

    def pack(stage, block):
        def comp(k, c):
            start = (((stage * 2 + k) * freqs) + block * 8) * 8 + c
            return strain_ref[pl.ds(start, 8, stride=8), :]

        comps = {(k, c): comp(k, c) for k in range(2) for c in range(6)}
        places = [
            (stage * parts + k * freqs, [(k, c) for c in range(4)]) for k in range(2)
        ] + [(3 * parts + stage * freqs, [(0, 4), (0, 5), (1, 4), (1, 5)])]
        for step in range(4):
            dest = lax.bitwise_xor(freq_group, STEPS[step])
            for row, names in places:
                held = None
                for i, name in enumerate(names):
                    moved = pltpu.roll(comps[name], quarter * ((i + 4 - dest) % 4), 1)
                    held = moved if held is None else jnp.where(cell == i, moved, held)
                outs[step][row + block * 8 : row + block * 8 + 8, :] = held

    for stage, step in enumerate((first, second, third)):
        rims = rim_stage(stage, rims)
        lax.fori_loop(0, freqs, step, 0, unroll=UNROLL)
        for block in range(freqs // 8):
            pack(stage, block)

    dots_ref[DOTS * freqs :, :] = jnp.zeros((256 - DOTS * freqs, LANES), F32)
    sums = [
        jnp.sum(jnp.transpose(dots_ref[i : i + LANES, :]), axis=0, keepdims=True)
        for i in (0, LANES)
    ]
    row = lax.broadcasted_iota(jnp.int32, (8, LANES), 0)
    pair = jnp.where(row % 2 == 0, sums[0], sums[1])
    for i in range(dots_out_ref.shape[0] // 8):
        dots_out_ref[8 * i : 8 * i + 8, :] = pair


def coefficients(h):
    def dot(a, b, energy):
        total = None
        for i, x in enumerate(a):
            for j, y in enumerate(b):
                weight = h[i + j] - h[i + j + 1] if energy else h[i + j]
                term = x * y * weight
                total = term if total is None else total + term
        return total

    one = jnp.ones_like(h[0])
    residual, direction = [one], [one]
    rho = h[0]
    result = []
    for iteration in range(3):
        alpha = rho / dot(direction, direction, True)
        result = [
            (result[i] if i < len(result) else 0.0) + alpha * direction[i]
            for i in range(len(direction))
        ]
        if iteration == 2:
            break
        image = (
            [direction[0]]
            + [direction[i] - direction[i - 1] for i in range(1, len(direction))]
            + [-direction[-1]]
        )
        residual = [
            (residual[i] if i < len(residual) else 0.0) - alpha * image[i]
            for i in range(len(image))
        ]
        rho_next = dot(residual, residual, False)
        beta = rho_next / rho
        rho = rho_next
        direction = [
            residual[i] + (beta * direction[i] if i < len(direction) else 0.0)
            for i in range(len(residual))
        ]
    return result


def final_kernel(
    curves_in_ref, dots_ref, part0_ref, part1_ref, part2_ref, part3_ref,
    table_high_ref, table_low_ref, modulus_in_ref, soil_in_ref,
    modulus_out_ref, strain_out_ref, spectra_ref, curves_ref, modulus_ref, soil_ref, copied,
):
    copies = [
        pltpu.make_async_copy(source, target, copied.at[i])
        for i, (source, target) in enumerate((
            (curves_in_ref, curves_ref), (modulus_in_ref, modulus_ref), (soil_in_ref, soil_ref),
        ))
    ]
    for copy in copies:
        copy.start()
    freq_group = lax.axis_index("freq")
    parts, freqs = 64, 32
    total = jnp.zeros((8, LANES), F32)
    for i in range(dots_ref.shape[0] // 8):
        total = total + dots_ref[8 * i : 8 * i + 8, :]
    square = jnp.concatenate([total, jnp.zeros((LANES - 8, LANES), F32)], 0)
    turned = jnp.transpose(square)
    beside = pltpu.roll(turned, 127, 1)
    h = [turned[freqs * i : freqs * (i + 1)] for i in range(4)]
    h += [beside[freqs * i : freqs * (i + 1)] for i in range(2)]
    coefs = coefficients(h)
    lanes = lane_ids(freqs)
    for step, part_ref in enumerate((part0_ref, part1_ref, part2_ref, part3_ref)):
        source = lax.bitwise_xor(freq_group, STEPS[step])
        weights = [
            jnp.sum(jnp.where(lanes == 2 * source, c, 0.0), axis=1, keepdims=True) for c in coefs
        ]

        def joined(base, per_stage):
            return sum(
                weights[j] * part_ref[base + j * per_stage : base + j * per_stage + freqs, :]
                for j in range(3)
            )

        rest = joined(3 * parts, freqs)
        for k in range(2):
            start = pl.multiple_of(source * parts + k * freqs, freqs)
            spectra_ref[pl.ds(start, freqs), :LANES] = joined(k * freqs, parts)
            side = pltpu.roll(rest, 64, 1) if k else rest
            spectra_ref[pl.ds(start, freqs), LANES:] = jnp.where(lanes < 64, side, 0.0)
    high, low = halves(spectra_ref[...])
    table_high, table_low = table_high_ref[...], table_low_ref[...]
    history = (
        jnp.dot(table_high, low, preferred_element_type=F32)
        + jnp.dot(table_low, high, preferred_element_type=F32)
        + jnp.dot(table_high, high, preferred_element_type=F32)
    )
    squares = history[:, :LANES] ** 2 + history[:, LANES:] ** 2
    squares = squares + pltpu.roll(squares, 64, 1)
    squares = squares + pltpu.roll(squares, 32, 1)
    peak = jnp.max(squares, axis=0, keepdims=True)[:, : LANES // 4] * (1.0 / (4 * freqs))
    peak_strain = STRAIN_FACTOR * jnp.sqrt(peak + EPSILON)
    position = (jnp.log(peak_strain) * (1.0 / np.log(10.0)) - LOG_LOW) / LOG_STEP
    for copy in copies:
        copy.wait()
    soil = soil_ref[...]
    ratio = jnp.zeros_like(position)
    for level in range(curves_ref.shape[1]):
        value = jnp.where(soil == 0, curves_ref[0, level], 0.0)
        for kind in range(1, curves_ref.shape[0]):
            value = jnp.where(soil == kind, curves_ref[kind, level], value)
        ratio = ratio + value * jnp.maximum(0.0, 1.0 - jnp.abs(position - level))
    own = pltpu.roll(modulus_ref[...], (LANES - LANES // 4 * freq_group) % LANES, 1)
    modulus_out_ref[...] = own[:, : LANES // 4] * ratio
    strain_out_ref[...] = peak_strain


def time_table(total_freq):
    order = np.arange(1, total_freq + 1)
    phase = (np.arange(NT)[:, None] * order[None, :] % NT) * (2.0 * np.pi / NT)
    waves = np.stack([np.cos(phase), -np.sin(phase)], 1)
    table = waves.reshape(NT, 2, 4, total_freq // 4).transpose(0, 2, 1, 3).reshape(NT, -1)
    high = table.astype(np.float32).astype(jnp.bfloat16)
    low = (table - high.astype(np.float64)).astype(np.float32).astype(jnp.bfloat16)
    return high, low


def per_device(
    load, stiffness, mass_template, modulus, element_mass, strain_map, curves, soil_type
):
    half, freq_dev, _, nodes = load.shape
    parts = 2 * freq_dev
    groups = lax.axis_size("freq")
    slabs = lax.axis_size("elem")
    rows = load.reshape(half * parts, nodes)
    modulus_row, mass_row = modulus.reshape(1, nodes), element_mass.reshape(1, nodes)
    first, second, own, lhs, cols, rows = pl.pallas_call(
        edges_kernel,
        out_shape=[
            pltpu.VMEM((SENT_ROWS, LANES), F32),
            pltpu.VMEM((SENT_ROWS, LANES), F32),
            pltpu.VMEM((OWN_ROWS, LANES), F32),
            pltpu.VMEM((4 * half + 16, 2 * LANES), BF16),
            pltpu.VMEM((half, LANES), F32),
            pltpu.VMEM((half * parts, LANES), F32),
        ],
        in_specs=[HBM] * 6,
        out_specs=[VMEM] * 6,
        scratch_shapes=[
            pltpu.VMEM((LANES, LANES), F32),
            pltpu.VMEM((LANES, LANES), F32),
            pltpu.VMEM((LANES, LANES), F32),
            pltpu.VMEM((2, 1, LANES), F32),
            pltpu.VMEM((half, LANES), F32),
            pltpu.VMEM((1, 2 * half), F32),
            pltpu.VMEM((2 * half, 2 * half), F32),
            pltpu.VMEM(strain_map.shape, F32),
            pltpu.SemaphoreType.DMA((3+6,)),
        ],
        name="edges",
    )(rows, modulus_row, mass_row, stiffness, mass_template.reshape(1, -1), strain_map)
    met_first = lax.ppermute(first, "elem", [(i, i ^ 1) for i in range(slabs)])
    met_second = lax.ppermute(
        second, "elem", [(i, i + 1 if i % 2 else i - 1) for i in range(1, slabs - 1)]
    )
    inner = pl.pallas_call(
        inner_kernel,
        out_shape=[
            pltpu.VMEM((parts, half, LANES), F32),
            pltpu.VMEM((parts, half, LANES), F32),
            pltpu.VMEM((freq_dev, half, LANES), F32),
            pltpu.VMEM((parts * 8, LANES), F32),
        ],
        in_specs=[VMEM] * 4,
        out_specs=[VMEM] * 4,
        compiler_params=pltpu.CompilerParams(vmem_limit_bytes=32 * 1024 * 1024),
        name="inner",
    )(rows, own, lhs, cols)
    packed = 9 * freq_dev
    outs = pl.pallas_call(
        main_kernel,
        out_shape=[jax.ShapeDtypeStruct((packed, LANES), F32)] * 4
        + [jax.ShapeDtypeStruct((2 * slabs * groups, LANES), F32)],
        in_specs=[VMEM] * 9,
        out_specs=[VMEM] * 5,
        scratch_shapes=[
            pltpu.VMEM((3 * parts * 8, LANES), F32),
            pltpu.VMEM((parts, half, LANES), F32),
            pltpu.VMEM((freq_dev, half, LANES), F32),
            pltpu.VMEM((5, half + 8, LANES), F32),
            pltpu.VMEM((256, LANES), F32),
        ],
        compiler_params=pltpu.CompilerParams(vmem_limit_bytes=32 * 1024 * 1024),
        name="krylov",
    )(*inner, own, met_second, met_first, lhs, cols)
    received = [outs[0]] + [
        lax.ppermute(outs[step], "freq", [(i, i ^ STEPS[step]) for i in range(groups)])
        for step in range(1, groups)
    ]
    dots = lax.all_to_all(
        outs[4].reshape(slabs * groups, 2, LANES), ("elem", "freq"), 0, 0
    ).reshape(-1, LANES)
    table_high, table_low = time_table(freq_dev * groups)
    quarter = nodes // groups
    new_modulus, peak_strain = pl.pallas_call(
        final_kernel,
        out_shape=[jax.ShapeDtypeStruct((1, quarter), F32)] * 2,
        in_specs=[HBM] + [VMEM] * 7 + [HBM] * 2,
        out_specs=[VMEM] * 2,
        scratch_shapes=[
            pltpu.VMEM((groups * parts, 2 * LANES), F32),
            pltpu.SMEM(curves.shape, F32),
            pltpu.VMEM((1, nodes), F32),
            pltpu.VMEM((1, quarter), jnp.int32),
            pltpu.SemaphoreType.DMA((3,)),
        ],
        compiler_params=pltpu.CompilerParams(vmem_limit_bytes=32 * 1024 * 1024),
        name="response",
    )(curves, dots, *received, jnp.asarray(table_high), jnp.asarray(table_low),
      modulus_row, soil_type.reshape(1, quarter))
    return new_modulus.reshape(quarter), peak_strain.reshape(quarter)


def solution(mesh):
    in_specs = (
        P(None, "freq", None, "elem"),
        P(),
        P(),
        P("elem"),
        P("elem"),
        P(),
        P(),
        P(("elem", "freq")),
    )
    out_specs = (P(("elem", "freq")), P(("elem", "freq")))
    return jax.shard_map(
        per_device, mesh=mesh, in_specs=in_specs, out_specs=out_specs, check_vma=False
    )
```

```python
import functools
import operator

import jax
import jax.numpy as jnp
import numpy as np
from jax import lax
from jax.experimental import pallas as pl
from jax.experimental.pallas import tpu as pltpu
from jax.sharding import PartitionSpec as P

NT = 512
MASS_COEF = 0.5
LOG_LOW = -1.5
LOG_STEP = 0.2
STRAIN_FACTOR = 0.65
EPSILON = 1e-06
LANES = 128
SLOT = 8
DEPTH = 176
UNROLL = 32
STEPS = (0, 1, 3, 2)
DOTS = 6
F32 = jnp.float32
BF16 = jnp.bfloat16
VMEM = pl.BlockSpec(memory_space=pltpu.VMEM)
SMEM = pl.BlockSpec(memory_space=pltpu.SMEM)
HBM = pl.BlockSpec(memory_space=pltpu.HBM)
OWN_ROWS, OWN_AT = 104, 96
SENT_ROWS, SENT_AT = 80, 72


def lane_ids(rows=1):
    return lax.broadcasted_iota(jnp.int32, (rows, LANES), 1)


def later(x):
    return pltpu.roll(x, 127, 1)


def earlier(x):
    return pltpu.roll(x, 1, 1)


def halves(x):
    high = x.astype(BF16)
    return high, (x - high.astype(F32)).astype(BF16)


def edges_kernel(
    load_ref, modulus_ref, mass_ref, stiffness_ref, template_ref, strain_map_ref,
    first_ref, second_ref, own_ref, lhs_ref, cols_ref, buffer_ref,
    slots_ref, turned_ref, square_ref, small_ref, third_ref, small_template_ref, small_stiff_ref, small_map_ref, copied,
):
    half, parts, chunks = 48, 64, 3
    per = half // chunks
    pieces = 3
    piece = half * parts // pieces
    full = 2 * half
    comps = strain_map_ref.shape[0]
    copies = [
        pltpu.make_async_copy(
            load_ref.at[pl.ds(i * piece, piece)], buffer_ref.at[pl.ds(i * piece, piece)],
            copied.at[i],
        )
        for i in range(pieces)
    ]
    smalls = [
        pltpu.make_async_copy(source, target, copied.at[pieces + i])
        for i, (source, target) in enumerate((
            (modulus_ref, small_ref.at[0]), (mass_ref, small_ref.at[1]),
            (template_ref, small_template_ref), (stiffness_ref, small_stiff_ref), (strain_map_ref, small_map_ref),
        ))
    ]
    for copy in smalls[2:] + copies + smalls[:2]:
        copy.start()
    square_ref[...] = jnp.zeros(square_ref.shape, F32)

    for copy in smalls[2:]:
        copy.wait()
    square_ref[:full, :full] = small_stiff_ref[...]
    square_ref[full : full + comps, :full] = small_map_ref[...]
    square_ref[full + 8 : full + 9, :full] = small_template_ref[...]
    stiff = square_ref[:full, :]
    same = lax.broadcasted_iota(jnp.int32, (full, LANES), 0) == lane_ids(full)
    kdiag = jnp.sum(jnp.where(same, stiff, 0.0), axis=1, keepdims=True)
    template = jnp.sum(
        jnp.where(same, square_ref[full + 8 : full + 9, :], 0.0), axis=1, keepdims=True
    )
    lane = lane_ids(half)
    columns = jnp.zeros((half, LANES), F32)
    for i, col in enumerate((kdiag[:half], kdiag[half:], template[:half], template[half:])):
        columns = jnp.where(lane == i, col, columns)
    cols_ref[...] = columns
    off = jnp.where(same, 0.0, stiff)
    strain_rows = square_ref[full : full + 8, :]
    moved = pltpu.roll(off, LANES - half, 1)
    moved_rows = pltpu.roll(strain_rows, LANES - half, 1)
    stacked = jnp.concatenate(
        [off[:half], moved[half:], moved[:half], strain_rows, moved_rows, off[half:]], 0
    )
    rows = stacked.shape[0]
    lane = lane_ids(rows)
    stacked = jnp.where(lane < half, stacked, 0.0)
    high, low = halves(stacked)
    high = high.astype(F32)
    lhs_ref[:, :LANES] = (high + pltpu.roll(high, half, 1)).astype(BF16)
    lhs_ref[:, LANES:] = low

    slot = lane_ids(parts) // SLOT
    for chunk in range(chunks):
        for copy in copies[chunk * pieces // chunks : (chunk + 1) * pieces // chunks]:
            copy.wait()
        held = jnp.zeros((parts, LANES), F32)
        for i in range(per):
            start = (chunk * per + i) * parts
            moved = pltpu.roll(buffer_ref[start : start + parts, :], 2 + SLOT * i, 1)
            held = jnp.where(slot == i, moved, held)
        at = chunk * per
        for turn, shift in enumerate((LANES - 1, LANES - 3)):
            slots_ref[pl.ds(0, parts, stride=2), :] = held
            slots_ref[pl.ds(1, parts, stride=2), :] = pltpu.roll(held, shift, 1)
            turned_ref[...] = jnp.transpose(slots_ref[...])
            if turn == 0:
                own_ref[at : at + per, :] = turned_ref[pl.ds(1, per, stride=SLOT), :]
            else:
                own_ref[half + at : half + at + per, :] = turned_ref[pl.ds(0, per, stride=SLOT), :]
                third_ref[at : at + per, :] = turned_ref[pl.ds(1, per, stride=SLOT), :]
    for copy in smalls[:2]:
        copy.wait()
    own_ref[OWN_AT : OWN_AT + 1, :] = small_ref[0]
    own_ref[OWN_AT + 1 : OWN_AT + 2, :] = small_ref[1]
    own_ref[OWN_AT + 2 :, :] = jnp.zeros((OWN_ROWS - OWN_AT - 2, LANES), F32)
    even = lane_ids() % 2 == 0
    outer, inner = own_ref[:half, :], own_ref[half : 2 * half, :]
    third = third_ref[...]
    up = [jnp.where(even, outer, earlier(inner)), jnp.zeros((half // 2, LANES), F32)]
    down = [
        jnp.where(even, later(inner), outer),
        jnp.where(even, later(third[half // 2 :]), third[: half // 2]),
    ]
    even_device = lax.axis_index("elem") % 2 == 0
    for ref, ahead in ((first_ref, even_device), (second_ref, jnp.logical_not(even_device))):
        ref[:half, :] = jnp.where(ahead, up[0], down[0])
        ref[half:SENT_AT, :] = jnp.where(ahead, up[1], down[1])
        ref[SENT_AT:, :] = own_ref[OWN_AT:, :]


def shift_of(order, total):
    return MASS_COEF * (order * (1.0 / total)) ** 2


def columns_of(cols):
    return [cols[:, i : i + 1] for i in range(4)]


def diagonals(columns, mod, mass):
    kd_top, kd_low, mt_top, mt_low = columns
    return kd_top * mod[0] + kd_low * mod[1], mt_top * mass[0] + mt_low * mass[1]


def products(lhs, *fields):
    half = fields[0].shape[0]
    split = [halves(field) for field in fields]
    high = jnp.concatenate([h for h, _ in split], 1)
    low = jnp.concatenate([l for _, l in split], 1)
    gap = jnp.zeros((DEPTH - 3 * half, high.shape[1]), BF16)
    result = jnp.dot(lhs, jnp.concatenate([high, low, gap, high], 0), preferred_element_type=F32)
    cut = [0, half, 2 * half, 3 * half, 3 * half + 8, 3 * half + 16, lhs.shape[0]]
    return [
        [result[cut[i] : cut[i + 1], LANES * k : LANES * (k + 1)] for i in (0, 1, 2, 5, 3, 4)]
        for k in range(len(fields))
    ]


def image_of(mod, z):
    lanes = lane_ids()
    own, prev = mod
    up = jnp.where(lanes == 127, 0.0, own)
    down = jnp.where(lanes == 0, 0.0, prev)
    return own * z[0] + prev * z[1] + later(down * z[2]) + earlier(up * z[3])


def strain_of(z):
    return z[4] + jnp.where(lane_ids() == 127, 0.0, later(z[5]))


def inner_kernel(
    load_ref, own_ref, lhs_ref, cols_ref, image_ref, field_ref, inv_ref, strain_ref
):
    half, parts = 48, 64
    freqs = parts // 2
    first_order = (lax.axis_index("freq") * freqs + 1).astype(F32)
    lanes = lane_ids()

    def row(at):
        own = own_ref[OWN_AT + at : OWN_AT + at + 1, :]
        return own, jnp.where(lanes == 0, 0.0, earlier(own))

    mod, mass = row(0), row(1)
    stiff, weight = diagonals(columns_of(cols_ref[...]), mod, mass)
    lhs = lhs_ref[:, :DEPTH]

    def step(f, carry):
        shift = shift_of(first_order + f.astype(F32), 4 * freqs)
        inv = jnp.where(lanes == 0, 0.0, 1.0 / (stiff + shift * weight))
        inv_ref[f] = inv
        loads = [load_ref[pl.ds(2 * f + k, half, stride=parts), :] for k in range(2)]
        for k, z in enumerate(products(lhs, *(inv * b for b in loads))):
            field_ref[2 * f + k] = loads[k]
            image_ref[2 * f + k] = image_of(mod, z)
            start = pl.multiple_of((k * freqs + f) * 8, 8)
            strain_ref[pl.ds(start, 8), :] = strain_of(z)
        return carry

    lax.fori_loop(0, freqs, step, 0, unroll=UNROLL)


def main_kernel(
    image_ref, load_ref, inner_inv_ref, inner_strain_ref,
    own_ref, second_ref, first_ref, lhs_ref, cols_ref,
    out0_ref, out1_ref, out2_ref, out3_ref, dots_out_ref,
    strain_ref, field_ref, inv_ref, border_ref, dots_ref,
):
    half, parts = 48, 64
    freqs = parts // 2
    freq_group = lax.axis_index("freq")
    slab = lax.axis_index("elem")
    is_last = slab == lax.axis_size("elem") - 1
    ahead = slab % 2 == 0
    met_first, met_second = first_ref[...], second_ref[...]
    from_right = jnp.where(ahead, met_first, met_second)
    from_left = jnp.where(ahead, met_second, met_first)
    first_order = (freq_group * freqs + 1).astype(F32)
    lanes = lane_ids()
    even = lanes % 2 == 0

    columns = columns_of(cols_ref[...])
    def rows_of(at):
        own = own_ref[OWN_AT + at : OWN_AT + at + 1, :]
        left, right = (r[SENT_AT + at : SENT_AT + at + 1] for r in (from_left, from_right))
        prev = jnp.where(lanes == 0, earlier(left), earlier(own))

        def sides(*upper_lower):
            (upper, i), (lower, j) = upper_lower
            upper, lower = upper[:, i : i + 1], lower[:, j : j + 1]
            return jnp.where(even, upper, lower)

        zero = jnp.zeros_like(own)
        pairs = [
            (sides((own, 126), (own, 1)), sides((own, 125), (own, 0))),
            (sides((own, 127), (own, 0)), sides((own, 126), (left, 127))),
            (sides((right, 0), (left, 127)), sides((own, 127), (left, 126))),
            (sides((right, 1), (left, 126)), sides((right, 0), (left, 125))),
            (sides((right, 2), (zero, 0)), sides((right, 1), (zero, 0))),
        ]
        return (own, prev), pairs

    mod_main, mod_pairs = rows_of(0)
    mass_main, mass_pairs = rows_of(1)

    lhs = lhs_ref[:, :DEPTH]

    order = first_order + (lanes // 4).astype(F32)
    beyond = jnp.logical_and(even, is_last)
    inverses = []
    for i, (mod, mass) in enumerate(zip(mod_pairs, mass_pairs)):
        stiff, weight = diagonals(columns, mod, mass)
        diag = stiff + shift_of(order, 4 * freqs) * weight
        good = diag > 0
        if i >= 2:
            good = jnp.logical_and(good, jnp.logical_not(beyond))
        inverses.append(jnp.where(good, 1.0 / diag, 0.0))

    third = from_right[half:SENT_AT]
    rims = [
        own_ref[half : 2 * half, :],
        own_ref[:half, :],
        jnp.where(even, later(from_right[:half]), earlier(from_left[:half])),
        jnp.where(even, from_right[:half], from_left[:half]),
        jnp.where(even, jnp.concatenate([later(third), third], 0), 0.0),
    ]
    rims = [field * inv for field, inv in zip(rims, inverses)]

    def rim_stage(stage, rims):
        first = stage
        z = {}
        for i in range(first, len(rims), 2):
            names = list(range(i, min(i + 2, len(rims))))
            for name, value in zip(names, products(lhs, *(rims[name] for name in names))):
                z[name] = value
        at_edge = mod_pairs[1]
        outer = z[2]
        if stage == 0:
            node = z[1]
            own_part = at_edge[0] * node[0] + at_edge[1] * (node[1] + outer[3])
            border = jnp.where(even, at_edge[0] * outer[2], own_part)
            border_ref[3, :half, :] = at_edge[0] * node[3]
            border_ref[4, :half, :] = inverses[1]
            tail = outer[5]
        elif stage == 1:
            border = jnp.where(even, at_edge[0] * outer[2], at_edge[1] * outer[3])
            tail = outer[5]
        else:
            border = jnp.where(even, at_edge[0] * outer[2], 0.0)
            energy = jnp.sum(at_edge[0] * rims[2] * outer[1], axis=0, keepdims=True)
            row = lax.broadcasted_iota(jnp.int32, (8, LANES), 0)
            tail = jnp.where(row == 6, energy, outer[5])
        border_ref[stage, :half, :] = border
        border_ref[stage, half:, :] = jnp.where(even, tail, z[1][4] if stage == 0 else 0.0)
        nexts = [None] * len(rims)
        for i in range(first + 1, len(rims) - 1):
            above = jnp.where(even, z[i + 1][2], z[i - 1][2])
            below = jnp.where(even, z[i - 1][3], z[i + 1][3])
            top, low = mod_pairs[i]
            nexts[i] = -inverses[i] * (top * (z[i][0] + above) + low * (z[i][1] + below))
        return nexts[: len(rims) - 1]

    mod_own, mod_prev = mod_main
    mod_sent_down = jnp.where(lanes == 0, 0.0, mod_prev)
    rim = jnp.logical_or(lanes == 0, lanes == 127)

    def borders(stage, f, k):
        moved = pltpu.roll(border_ref[stage], LANES - 1 - 2 * (2 * f + k), 1)
        moved = jnp.where(rim, moved, 0.0)
        return moved[:half], moved[half:]

    def put_dot(which, f, pairs):
        total = functools.reduce(operator.add, (a * b for a, b in pairs))
        dots_ref[pl.ds(which * freqs + f, 1), :] = jnp.sum(total, axis=0, keepdims=True)

    def put_strain(stage, f, k, value):
        start = ((stage * 2 + k) * freqs + f) * 8
        strain_ref[pl.ds(pl.multiple_of(start, 8), 8), :] = value

    def moved_to(which, lane, place, f, k):
        shift = (lane + 2 * LANES - 1 - 2 * (2 * f + k)) % LANES
        return jnp.where(lanes == lane, pltpu.roll(border_ref[which, :half, :], shift, 1), place)

    def images(f, stage, fields):
        result = []
        for k, z in enumerate(products(lhs, *fields)):
            added, added_strain = borders(stage, f, k)
            put_strain(stage, f, k, strain_of(z) + added_strain)
            result.append(-(image_of(mod_main, z) + added))
        return result

    def first(f, carry):
        inv = moved_to(4, 0, inner_inv_ref[f], f, 0)
        inv_ref[f] = inv
        loads = [load_ref[2 * f + k] for k in range(2)]
        fields = [inv * b for b in loads]
        image = []
        for k in range(2):
            added, added_strain = borders(0, f, k)
            added = added + moved_to(3, 1, 0.0, f, k)
            image.append(-(image_ref[2 * f + k] + added))
            start = pl.multiple_of((k * freqs + f) * 8, 8)
            put_strain(0, f, k, inner_strain_ref[pl.ds(start, 8), :] + added_strain)
        nexts = [inv * t for t in image]
        for k in range(2):
            field_ref[2 * f + k] = nexts[k]
        put_dot(0, f, zip(fields, loads))
        put_dot(1, f, zip(fields, image))
        put_dot(2, f, zip(nexts, image))
        return carry

    def second(f, carry):
        inv = inv_ref[f]
        fields = [field_ref[2 * f + k] for k in range(2)]
        image = images(f, 1, fields)
        nexts = [inv * t for t in image]
        for k in range(2):
            field_ref[2 * f + k] = nexts[k]
        put_dot(3, f, zip(fields, image))
        put_dot(4, f, zip(nexts, image))
        return carry

    def third(f, carry):
        fields = [field_ref[2 * f + k] for k in range(2)]
        totals, extras = [], []
        for k, z in enumerate(products(lhs[: 3 * half + 16], *fields)):
            z11, z22, z12 = z[:3]
            added, added_strain = borders(2, f, k)
            twice = 2.0 * (later(mod_sent_down * z12) + added)
            totals.append(fields[k] * (mod_own * z11 + mod_sent_down * z22 + twice))
            strain = strain_of(z) + added_strain
            put_strain(2, f, k, strain)
            extras.append(strain[6:7])
        energy = jnp.sum(totals[0] + totals[1], axis=0, keepdims=True) + extras[0] + extras[1]
        dots_ref[pl.ds(5 * freqs + f, 1), :] = -energy
        return carry

    quarter = LANES // 4
    cell = lane_ids(8) // quarter
    outs = (out0_ref, out1_ref, out2_ref, out3_ref)

    def pack(stage, block):
        def comp(k, c):
            start = (((stage * 2 + k) * freqs) + block * 8) * 8 + c
            return strain_ref[pl.ds(start, 8, stride=8), :]

        comps = {(k, c): comp(k, c) for k in range(2) for c in range(6)}
        places = [
            (stage * parts + k * freqs, [(k, c) for c in range(4)]) for k in range(2)
        ] + [(3 * parts + stage * freqs, [(0, 4), (0, 5), (1, 4), (1, 5)])]
        stores = []
        for step in range(4):
            dest = lax.bitwise_xor(freq_group, STEPS[step])
            for row, names in places:
                held = None
                for i, name in enumerate(names):
                    moved = pltpu.roll(comps[name], quarter * ((i + 4 - dest) % 4), 1)
                    held = moved if held is None else jnp.where(cell == i, moved, held)
                stores.append((step, row + block * 8, held))
        for step, start, held in stores:
            outs[step][start : start + 8, :] = held

    for stage, step in enumerate((first, second, third)):
        rims = rim_stage(stage, rims)
        lax.fori_loop(0, freqs, step, 0, unroll=UNROLL)
        for block in range(freqs // 8):
            pack(stage, block)

    dots_ref[DOTS * freqs :, :] = jnp.zeros((256 - DOTS * freqs, LANES), F32)
    sums = [
        jnp.sum(jnp.transpose(dots_ref[i : i + LANES, :]), axis=0, keepdims=True)
        for i in (0, LANES)
    ]
    row = lax.broadcasted_iota(jnp.int32, (8, LANES), 0)
    pair = jnp.where(row % 2 == 0, sums[0], sums[1])
    for i in range(dots_out_ref.shape[0] // 8):
        dots_out_ref[8 * i : 8 * i + 8, :] = pair


def coefficients(h):
    def dot(a, b, energy):
        total = None
        for i, x in enumerate(a):
            for j, y in enumerate(b):
                weight = h[i + j] - h[i + j + 1] if energy else h[i + j]
                term = x * y * weight
                total = term if total is None else total + term
        return total

    one = jnp.ones_like(h[0])
    residual, direction = [one], [one]
    rho = h[0]
    result = []
    for iteration in range(3):
        alpha = rho / dot(direction, direction, True)
        result = [
            (result[i] if i < len(result) else 0.0) + alpha * direction[i]
            for i in range(len(direction))
        ]
        if iteration == 2:
            break
        image = (
            [direction[0]]
            + [direction[i] - direction[i - 1] for i in range(1, len(direction))]
            + [-direction[-1]]
        )
        residual = [
            (residual[i] if i < len(residual) else 0.0) - alpha * image[i]
            for i in range(len(image))
        ]
        rho_next = dot(residual, residual, False)
        beta = rho_next / rho
        rho = rho_next
        direction = [
            residual[i] + (beta * direction[i] if i < len(direction) else 0.0)
            for i in range(len(residual))
        ]
    return result


def final_kernel(
    curves_in_ref, dots_ref, part0_ref, part1_ref, part2_ref, part3_ref,
    table_high_ref, table_low_ref, modulus_in_ref, soil_in_ref,
    modulus_out_ref, strain_out_ref, spectra_ref, curves_ref, modulus_ref, soil_ref, copied,
):
    copies = [
        pltpu.make_async_copy(source, target, copied.at[i])
        for i, (source, target) in enumerate((
            (curves_in_ref, curves_ref), (modulus_in_ref, modulus_ref), (soil_in_ref, soil_ref),
        ))
    ]
    for copy in copies:
        copy.start()
    freq_group = lax.axis_index("freq")
    parts, freqs = 64, 32
    total = jnp.zeros((8, LANES), F32)
    for i in range(dots_ref.shape[0] // 8):
        total = total + dots_ref[8 * i : 8 * i + 8, :]
    square = jnp.concatenate([total, jnp.zeros((LANES - 8, LANES), F32)], 0)
    turned = jnp.transpose(square)
    beside = pltpu.roll(turned, 127, 1)
    h = [turned[freqs * i : freqs * (i + 1)] for i in range(4)]
    h += [beside[freqs * i : freqs * (i + 1)] for i in range(2)]
    coefs = coefficients(h)
    lanes = lane_ids(freqs)
    for step, part_ref in enumerate((part0_ref, part1_ref, part2_ref, part3_ref)):
        source = lax.bitwise_xor(freq_group, STEPS[step])
        weights = [
            jnp.sum(jnp.where(lanes == 2 * source, c, 0.0), axis=1, keepdims=True) for c in coefs
        ]

        def joined(base, per_stage):
            return functools.reduce(operator.add, (
                weights[j] * part_ref[base + j * per_stage : base + j * per_stage + freqs, :]
                for j in range(3)
            ))

        rest = joined(3 * parts, freqs)
        for k in range(2):
            start = pl.multiple_of(source * parts + k * freqs, freqs)
            spectra_ref[pl.ds(start, freqs), :LANES] = joined(k * freqs, parts)
            side = pltpu.roll(rest, 64, 1) if k else rest
            spectra_ref[pl.ds(start, freqs), LANES:] = jnp.where(lanes < 64, side, 0.0)
    high, low = halves(spectra_ref[...])
    table_high, table_low = table_high_ref[...], table_low_ref[...]
    history = jnp.dot(
        jnp.concatenate([table_high, table_low, table_high], 1),
        jnp.concatenate([high, high, low], 0), preferred_element_type=F32,
    )
    squares = history[:, :LANES] ** 2 + history[:, LANES:] ** 2
    squares = squares + pltpu.roll(squares, 64, 1)
    squares = squares + pltpu.roll(squares, 32, 1)
    peak = jnp.max(squares, axis=0, keepdims=True)[:, : LANES // 4] * (1.0 / (4 * freqs))
    peak_strain = STRAIN_FACTOR * jnp.sqrt(peak + EPSILON)
    position = (jnp.log(peak_strain) * (1.0 / np.log(10.0)) - LOG_LOW) / LOG_STEP
    for copy in copies:
        copy.wait()
    soil = soil_ref[...]
    ratio = jnp.zeros_like(position)
    for level in range(curves_ref.shape[1]):
        value = jnp.where(soil == 0, curves_ref[0, level], 0.0)
        for kind in range(1, curves_ref.shape[0]):
            value = jnp.where(soil == kind, curves_ref[kind, level], value)
        ratio = ratio + value * jnp.maximum(0.0, 1.0 - jnp.abs(position - level))
    own = pltpu.roll(modulus_ref[...], (LANES - LANES // 4 * freq_group) % LANES, 1)
    modulus_out_ref[...] = own[:, : LANES // 4] * ratio
    strain_out_ref[...] = peak_strain


def time_table(total_freq):
    order = np.arange(1, total_freq + 1)
    phase = (np.arange(NT)[:, None] * order[None, :] % NT) * (2.0 * np.pi / NT)
    waves = np.stack([np.cos(phase), -np.sin(phase)], 1)
    table = waves.reshape(NT, 2, 4, total_freq // 4).transpose(0, 2, 1, 3).reshape(NT, -1)
    high = table.astype(np.float32).astype(jnp.bfloat16)
    low = (table - high.astype(np.float64)).astype(np.float32).astype(jnp.bfloat16)
    return high, low


def per_device(
    load, stiffness, mass_template, modulus, element_mass, strain_map, curves, soil_type
):
    half, freq_dev, _, nodes = load.shape
    parts = 2 * freq_dev
    groups = lax.axis_size("freq")
    slabs = lax.axis_size("elem")
    rows = load.reshape(half * parts, nodes)
    modulus_row, mass_row = modulus.reshape(1, nodes), element_mass.reshape(1, nodes)
    first, second, own, lhs, cols, rows = pl.pallas_call(
        edges_kernel,
        out_shape=[
            pltpu.VMEM((SENT_ROWS, LANES), F32),
            pltpu.VMEM((SENT_ROWS, LANES), F32),
            pltpu.VMEM((OWN_ROWS, LANES), F32),
            pltpu.VMEM((4 * half + 16, 2 * LANES), BF16),
            pltpu.VMEM((half, LANES), F32),
            pltpu.VMEM((half * parts, LANES), F32),
        ],
        in_specs=[HBM] * 6,
        out_specs=[VMEM] * 6,
        scratch_shapes=[
            pltpu.VMEM((LANES, LANES), F32),
            pltpu.VMEM((LANES, LANES), F32),
            pltpu.VMEM((LANES, LANES), F32),
            pltpu.VMEM((2, 1, LANES), F32),
            pltpu.VMEM((half, LANES), F32),
            pltpu.VMEM((1, 2 * half), F32),
            pltpu.VMEM((2 * half, 2 * half), F32),
            pltpu.VMEM(strain_map.shape, F32),
            pltpu.SemaphoreType.DMA((3+6,)),
        ],
        name="edges",
    )(rows, modulus_row, mass_row, stiffness, mass_template.reshape(1, -1), strain_map)
    met_first = lax.ppermute(first, "elem", [(i, i ^ 1) for i in range(slabs)])
    met_second = lax.ppermute(
        second, "elem", [(i, i + 1 if i % 2 else i - 1) for i in range(1, slabs - 1)]
    )
    inner = pl.pallas_call(
        inner_kernel,
        out_shape=[
            pltpu.VMEM((parts, half, LANES), F32),
            pltpu.VMEM((parts, half, LANES), F32),
            pltpu.VMEM((freq_dev, half, LANES), F32),
            pltpu.VMEM((parts * 8, LANES), F32),
        ],
        in_specs=[VMEM] * 4,
        out_specs=[VMEM] * 4,
        compiler_params=pltpu.CompilerParams(vmem_limit_bytes=32 * 1024 * 1024),
        name="inner",
    )(rows, own, lhs, cols)
    packed = 9 * freq_dev
    outs = pl.pallas_call(
        main_kernel,
        out_shape=[jax.ShapeDtypeStruct((packed, LANES), F32)] * 4
        + [jax.ShapeDtypeStruct((2 * slabs * groups, LANES), F32)],
        in_specs=[VMEM] * 9,
        out_specs=[VMEM] * 5,
        scratch_shapes=[
            pltpu.VMEM((3 * parts * 8, LANES), F32),
            pltpu.VMEM((parts, half, LANES), F32),
            pltpu.VMEM((freq_dev, half, LANES), F32),
            pltpu.VMEM((5, half + 8, LANES), F32),
            pltpu.VMEM((256, LANES), F32),
        ],
        compiler_params=pltpu.CompilerParams(vmem_limit_bytes=32 * 1024 * 1024),
        name="krylov",
    )(*inner, own, met_second, met_first, lhs, cols)
    received = [outs[0]] + [
        lax.ppermute(outs[step], "freq", [(i, i ^ STEPS[step]) for i in range(groups)])
        for step in range(1, groups)
    ]
    dots = lax.all_to_all(
        outs[4].reshape(slabs * groups, 2, LANES), ("elem", "freq"), 0, 0
    ).reshape(-1, LANES)
    table_high, table_low = time_table(freq_dev * groups)
    quarter = nodes // groups
    new_modulus, peak_strain = pl.pallas_call(
        final_kernel,
        out_shape=[jax.ShapeDtypeStruct((1, quarter), F32)] * 2,
        in_specs=[HBM] + [VMEM] * 7 + [HBM] * 2,
        out_specs=[VMEM] * 2,
        scratch_shapes=[
            pltpu.VMEM((groups * parts, 2 * LANES), F32),
            pltpu.SMEM(curves.shape, F32),
            pltpu.VMEM((1, nodes), F32),
            pltpu.VMEM((1, quarter), jnp.int32),
            pltpu.SemaphoreType.DMA((3,)),
        ],
        compiler_params=pltpu.CompilerParams(vmem_limit_bytes=32 * 1024 * 1024),
        name="response",
    )(curves, dots, *received, jnp.asarray(table_high), jnp.asarray(table_low),
      modulus_row, soil_type.reshape(1, quarter))
    return new_modulus.reshape(quarter), peak_strain.reshape(quarter)


def solution(mesh):
    in_specs = (
        P(None, "freq", None, "elem"),
        P(),
        P(),
        P("elem"),
        P("elem"),
        P(),
        P(),
        P(("elem", "freq")),
    )
    out_specs = (P(("elem", "freq")), P(("elem", "freq")))
    return jax.shard_map(
        per_device, mesh=mesh, in_specs=in_specs, out_specs=out_specs, check_vma=False
    )
```

```python
import functools
import operator

import jax
import jax.numpy as jnp
import numpy as np
from jax import lax
from jax.experimental import pallas as pl
from jax.experimental.pallas import tpu as pltpu
from jax.sharding import PartitionSpec as P

NT = 512
MASS_COEF = 0.5
LOG_LOW = -1.5
LOG_STEP = 0.2
STRAIN_FACTOR = 0.65
EPSILON = 1e-06
LANES = 128
SLOT = 8
DEPTH = 176
UNROLL = 32
AHEAD = 1
STEPS = (0, 1, 3, 2)
DOTS = 6
F32 = jnp.float32
BF16 = jnp.bfloat16
VMEM = pl.BlockSpec(memory_space=pltpu.VMEM)
SMEM = pl.BlockSpec(memory_space=pltpu.SMEM)
HBM = pl.BlockSpec(memory_space=pltpu.HBM)
OWN_ROWS, OWN_AT = 104, 96
SENT_ROWS, SENT_AT = 80, 72


def lane_ids(rows=1):
    return lax.broadcasted_iota(jnp.int32, (rows, LANES), 1)


def later(x):
    return pltpu.roll(x, 127, 1)


def earlier(x):
    return pltpu.roll(x, 1, 1)


def halves(x):
    high = x.astype(BF16)
    return high, (x - high.astype(F32)).astype(BF16)


def edges_kernel(
    load_ref, modulus_ref, mass_ref, stiffness_ref, template_ref, strain_map_ref,
    first_ref, second_ref, own_ref, lhs_ref, cols_ref, buffer_ref,
    slots_ref, turned_ref, square_ref, small_ref, third_ref, small_template_ref, small_stiff_ref, small_map_ref, copied,
):
    half, parts, chunks = 48, 64, 3
    per = half // chunks
    pieces = 3
    piece = half * parts // pieces
    full = 2 * half
    comps = strain_map_ref.shape[0]
    copies = [
        pltpu.make_async_copy(
            load_ref.at[pl.ds(i * piece, piece)], buffer_ref.at[pl.ds(i * piece, piece)],
            copied.at[i],
        )
        for i in range(pieces)
    ]
    smalls = [
        pltpu.make_async_copy(source, target, copied.at[pieces + i])
        for i, (source, target) in enumerate((
            (modulus_ref, small_ref.at[0]), (mass_ref, small_ref.at[1]),
            (template_ref, small_template_ref), (stiffness_ref, small_stiff_ref), (strain_map_ref, small_map_ref),
        ))
    ]
    for copy in smalls[2:] + copies + smalls[:2]:
        copy.start()
    square_ref[...] = jnp.zeros(square_ref.shape, F32)

    for copy in smalls[2:]:
        copy.wait()
    square_ref[:full, :full] = small_stiff_ref[...]
    square_ref[full : full + comps, :full] = small_map_ref[...]
    square_ref[full + 8 : full + 9, :full] = small_template_ref[...]
    stiff = square_ref[:full, :]
    same = lax.broadcasted_iota(jnp.int32, (full, LANES), 0) == lane_ids(full)
    kdiag = jnp.sum(jnp.where(same, stiff, 0.0), axis=1, keepdims=True)
    template = jnp.sum(
        jnp.where(same, square_ref[full + 8 : full + 9, :], 0.0), axis=1, keepdims=True
    )
    lane = lane_ids(half)
    columns = jnp.zeros((half, LANES), F32)
    for i, col in enumerate((kdiag[:half], kdiag[half:], template[:half], template[half:])):
        columns = jnp.where(lane == i, col, columns)
    cols_ref[...] = columns
    off = jnp.where(same, 0.0, stiff)
    strain_rows = square_ref[full : full + 8, :]
    moved = pltpu.roll(off, LANES - half, 1)
    moved_rows = pltpu.roll(strain_rows, LANES - half, 1)
    stacked = jnp.concatenate(
        [off[:half], moved[half:], moved[:half], strain_rows, moved_rows, off[half:]], 0
    )
    rows = stacked.shape[0]
    lane = lane_ids(rows)
    stacked = jnp.where(lane < half, stacked, 0.0)
    high, low = halves(stacked)
    high = high.astype(F32)
    lhs_ref[:, :LANES] = (high + pltpu.roll(high, half, 1)).astype(BF16)
    lhs_ref[:, LANES:] = low

    slot = lane_ids(parts) // SLOT
    for chunk in range(chunks):
        for copy in copies[chunk * pieces // chunks : (chunk + 1) * pieces // chunks]:
            copy.wait()
        held = jnp.zeros((parts, LANES), F32)
        for i in range(per):
            start = (chunk * per + i) * parts
            moved = pltpu.roll(buffer_ref[start : start + parts, :], 2 + SLOT * i, 1)
            held = jnp.where(slot == i, moved, held)
        at = chunk * per
        for turn, shift in enumerate((LANES - 1, LANES - 3)):
            slots_ref[pl.ds(0, parts, stride=2), :] = held
            slots_ref[pl.ds(1, parts, stride=2), :] = pltpu.roll(held, shift, 1)
            turned_ref[...] = jnp.transpose(slots_ref[...])
            if turn == 0:
                own_ref[at : at + per, :] = turned_ref[pl.ds(1, per, stride=SLOT), :]
            else:
                own_ref[half + at : half + at + per, :] = turned_ref[pl.ds(0, per, stride=SLOT), :]
                third_ref[at : at + per, :] = turned_ref[pl.ds(1, per, stride=SLOT), :]
    for copy in smalls[:2]:
        copy.wait()
    own_ref[OWN_AT : OWN_AT + 1, :] = small_ref[0]
    own_ref[OWN_AT + 1 : OWN_AT + 2, :] = small_ref[1]
    own_ref[OWN_AT + 2 :, :] = jnp.zeros((OWN_ROWS - OWN_AT - 2, LANES), F32)
    even = lane_ids() % 2 == 0
    outer, inner = own_ref[:half, :], own_ref[half : 2 * half, :]
    third = third_ref[...]
    up = [jnp.where(even, outer, earlier(inner)), jnp.zeros((half // 2, LANES), F32)]
    down = [
        jnp.where(even, later(inner), outer),
        jnp.where(even, later(third[half // 2 :]), third[: half // 2]),
    ]
    even_device = lax.axis_index("elem") % 2 == 0
    for ref, ahead in ((first_ref, even_device), (second_ref, jnp.logical_not(even_device))):
        ref[:half, :] = jnp.where(ahead, up[0], down[0])
        ref[half:SENT_AT, :] = jnp.where(ahead, up[1], down[1])
        ref[SENT_AT:, :] = own_ref[OWN_AT:, :]


def shift_of(order, total):
    return MASS_COEF * (order * (1.0 / total)) ** 2


def columns_of(cols):
    return [cols[:, i : i + 1] for i in range(4)]


def diagonals(columns, mod, mass):
    kd_top, kd_low, mt_top, mt_low = columns
    return kd_top * mod[0] + kd_low * mod[1], mt_top * mass[0] + mt_low * mass[1]


def products(lhs, *fields):
    half = fields[0].shape[0]
    split = [halves(field) for field in fields]
    high = jnp.concatenate([h for h, _ in split], 1)
    low = jnp.concatenate([l for _, l in split], 1)
    gap = jnp.zeros((DEPTH - 3 * half, high.shape[1]), BF16)
    result = jnp.dot(lhs, jnp.concatenate([high, low, gap, high], 0), preferred_element_type=F32)
    cut = [0, half, 2 * half, 3 * half, 3 * half + 8, 3 * half + 16, lhs.shape[0]]
    return [
        [result[cut[i] : cut[i + 1], LANES * k : LANES * (k + 1)] for i in (0, 1, 2, 5, 3, 4)]
        for k in range(len(fields))
    ]


def image_of(mod, z):
    lanes = lane_ids()
    own, prev = mod
    up = jnp.where(lanes == 127, 0.0, own)
    down = jnp.where(lanes == 0, 0.0, prev)
    return own * z[0] + prev * z[1] + later(down * z[2]) + earlier(up * z[3])


def strain_of(z):
    return z[4] + jnp.where(lane_ids() == 127, 0.0, later(z[5]))


def inner_kernel(
    load_ref, own_ref, lhs_ref, cols_ref, image_ref, field_ref, inv_ref, strain_ref
):
    half, parts = 48, 64
    freqs = parts // 2
    first_order = (lax.axis_index("freq") * freqs + 1).astype(F32)
    lanes = lane_ids()

    def row(at):
        own = own_ref[OWN_AT + at : OWN_AT + at + 1, :]
        return own, jnp.where(lanes == 0, 0.0, earlier(own))

    mod, mass = row(0), row(1)
    stiff, weight = diagonals(columns_of(cols_ref[...]), mod, mass)
    lhs = lhs_ref[:, :DEPTH]

    def step(f, carry):
        shift = shift_of(first_order + f.astype(F32), 4 * freqs)
        inv = jnp.where(lanes == 0, 0.0, 1.0 / (stiff + shift * weight))
        inv_ref[f] = inv
        loads = [load_ref[pl.ds(2 * f + k, half, stride=parts), :] for k in range(2)]
        for k, z in enumerate(products(lhs, *(inv * b for b in loads))):
            field_ref[2 * f + k] = loads[k]
            image_ref[2 * f + k] = image_of(mod, z)
            start = pl.multiple_of((k * freqs + f) * 8, 8)
            strain_ref[pl.ds(start, 8), :] = strain_of(z)
        return carry

    lax.fori_loop(0, freqs, step, 0, unroll=UNROLL)


def main_kernel(
    image_ref, load_ref, inner_inv_ref, inner_strain_ref,
    own_ref, second_ref, first_ref, lhs_ref, cols_ref,
    out0_ref, out1_ref, out2_ref, out3_ref, dots_out_ref,
    strain_ref, field_ref, inv_ref, border_ref, dots_ref,
):
    half, parts = 48, 64
    freqs = parts // 2
    freq_group = lax.axis_index("freq")
    slab = lax.axis_index("elem")
    is_last = slab == lax.axis_size("elem") - 1
    ahead = slab % 2 == 0
    met_first, met_second = first_ref[...], second_ref[...]
    from_right = jnp.where(ahead, met_first, met_second)
    from_left = jnp.where(ahead, met_second, met_first)
    first_order = (freq_group * freqs + 1).astype(F32)
    lanes = lane_ids()
    even = lanes % 2 == 0

    columns = columns_of(cols_ref[...])
    def rows_of(at):
        own = own_ref[OWN_AT + at : OWN_AT + at + 1, :]
        left, right = (r[SENT_AT + at : SENT_AT + at + 1] for r in (from_left, from_right))
        prev = jnp.where(lanes == 0, earlier(left), earlier(own))

        def sides(*upper_lower):
            (upper, i), (lower, j) = upper_lower
            upper, lower = upper[:, i : i + 1], lower[:, j : j + 1]
            return jnp.where(even, upper, lower)

        zero = jnp.zeros_like(own)
        pairs = [
            (sides((own, 126), (own, 1)), sides((own, 125), (own, 0))),
            (sides((own, 127), (own, 0)), sides((own, 126), (left, 127))),
            (sides((right, 0), (left, 127)), sides((own, 127), (left, 126))),
            (sides((right, 1), (left, 126)), sides((right, 0), (left, 125))),
            (sides((right, 2), (zero, 0)), sides((right, 1), (zero, 0))),
        ]
        return (own, prev), pairs

    mod_main, mod_pairs = rows_of(0)
    mass_main, mass_pairs = rows_of(1)

    lhs = lhs_ref[:, :DEPTH]

    order = first_order + (lanes // 4).astype(F32)
    beyond = jnp.logical_and(even, is_last)
    inverses = []
    for i, (mod, mass) in enumerate(zip(mod_pairs, mass_pairs)):
        stiff, weight = diagonals(columns, mod, mass)
        diag = stiff + shift_of(order, 4 * freqs) * weight
        good = diag > 0
        if i >= 2:
            good = jnp.logical_and(good, jnp.logical_not(beyond))
        inverses.append(jnp.where(good, 1.0 / diag, 0.0))

    third = from_right[half:SENT_AT]
    rims = [
        own_ref[half : 2 * half, :],
        own_ref[:half, :],
        jnp.where(even, later(from_right[:half]), earlier(from_left[:half])),
        jnp.where(even, from_right[:half], from_left[:half]),
        jnp.where(even, jnp.concatenate([later(third), third], 0), 0.0),
    ]
    rims = [field * inv for field, inv in zip(rims, inverses)]

    def rim_stage(stage, rims):
        first = stage
        z = {}
        for i in range(first, len(rims), 2):
            names = list(range(i, min(i + 2, len(rims))))
            for name, value in zip(names, products(lhs, *(rims[name] for name in names))):
                z[name] = value
        at_edge = mod_pairs[1]
        outer = z[2]
        if stage == 0:
            node = z[1]
            own_part = at_edge[0] * node[0] + at_edge[1] * (node[1] + outer[3])
            border = jnp.where(even, at_edge[0] * outer[2], own_part)
            border_ref[3, :half, :] = at_edge[0] * node[3]
            border_ref[4, :half, :] = inverses[1]
            tail = outer[5]
        elif stage == 1:
            border = jnp.where(even, at_edge[0] * outer[2], at_edge[1] * outer[3])
            tail = outer[5]
        else:
            border = jnp.where(even, at_edge[0] * outer[2], 0.0)
            energy = jnp.sum(at_edge[0] * rims[2] * outer[1], axis=0, keepdims=True)
            row = lax.broadcasted_iota(jnp.int32, (8, LANES), 0)
            tail = jnp.where(row == 6, energy, outer[5])
        border_ref[stage, :half, :] = border
        border_ref[stage, half:, :] = jnp.where(even, tail, z[1][4] if stage == 0 else 0.0)
        nexts = [None] * len(rims)
        for i in range(first + 1, len(rims) - 1):
            above = jnp.where(even, z[i + 1][2], z[i - 1][2])
            below = jnp.where(even, z[i - 1][3], z[i + 1][3])
            top, low = mod_pairs[i]
            nexts[i] = -inverses[i] * (top * (z[i][0] + above) + low * (z[i][1] + below))
        return nexts[: len(rims) - 1]

    mod_own, mod_prev = mod_main
    mod_sent_down = jnp.where(lanes == 0, 0.0, mod_prev)
    rim = jnp.logical_or(lanes == 0, lanes == 127)

    def borders(stage, f, k):
        moved = pltpu.roll(border_ref[stage], LANES - 1 - 2 * (2 * f + k), 1)
        moved = jnp.where(rim, moved, 0.0)
        return moved[:half], moved[half:]

    def put_dot(which, f, pairs):
        total = functools.reduce(operator.add, (a * b for a, b in pairs))
        dots_ref[pl.ds(which * freqs + f, 1), :] = jnp.sum(total, axis=0, keepdims=True)

    def put_strain(stage, f, k, value):
        start = ((stage * 2 + k) * freqs + f) * 8
        strain_ref[pl.ds(pl.multiple_of(start, 8), 8), :] = value

    def moved_to(which, lane, place, f, k):
        shift = (lane + 2 * LANES - 1 - 2 * (2 * f + k)) % LANES
        return jnp.where(lanes == lane, pltpu.roll(border_ref[which, :half, :], shift, 1), place)

    def images(f, stage, ready):
        result = []
        for k, z in enumerate(ready):
            added, added_strain = borders(stage, f, k)
            put_strain(stage, f, k, strain_of(z) + added_strain)
            result.append(-(image_of(mod_main, z) + added))
        return result

    def first(f, carry):
        inv = moved_to(4, 0, inner_inv_ref[f], f, 0)
        inv_ref[f] = inv
        loads = [load_ref[2 * f + k] for k in range(2)]
        fields = [inv * b for b in loads]
        image = []
        for k in range(2):
            added, added_strain = borders(0, f, k)
            added = added + moved_to(3, 1, 0.0, f, k)
            image.append(-(image_ref[2 * f + k] + added))
            start = pl.multiple_of((k * freqs + f) * 8, 8)
            put_strain(0, f, k, inner_strain_ref[pl.ds(start, 8), :] + added_strain)
        nexts = [inv * t for t in image]
        for k in range(2):
            field_ref[2 * f + k] = nexts[k]
        put_dot(0, f, zip(fields, loads))
        put_dot(1, f, zip(fields, image))
        put_dot(2, f, zip(nexts, image))
        return carry

    def second(f, fields, ready):
        inv = inv_ref[f]
        image = images(f, 1, ready)
        nexts = [inv * t for t in image]
        for k in range(2):
            field_ref[2 * f + k] = nexts[k]
        put_dot(3, f, zip(fields, image))
        put_dot(4, f, zip(nexts, image))

    def third(f, fields, ready):
        totals, extras = [], []
        for k, z in enumerate(ready):
            z11, z22, z12 = z[:3]
            added, added_strain = borders(2, f, k)
            twice = 2.0 * (later(mod_sent_down * z12) + added)
            totals.append(fields[k] * (mod_own * z11 + mod_sent_down * z22 + twice))
            strain = strain_of(z) + added_strain
            put_strain(2, f, k, strain)
            extras.append(strain[6:7])
        energy = jnp.sum(totals[0] + totals[1], axis=0, keepdims=True) + extras[0] + extras[1]
        dots_ref[pl.ds(5 * freqs + f, 1), :] = -energy

    def run_ahead(step, matrix):
        waiting = []
        for f in range(freqs + AHEAD):
            if f < freqs:
                fields = [field_ref[2 * f + k] for k in range(2)]
                waiting.append((f, fields, products(matrix, *fields)))
            if f >= AHEAD:
                step(*waiting.pop(0))

    quarter = LANES // 4
    cell = lane_ids(8) // quarter
    outs = (out0_ref, out1_ref, out2_ref, out3_ref)

    def pack(stage, block):
        def comp(k, c):
            start = (((stage * 2 + k) * freqs) + block * 8) * 8 + c
            return strain_ref[pl.ds(start, 8, stride=8), :]

        comps = {(k, c): comp(k, c) for k in range(2) for c in range(6)}
        places = [
            (stage * parts + k * freqs, [(k, c) for c in range(4)]) for k in range(2)
        ] + [(3 * parts + stage * freqs, [(0, 4), (0, 5), (1, 4), (1, 5)])]
        stores = []
        for step in range(4):
            dest = lax.bitwise_xor(freq_group, STEPS[step])
            for row, names in places:
                held = None
                for i, name in enumerate(names):
                    moved = pltpu.roll(comps[name], quarter * ((i + 4 - dest) % 4), 1)
                    held = moved if held is None else jnp.where(cell == i, moved, held)
                stores.append((step, row + block * 8, held))
        for step, start, held in stores:
            outs[step][start : start + 8, :] = held

    for stage, step in enumerate((first, second, third)):
        rims = rim_stage(stage, rims)
        if stage == 0:
            lax.fori_loop(0, freqs, step, 0, unroll=UNROLL)
        else:
            run_ahead(step, lhs if stage == 1 else lhs[: 3 * half + 16])
        for block in range(freqs // 8):
            pack(stage, block)

    dots_ref[DOTS * freqs :, :] = jnp.zeros((256 - DOTS * freqs, LANES), F32)
    sums = [
        jnp.sum(jnp.transpose(dots_ref[i : i + LANES, :]), axis=0, keepdims=True)
        for i in (0, LANES)
    ]
    row = lax.broadcasted_iota(jnp.int32, (8, LANES), 0)
    pair = jnp.where(row % 2 == 0, sums[0], sums[1])
    for i in range(dots_out_ref.shape[0] // 8):
        dots_out_ref[8 * i : 8 * i + 8, :] = pair


def coefficients(h):
    def dot(a, b, energy):
        total = None
        for i, x in enumerate(a):
            for j, y in enumerate(b):
                weight = h[i + j] - h[i + j + 1] if energy else h[i + j]
                term = x * y * weight
                total = term if total is None else total + term
        return total

    one = jnp.ones_like(h[0])
    residual, direction = [one], [one]
    rho = h[0]
    result = []
    for iteration in range(3):
        alpha = rho / dot(direction, direction, True)
        result = [
            (result[i] if i < len(result) else 0.0) + alpha * direction[i]
            for i in range(len(direction))
        ]
        if iteration == 2:
            break
        image = (
            [direction[0]]
            + [direction[i] - direction[i - 1] for i in range(1, len(direction))]
            + [-direction[-1]]
        )
        residual = [
            (residual[i] if i < len(residual) else 0.0) - alpha * image[i]
            for i in range(len(image))
        ]
        rho_next = dot(residual, residual, False)
        beta = rho_next / rho
        rho = rho_next
        direction = [
            residual[i] + (beta * direction[i] if i < len(direction) else 0.0)
            for i in range(len(residual))
        ]
    return result


def final_kernel(
    curves_in_ref, dots_ref, part0_ref, part1_ref, part2_ref, part3_ref,
    table_high_ref, table_low_ref, modulus_in_ref, soil_in_ref,
    modulus_out_ref, strain_out_ref, spectra_ref, curves_ref, modulus_ref, soil_ref, copied,
):
    copies = [
        pltpu.make_async_copy(source, target, copied.at[i])
        for i, (source, target) in enumerate((
            (curves_in_ref, curves_ref), (modulus_in_ref, modulus_ref), (soil_in_ref, soil_ref),
        ))
    ]
    for copy in copies:
        copy.start()
    freq_group = lax.axis_index("freq")
    parts, freqs = 64, 32
    total = jnp.zeros((8, LANES), F32)
    for i in range(dots_ref.shape[0] // 8):
        total = total + dots_ref[8 * i : 8 * i + 8, :]
    square = jnp.concatenate([total, jnp.zeros((LANES - 8, LANES), F32)], 0)
    turned = jnp.transpose(square)
    beside = pltpu.roll(turned, 127, 1)
    h = [turned[freqs * i : freqs * (i + 1)] for i in range(4)]
    h += [beside[freqs * i : freqs * (i + 1)] for i in range(2)]
    coefs = coefficients(h)
    lanes = lane_ids(freqs)
    for step, part_ref in enumerate((part0_ref, part1_ref, part2_ref, part3_ref)):
        source = lax.bitwise_xor(freq_group, STEPS[step])
        weights = [
            jnp.sum(jnp.where(lanes == 2 * source, c, 0.0), axis=1, keepdims=True) for c in coefs
        ]

        def joined(base, per_stage):
            return functools.reduce(operator.add, (
                weights[j] * part_ref[base + j * per_stage : base + j * per_stage + freqs, :]
                for j in range(3)
            ))

        rest = joined(3 * parts, freqs)
        for k in range(2):
            start = pl.multiple_of(source * parts + k * freqs, freqs)
            spectra_ref[pl.ds(start, freqs), :LANES] = joined(k * freqs, parts)
            side = pltpu.roll(rest, 64, 1) if k else rest
            spectra_ref[pl.ds(start, freqs), LANES:] = jnp.where(lanes < 64, side, 0.0)
    high, low = halves(spectra_ref[...])
    table_high, table_low = table_high_ref[...], table_low_ref[...]
    history = jnp.dot(
        jnp.concatenate([table_high, table_low, table_high], 1),
        jnp.concatenate([high, high, low], 0), preferred_element_type=F32,
    )
    squares = history[:, :LANES] ** 2 + history[:, LANES:] ** 2
    squares = squares + pltpu.roll(squares, 64, 1)
    squares = squares + pltpu.roll(squares, 32, 1)
    peak = jnp.max(squares, axis=0, keepdims=True)[:, : LANES // 4] * (1.0 / (4 * freqs))
    peak_strain = STRAIN_FACTOR * jnp.sqrt(peak + EPSILON)
    position = (jnp.log(peak_strain) * (1.0 / np.log(10.0)) - LOG_LOW) / LOG_STEP
    for copy in copies:
        copy.wait()
    soil = soil_ref[...]
    ratio = jnp.zeros_like(position)
    for level in range(curves_ref.shape[1]):
        value = jnp.where(soil == 0, curves_ref[0, level], 0.0)
        for kind in range(1, curves_ref.shape[0]):
            value = jnp.where(soil == kind, curves_ref[kind, level], value)
        ratio = ratio + value * jnp.maximum(0.0, 1.0 - jnp.abs(position - level))
    own = pltpu.roll(modulus_ref[...], (LANES - LANES // 4 * freq_group) % LANES, 1)
    modulus_out_ref[...] = own[:, : LANES // 4] * ratio
    strain_out_ref[...] = peak_strain


def time_table(total_freq):
    order = np.arange(1, total_freq + 1)
    phase = (np.arange(NT)[:, None] * order[None, :] % NT) * (2.0 * np.pi / NT)
    waves = np.stack([np.cos(phase), -np.sin(phase)], 1)
    table = waves.reshape(NT, 2, 4, total_freq // 4).transpose(0, 2, 1, 3).reshape(NT, -1)
    high = table.astype(np.float32).astype(jnp.bfloat16)
    low = (table - high.astype(np.float64)).astype(np.float32).astype(jnp.bfloat16)
    return high, low


def per_device(
    load, stiffness, mass_template, modulus, element_mass, strain_map, curves, soil_type
):
    half, freq_dev, _, nodes = load.shape
    parts = 2 * freq_dev
    groups = lax.axis_size("freq")
    slabs = lax.axis_size("elem")
    rows = load.reshape(half * parts, nodes)
    modulus_row, mass_row = modulus.reshape(1, nodes), element_mass.reshape(1, nodes)
    first, second, own, lhs, cols, rows = pl.pallas_call(
        edges_kernel,
        out_shape=[
            pltpu.VMEM((SENT_ROWS, LANES), F32),
            pltpu.VMEM((SENT_ROWS, LANES), F32),
            pltpu.VMEM((OWN_ROWS, LANES), F32),
            pltpu.VMEM((4 * half + 16, 2 * LANES), BF16),
            pltpu.VMEM((half, LANES), F32),
            pltpu.VMEM((half * parts, LANES), F32),
        ],
        in_specs=[HBM] * 6,
        out_specs=[VMEM] * 6,
        scratch_shapes=[
            pltpu.VMEM((LANES, LANES), F32),
            pltpu.VMEM((LANES, LANES), F32),
            pltpu.VMEM((LANES, LANES), F32),
            pltpu.VMEM((2, 1, LANES), F32),
            pltpu.VMEM((half, LANES), F32),
            pltpu.VMEM((1, 2 * half), F32),
            pltpu.VMEM((2 * half, 2 * half), F32),
            pltpu.VMEM(strain_map.shape, F32),
            pltpu.SemaphoreType.DMA((3+6,)),
        ],
        name="edges",
    )(rows, modulus_row, mass_row, stiffness, mass_template.reshape(1, -1), strain_map)
    met_first = lax.ppermute(first, "elem", [(i, i ^ 1) for i in range(slabs)])
    met_second = lax.ppermute(
        second, "elem", [(i, i + 1 if i % 2 else i - 1) for i in range(1, slabs - 1)]
    )
    inner = pl.pallas_call(
        inner_kernel,
        out_shape=[
            pltpu.VMEM((parts, half, LANES), F32),
            pltpu.VMEM((parts, half, LANES), F32),
            pltpu.VMEM((freq_dev, half, LANES), F32),
            pltpu.VMEM((parts * 8, LANES), F32),
        ],
        in_specs=[VMEM] * 4,
        out_specs=[VMEM] * 4,
        compiler_params=pltpu.CompilerParams(vmem_limit_bytes=32 * 1024 * 1024),
        name="inner",
    )(rows, own, lhs, cols)
    packed = 9 * freq_dev
    outs = pl.pallas_call(
        main_kernel,
        out_shape=[jax.ShapeDtypeStruct((packed, LANES), F32)] * 4
        + [jax.ShapeDtypeStruct((2 * slabs * groups, LANES), F32)],
        in_specs=[VMEM] * 9,
        out_specs=[VMEM] * 5,
        scratch_shapes=[
            pltpu.VMEM((3 * parts * 8, LANES), F32),
            pltpu.VMEM((parts, half, LANES), F32),
            pltpu.VMEM((freq_dev, half, LANES), F32),
            pltpu.VMEM((5, half + 8, LANES), F32),
            pltpu.VMEM((256, LANES), F32),
        ],
        compiler_params=pltpu.CompilerParams(vmem_limit_bytes=32 * 1024 * 1024),
        name="krylov",
    )(*inner, own, met_second, met_first, lhs, cols)
    received = [outs[0]] + [
        lax.ppermute(outs[step], "freq", [(i, i ^ STEPS[step]) for i in range(groups)])
        for step in range(1, groups)
    ]
    dots = lax.all_to_all(
        outs[4].reshape(slabs * groups, 2, LANES), ("elem", "freq"), 0, 0
    ).reshape(-1, LANES)
    table_high, table_low = time_table(freq_dev * groups)
    quarter = nodes // groups
    new_modulus, peak_strain = pl.pallas_call(
        final_kernel,
        out_shape=[jax.ShapeDtypeStruct((1, quarter), F32)] * 2,
        in_specs=[HBM] + [VMEM] * 7 + [HBM] * 2,
        out_specs=[VMEM] * 2,
        scratch_shapes=[
            pltpu.VMEM((groups * parts, 2 * LANES), F32),
            pltpu.SMEM(curves.shape, F32),
            pltpu.VMEM((1, nodes), F32),
            pltpu.VMEM((1, quarter), jnp.int32),
            pltpu.SemaphoreType.DMA((3,)),
        ],
        compiler_params=pltpu.CompilerParams(vmem_limit_bytes=32 * 1024 * 1024),
        name="response",
    )(curves, dots, *received, jnp.asarray(table_high), jnp.asarray(table_low),
      modulus_row, soil_type.reshape(1, quarter))
    return new_modulus.reshape(quarter), peak_strain.reshape(quarter)


def solution(mesh):
    in_specs = (
        P(None, "freq", None, "elem"),
        P(),
        P(),
        P("elem"),
        P("elem"),
        P(),
        P(),
        P(("elem", "freq")),
    )
    out_specs = (P(("elem", "freq")), P(("elem", "freq")))
    return jax.shard_map(
        per_device, mesh=mesh, in_specs=in_specs, out_specs=out_specs, check_vma=False
    )
```
